128 devices in a mesh: blk: 32 (over z, y, core), vec: 4 (over x).
Axes of the slice: x: 4, y: 4, z: 4, core: 2. Of those that a mesh axis runs over, the one named last changes fastest.
Arguments:
- label_features: bfloat16 [65536, 768], P('blk'), may hold values from -600 to 600
- start_basis: float32 [65536, 256], P('blk', 'vec'), may hold values from -6 to 6
- pair_block: int32 [32, 32], P('blk'), may hold values from 0 to 3
- pair_live: int32 [32, 32], P('blk'), may hold values from 0 to 1, as said below
Outputs:
- final_basis: float32 [65536, 256], P('blk', 'vec')
The draws below stay inside these ranges and needn't reach their ends.
Inputs may be any that keep to these rules, and one draw needn't show every extreme that they name: pair_live is symmetric with zeros on its diagonal; owners differ widely in how many partners they have.
All inputs are finite; a program needn't handle non-finite values.
Results may differ from the reference program's by a relative error of at most 0.005.
Values may be sent and summed in bfloat16 or wider, within the bound.
No kernel may reach another device: no remote copies, remote signals or barrier semaphores. Data moves between devices by JAX's collectives and lax.ppermute only.
A program may use at most 192 MiB of HBM per device.

```python
import jax
import jax.numpy as jnp
from jax import lax

BS = 512
F = 768
K = 256
ITERS = 2
NB_DEV = 4
OWNERS = 32
LABELS = 65536


def draw_label_features(key, part):
    centre_key, pick_key, mix_key, noise_key, row_key, col_key = jax.random.split(key, 6)
    groups = max(BS // 4, 2)
    picks = jax.random.randint(pick_key, (LABELS,), 0, groups)
    centres = jnp.clip(jax.random.normal(centre_key, (groups, F), jnp.float32), -4.0, 4.0)
    noise = jnp.clip(jax.random.normal(noise_key, (LABELS, F), jnp.float32), -4.0, 4.0)
    share = jax.random.uniform(mix_key, (LABELS, 1), jnp.float32, 0.3, 0.9)
    row_scale = jnp.exp(jax.random.uniform(row_key, (LABELS, 1), jnp.float32, 0.0, 2.3))
    col_scale = jnp.exp(jax.random.uniform(col_key, (1, F), jnp.float32, 0.0, 1.6))
    mixed = jnp.sqrt(share) * jnp.take(centres, picks, axis=0) + jnp.sqrt(1.0 - share) * noise
    return (mixed * row_scale * col_scale).astype(jnp.bfloat16)


def draw_pair_live(key, part):
    weight_key, score_key = jax.random.split(jax.random.fold_in(key, 7))
    weights = jax.random.randint(weight_key, (OWNERS,), 1, 5)
    scores = jax.random.randint(score_key, (OWNERS, OWNERS), 0, 12)
    upper_part = jnp.triu(scores, 1)
    symmetric = upper_part + upper_part.T
    links = (symmetric < weights[:, None] * weights[None, :]).astype(jnp.int32)
    return links * (1 - jnp.eye(OWNERS, dtype=jnp.int32))


def with_ends(drawn, own_key, least, top_value):
    index_at = [jax.random.randint(jax.random.fold_in(own_key, axis), (), 0, length) for axis, length in enumerate(drawn.shape)]
    main_axis = drawn.shape.index(max(drawn.shape))
    neighbour = index_at[:main_axis] + [(index_at[main_axis] + 1) % drawn.shape[main_axis]] + index_at[main_axis + 1:]
    return drawn.at[tuple(index_at)].set(least).at[tuple(neighbour)].set(top_value)


def level_of(own_key, dims, pieces, low, largest):
    loudness, own = 1.0, jax.random.fold_in(own_key, 6)
    for dim, shards_of in pieces:
        steps = jnp.exp(jax.random.uniform(jax.random.fold_in(own, dim), (shards_of,), jnp.float32, low / len(pieces), largest / len(pieces)))
        loudness = loudness * jnp.repeat(steps, dims[dim] // shards_of).reshape([-1 if axis == dim else 1 for axis in range(len(dims))])
    return loudness


def centred(key, dims, width, most, shards=(), held_as=jnp.bfloat16):
    factor_of = level_of(key, dims, shards, -0.22, 0.18) if shards else 1.0
    result = jax.random.normal(key, dims, jnp.float32) * width * factor_of
    return jnp.minimum(jnp.maximum(result, -most), most).astype(held_as)


def setup_inputs(seed: int = 0) -> dict:
    splits = jax.random.split(jax.random.key(seed), 5)
    return {
        "label_features": draw_label_features(jax.random.fold_in(splits[4], 71), 0),
        "start_basis": centred(splits[1], (LABELS, K), 1.0, 6.0, ((0, 32), (1, 4)), jnp.float32),
        "pair_block": with_ends(jax.random.randint(splits[2], (OWNERS, OWNERS), 0, NB_DEV), jax.random.fold_in(splits[2], 1), 0, NB_DEV - 1).astype(jnp.int32),
        "pair_live": draw_pair_live(jax.random.fold_in(splits[4], 71), 0),
    }


SHARPNESS = 5.0
EPSILON = 1e-06

def normalize(features):
    widened = features.astype(jnp.float32)
    inv_norm = lax.rsqrt(lax.optimization_barrier(jnp.mean(widened * widened, axis=-1, keepdims=True)) + EPSILON)
    return (widened * inv_norm).astype(jnp.bfloat16)

def affinity(left_side, right_side):
    scores = jnp.einsum('...af,...bf->...ab', left_side.astype(jnp.float32), right_side.astype(jnp.float32)) / left_side.shape[-1]
    return (jnp.exp(SHARPNESS * (scores - 1.0)) - jnp.exp(-SHARPNESS * (scores + 1.0))).astype(jnp.bfloat16)

def orthonormal(flat_rows, label_total):
    gram_total = jnp.dot(flat_rows.T, flat_rows, precision=lax.Precision.HIGHEST)
    lower_factor = jnp.linalg.cholesky(gram_total / label_total)
    inverse = jax.scipy.linalg.solve_triangular(lower_factor, jnp.eye(gram_total.shape[0], dtype=jnp.float32), lower=True)
    return jnp.dot(flat_rows, inverse.T, precision=lax.Precision.HIGHEST)

def reference(label_features, start_basis, pair_block, pair_live):
    unit_rows = normalize(label_features).reshape(OWNERS, NB_DEV, BS, F)
    owner_ids = jnp.arange(OWNERS, dtype=jnp.int32)
    current = start_basis
    for iteration in range(ITERS):
        vec_half = current.astype(jnp.bfloat16).reshape(OWNERS, NB_DEV, BS, K)

        def owner_sum(owner_index):
            own_blocks = unit_rows[owner_index]
            own_vectors = vec_half[owner_index]
            own_aff = affinity(own_blocks, own_blocks)
            summed = jnp.einsum('nab,nbk->nak', own_aff.astype(jnp.float32), own_vectors.astype(jnp.float32))

            def visit(running, peer_index):
                target = pair_block[owner_index, peer_index].astype(jnp.int32)
                other_block = pair_block[peer_index, owner_index].astype(jnp.int32)
                left_side = lax.dynamic_index_in_dim(own_blocks, target, 0, keepdims=False)
                right_side = unit_rows[peer_index, other_block]
                far_vectors = vec_half[peer_index, other_block]

                def add_term(state):
                    far_term = jnp.dot(affinity(left_side, right_side).astype(jnp.float32), far_vectors.astype(jnp.float32), preferred_element_type=jnp.float32)
                    before = lax.dynamic_index_in_dim(state, target, 0, keepdims=False)
                    return lax.dynamic_update_index_in_dim(state, before + far_term, target, 0)

                def keep_state(state):
                    return state
                return (lax.cond(pair_live[owner_index, peer_index] > 0, add_term, keep_state, running), None)
            summed, unused = lax.scan(visit, summed, owner_ids)
            return summed
        summed_all = lax.map(owner_sum, owner_ids)
        current = orthonormal(summed_all.reshape(LABELS, K), LABELS)
    return current
```

```python
import functools

import jax
import jax.numpy as jnp
from jax import lax
from jax.experimental import pallas as pl
from jax.experimental.pallas import tpu as pltpu
from jax.sharding import PartitionSpec as P

BS = 512
ITERS = 2
SHARPNESS = 5.0
EPSILON = 1e-06
AXES = ("blk", "vec")
HI = lax.Precision.HIGHEST
f32 = jnp.float32
bf16 = jnp.bfloat16


def normalize(features):
    widened = features.astype(f32)
    inv_norm = lax.rsqrt(jnp.mean(widened * widened, axis=-1, keepdims=True) + EPSILON)
    return (widened * inv_norm).astype(bf16)


def affinity(scores_sum, width):
    scores = scores_sum * (1.0 / width)
    return (jnp.exp(SHARPNESS * (scores - 1.0)) - jnp.exp(-SHARPNESS * (scores + 1.0))).astype(bf16)


def nt(a, b, **kw):
    return lax.dot_general(a, b, (((1,), (1,)), ((), ())), preferred_element_type=f32, **kw)


def send_body(pb_ref, v_ref, x_ref, out_ref, buf, nrm, sem_in, sem_out):
    blocks, quarter = nrm.shape[0], nrm.shape[1]
    slots = out_ref.shape[0]
    size = BS
    for t in range(blocks):
        pltpu.make_async_copy(
            x_ref.at[pl.ds(t * size + v_ref[0] * quarter, quarter)], buf.at[t], sem_in.at[t]
        ).start()
    for t in range(blocks):
        pltpu.make_async_copy(x_ref.at[pl.ds(0, quarter)], buf.at[t], sem_in.at[t]).wait()
        nrm[t] = normalize(buf[t])
    for c in range(slots):
        pltpu.make_async_copy(nrm.at[pb_ref[c]], out_ref.at[c], sem_out.at[c]).start()
    for c in range(slots):
        pltpu.make_async_copy(nrm.at[0], out_ref.at[c], sem_out.at[c]).wait()


def send_features(x, pb, v, quarter):
    rows, width = x.shape
    slots = pb.shape[0]
    blocks = rows // BS
    return pl.pallas_call(
        send_body,
        out_shape=jax.ShapeDtypeStruct((slots, quarter, width), bf16),
        in_specs=[
            pl.BlockSpec(memory_space=pltpu.SMEM),
            pl.BlockSpec(memory_space=pltpu.SMEM),
            pl.BlockSpec(memory_space=pl.ANY),
        ],
        out_specs=pl.BlockSpec(memory_space=pl.ANY),
        scratch_shapes=[
            pltpu.VMEM((blocks, quarter, width), bf16),
            pltpu.VMEM((blocks, quarter, width), bf16),
            pltpu.SemaphoreType.DMA((blocks,)),
            pltpu.SemaphoreType.DMA((slots,)),
        ],
        name="send_features",
    )(pb, v, x)


def spread(src, pb_ref, out_ref, sem):
    slots = out_ref.shape[0]
    for c in range(slots):
        pltpu.make_async_copy(src.at[pb_ref[c]], out_ref.at[c], sem.at[c]).start()
    for c in range(slots):
        pltpu.make_async_copy(src.at[0], out_ref.at[c], sem.at[c]).wait()


def start_body(pb_ref, vt_ref, own_ref, out_ref, sem):
    groups, narrow, rows = vt_ref.shape
    blocks, quarter, width = own_ref.shape
    for g in range(groups):
        own_ref[:, :, g * narrow : (g + 1) * narrow] = (
            vt_ref[g].astype(f32).T.astype(bf16).reshape(blocks, quarter, narrow)
        )
    spread(own_ref, pb_ref, out_ref, sem)


def start_vectors(vt, pb, blocks, quarter):
    groups, narrow, rows = vt.shape
    slots = pb.shape[0]
    width = groups * narrow
    return pl.pallas_call(
        start_body,
        out_shape=(
            jax.ShapeDtypeStruct((blocks, quarter, width), bf16),
            jax.ShapeDtypeStruct((slots, quarter, width), bf16),
        ),
        in_specs=[
            pl.BlockSpec(memory_space=pltpu.SMEM),
            pl.BlockSpec(memory_space=pltpu.VMEM),
        ],
        out_specs=(pl.BlockSpec(memory_space=pltpu.VMEM), pl.BlockSpec(memory_space=pl.ANY)),
        scratch_shapes=[pltpu.SemaphoreType.DMA((slots,))],
        name="start_vectors",
    )(pb, vt)


def add_product(out_ref, t, p, first):
    quarters, quarter = out_ref.shape[0], out_ref.shape[2]
    for q in range(quarters):
        piece = p[q * quarter : (q + 1) * quarter]
        if first:
            out_ref[q, t] = piece
        else:
            out_ref[q, t] += piece


def pairs_first_body(sc_ref, unit_ref, far_ref, vfar_ref, vown_ref, aff_ref, out_ref):
    blocks, quarter, width = vown_ref.shape
    feat = unit_ref.shape[1]
    s = pl.program_id(0)

    def one(rhs, vec, t, first):
        aff = affinity(nt(unit_ref[pl.ds(t * BS, BS), :], rhs), feat)
        aff_ref[0] = aff
        add_product(out_ref, t, jnp.dot(aff, vec, preferred_element_type=f32), first)

    @pl.when(s < blocks)
    def _():
        t = jnp.minimum(s, blocks - 1)
        one(unit_ref[pl.ds(t * BS + sc_ref[65] * quarter, quarter), :], vown_ref[t], t, True)

    @pl.when((s >= blocks) & (s < blocks + sc_ref[64]))
    def _():
        one(far_ref[0], vfar_ref[0], sc_ref[32 + jnp.maximum(s - blocks, 0)], False)


def pairs_next_body(sc_ref, aff_ref, vfar_ref, vown_ref, out_ref):
    blocks = vown_ref.shape[0]
    s = pl.program_id(0)

    @pl.when(s < blocks)
    def _():
        t = jnp.minimum(s, blocks - 1)
        add_product(out_ref, t, jnp.dot(aff_ref[0], vown_ref[t], preferred_element_type=f32), True)

    @pl.when((s >= blocks) & (s < blocks + sc_ref[64]))
    def _():
        t = sc_ref[32 + jnp.maximum(s - blocks, 0)]
        add_product(out_ref, t, jnp.dot(aff_ref[0], vfar_ref[0], preferred_element_type=f32), False)


def pairs(sc, unit, far, vfar, vown, aff=None):
    slots, quarter, width = vfar.shape
    blocks = vown.shape[0]
    quarters = BS // quarter

    def slot_map(s, sc):
        return (sc[jnp.clip(s - blocks, 0, jnp.maximum(sc[64] - 1, 0))], 0, 0)

    def aff_map(s, sc):
        return (jnp.minimum(s, blocks - 1 + sc[64]), 0, 0)

    whole3 = lambda s, sc: (0, 0, 0)
    out_spec = pl.BlockSpec((quarters, blocks, quarter, width), lambda s, sc: (0, 0, 0, 0))
    out_shape = jax.ShapeDtypeStruct((quarters, blocks, quarter, width), f32)
    vspecs = [
        pl.BlockSpec((1, quarter, width), slot_map),
        pl.BlockSpec((blocks, quarter, width), whole3),
    ]
    aff_spec = pl.BlockSpec((1, BS, quarter), aff_map)
    grid = (blocks + slots,)
    if aff is None:
        return pl.pallas_call(
            pairs_first_body,
            out_shape=(jax.ShapeDtypeStruct((blocks + slots, BS, quarter), bf16), out_shape),
            grid_spec=pltpu.PrefetchScalarGridSpec(
                num_scalar_prefetch=1,
                grid=grid,
                in_specs=[
                    pl.BlockSpec(unit.shape, lambda s, sc: (0, 0)),
                    pl.BlockSpec((1, quarter, unit.shape[1]), slot_map),
                ]
                + vspecs,
                out_specs=(aff_spec, out_spec),
            ),
            name="pairs_first",
        )(sc, unit, far, vfar, vown)
    return pl.pallas_call(
        pairs_next_body,
        out_shape=out_shape,
        grid_spec=pltpu.PrefetchScalarGridSpec(
            num_scalar_prefetch=1, grid=grid, in_specs=[aff_spec] + vspecs, out_specs=out_spec
        ),
        name="pairs_next",
    )(sc, aff, vfar, vown)


def gram_body(my_ref, parts_ref, prod_ref, gram_ref, full):
    p = (parts_ref[0] + parts_ref[1]) + (parts_ref[2] + parts_ref[3])
    prod_ref[...] = p
    full[...] = lax.dot_general(
        p, p, (((0,), (0,)), ((), ())), precision=HI, preferred_element_type=f32
    )
    chunks, rows = gram_ref.shape[0], gram_ref.shape[1]
    for d in range(chunks):
        at = pl.multiple_of((my_ref[0] ^ d) * rows, rows)
        gram_ref[d] = full[pl.ds(at, rows), :]


def gram(parts, my, chunks):
    _, rows, width = parts.shape
    return pl.pallas_call(
        gram_body,
        out_shape=(
            jax.ShapeDtypeStruct((rows, width), f32),
            jax.ShapeDtypeStruct((chunks, width // chunks, width), f32),
        ),
        in_specs=[
            pl.BlockSpec(memory_space=pltpu.SMEM),
            pl.BlockSpec(memory_space=pltpu.VMEM),
        ],
        out_specs=(pl.BlockSpec(memory_space=pltpu.VMEM), pl.BlockSpec(memory_space=pltpu.VMEM)),
        scratch_shapes=[pltpu.VMEM((width, width), f32)],
        name="gram",
    )(my, parts)


def lane_splat(x, j):
    return jnp.broadcast_to(x[:, j : j + 1], x.shape)


def row_splat(x, s):
    return jnp.broadcast_to(x[s : s + 1, :], x.shape)


def inverse_factor(a):
    n = a.shape[0]
    groups = n // 8
    rows = [a[8 * i : 8 * i + 8, :] for i in range(groups)]
    row_at = lax.broadcasted_iota(jnp.int32, (8, n), 0)
    lane_at = lax.broadcasted_iota(jnp.int32, (8, n), 1)
    inv = [jnp.where(lane_at == row_at + 8 * i, 1.0, 0.0).astype(f32) for i in range(groups)]
    for j in range(n):
        g, s = divmod(j, 8)
        pivot_row = row_splat(rows[g], s)
        scale = lax.rsqrt(lane_splat(pivot_row, j))
        pivot_row = pivot_row * scale
        inv_row = row_splat(inv[g], s) * scale
        for i in range(g, groups):
            factor = lane_splat(rows[i], j) * scale
            if i == g:
                factor = jnp.where(row_at > s, factor, 0.0)
            if not (i == g and s == 7):
                rows[i] = rows[i] - factor * pivot_row
            new = inv[i] - factor * inv_row
            inv[i] = jnp.where(row_at == s, inv_row, new) if i == g else new
    return jnp.concatenate(inv, axis=0)


def whiten(my_ref, chunk_refs, a_ref, w_ref, label_total):
    n = a_ref.shape[0]
    h = n // 2
    rows = chunk_refs[0].shape[0]
    for d, chunk in enumerate(chunk_refs):
        at = pl.multiple_of((my_ref[0] ^ d) * rows, rows)
        a_ref[pl.ds(at, rows), :] = chunk[...] * (1.0 / label_total)
    w11 = inverse_factor(a_ref[:h, :h])
    low = nt(a_ref[h:, :h], w11, precision=HI)
    w22 = inverse_factor(a_ref[h:, h:] - nt(low, low, precision=HI))
    mid = jnp.dot(low, w11, precision=HI, preferred_element_type=f32)
    w_ref[:h, :h] = w11
    w_ref[:h, h:] = jnp.zeros((h, h), f32)
    w_ref[h:, :h] = -jnp.dot(w22, mid, precision=HI, preferred_element_type=f32)
    w_ref[h:, h:] = w22


def step_body(label_total, chunks, my_ref, pb_ref, *refs):
    chunk_refs, (prod_ref, own_ref, out_ref, a_ref, w_ref, sem) = refs[:chunks], refs[chunks:]
    whiten(my_ref, chunk_refs, a_ref, w_ref, label_total)
    blocks, quarter, width = own_ref.shape
    own_ref[...] = nt(prod_ref[...], w_ref[...], precision=HI).astype(bf16).reshape(own_ref.shape)
    spread(own_ref, pb_ref, out_ref, sem)


def step(gram_chunks, prod, my, pb, blocks, quarter, label_total):
    width = prod.shape[1]
    slots = pb.shape[0]
    chunks = len(gram_chunks)
    smem = pl.BlockSpec(memory_space=pltpu.SMEM)
    vmem = pl.BlockSpec(memory_space=pltpu.VMEM)
    return pl.pallas_call(
        functools.partial(step_body, label_total, chunks),
        out_shape=(
            jax.ShapeDtypeStruct((blocks, quarter, width), bf16),
            jax.ShapeDtypeStruct((slots, quarter, width), bf16),
        ),
        in_specs=[smem, smem] + [vmem] * (chunks + 1),
        out_specs=(vmem, pl.BlockSpec(memory_space=pl.ANY)),
        scratch_shapes=[
            pltpu.VMEM((width, width), f32),
            pltpu.VMEM((width, width), f32),
            pltpu.SemaphoreType.DMA((slots,)),
        ],
        name="step",
    )(my, pb, *gram_chunks, prod)


def last_body(label_total, chunks, my_ref, *refs):
    chunk_refs, (prod_ref, out_ref, a_ref, w_ref) = refs[:chunks], refs[chunks:]
    whiten(my_ref, chunk_refs, a_ref, w_ref, label_total)
    quarters, narrow, rows = out_ref.shape
    for q in range(quarters):
        out_ref[q] = nt(w_ref[q * narrow : (q + 1) * narrow, :], prod_ref[...], precision=HI)


def last(gram_chunks, prod, my, quarters, label_total):
    rows, width = prod.shape
    chunks = len(gram_chunks)
    smem = pl.BlockSpec(memory_space=pltpu.SMEM)
    vmem = pl.BlockSpec(memory_space=pltpu.VMEM)
    return pl.pallas_call(
        functools.partial(last_body, label_total, chunks),
        out_shape=jax.ShapeDtypeStruct((quarters, width // quarters, rows), f32),
        in_specs=[smem] + [vmem] * (chunks + 1),
        out_specs=vmem,
        scratch_shapes=[pltpu.VMEM((width, width), f32), pltpu.VMEM((width, width), f32)],
        name="last",
    )(my, *gram_chunks, prod)


def make(mesh):
    nblk, nvec = mesh.shape["blk"], mesh.shape["vec"]

    def swap(x, owner_bits, vec_bits):
        perm = [
            (o * nvec + v, (o ^ owner_bits) * nvec + (v ^ vec_bits))
            for o in range(nblk)
            for v in range(nvec)
        ]
        return lax.ppermute(x, AXES, perm)

    def exchange(x, axis):
        return lax.all_to_all(x, axis, split_axis=0, concat_axis=0, tiled=True)

    def gram_sum(pieces):
        total = pieces[0]
        for d in range(1, 8):
            total = total + swap(pieces[d], d & 1, d >> 1)
        for shift in (1, 3):
            got = [swap(total, d << shift, 0) for d in (1, 2, 3)]
            total = (total + got[0]) + (got[1] + got[2])
        return [total] + [swap(total, d & 1, d >> 1) for d in range(1, 8)]

    def body(x, basis, pair_block, pair_live):
        rows, feat = x.shape
        narrow = basis.shape[1]
        blocks = rows // BS
        quarter = BS // nvec
        label_total = rows * nblk
        b = lax.axis_index("blk")
        v = lax.axis_index("vec")
        v1 = v[None].astype(jnp.int32)
        my = (v * 2 + (b & 1))[None].astype(jnp.int32)
        pb, live = pair_block[0], pair_live[0]

        send = send_features(x, pb, v1, quarter)
        far = exchange(send, "blk")
        vt = basis.T.astype(bf16).reshape(narrow, blocks, nvec, quarter)
        vt = jnp.transpose(vt, (2, 0, 1, 3)).reshape(nvec, narrow, blocks * quarter)
        vown, vsend = start_vectors(exchange(vt, "vec"), pb, blocks, quarter)
        vfar = exchange(vsend, "blk")

        order = jnp.argsort((1 - live) * blocks + pb, stable=True).astype(jnp.int32)
        count = jnp.sum(live)[None].astype(jnp.int32)
        sc = jnp.concatenate([order, jnp.take(pb, order), count, v1])
        unit = normalize(x)

        aff, out = pairs(sc, unit, far, vfar, vown)
        for it in range(ITERS):
            if it:
                out = pairs(sc, None, None, vfar, vown, aff)
            parts = exchange(out.reshape(nvec, blocks * quarter, nvec * narrow), "vec")
            prod, pieces = gram(parts, my, 8)
            sums = gram_sum(pieces)
            if it + 1 < ITERS:
                vown, vsend = step(sums, prod, my, pb, blocks, quarter, label_total)
                vfar = exchange(vsend, "blk")
        final = exchange(last(sums, prod, my, nvec, label_total), "vec")
        final = final.reshape(nvec, narrow, blocks, quarter)
        return jnp.transpose(final, (2, 0, 3, 1)).reshape(rows, narrow)

    return body


def solution(mesh):
    in_specs = (P("blk", None), P("blk", "vec"), P("blk", None), P("blk", None))
    return jax.shard_map(
        make(mesh), mesh=mesh, in_specs=in_specs, out_specs=P("blk", "vec"), check_vma=False
    )
```

```python
import functools

import jax
import jax.numpy as jnp
from jax import lax
from jax.experimental import pallas as pl
from jax.experimental.pallas import tpu as pltpu
from jax.sharding import PartitionSpec as P

BS = 512
ITERS = 2
SHARPNESS = 5.0
EPSILON = 1e-06
AXES = ("blk", "vec")
HI = lax.Precision.HIGHEST
f32 = jnp.float32
bf16 = jnp.bfloat16


def normalize(features):
    widened = features.astype(f32)
    inv_norm = lax.rsqrt(jnp.mean(widened * widened, axis=-1, keepdims=True) + EPSILON)
    return (widened * inv_norm).astype(bf16)


def affinity(scores_sum, width):
    scores = scores_sum * (1.0 / width)
    return (jnp.exp(SHARPNESS * (scores - 1.0)) - jnp.exp(-SHARPNESS * (scores + 1.0))).astype(bf16)


def nt(a, b, **kw):
    return lax.dot_general(a, b, (((1,), (1,)), ((), ())), preferred_element_type=f32, **kw)


def spread(src, pb_ref, out_ref, sem):
    slots = out_ref.shape[0]
    for c in range(slots):
        pltpu.make_async_copy(src.at[pb_ref[c]], out_ref.at[c], sem.at[c]).start()
    for c in range(slots):
        pltpu.make_async_copy(src.at[0], out_ref.at[c], sem.at[c]).wait()


def send_body(my_ref, pb_ref, x_ref, v0_ref, v1_ref, v2_ref, v3_ref, own_ref, out_ref, buf, pack, sem_in, sem_out):
    blocks, quarter, feat = buf.shape
    narrow = v0_ref.shape[0]
    groups = 4
    v = my_ref[0]
    for t in range(blocks):
        pltpu.make_async_copy(
            x_ref.at[pl.ds(t * BS + v * quarter, quarter)], buf.at[t], sem_in.at[t]
        ).start()
    for d, vt_ref in enumerate((v0_ref, v1_ref, v2_ref, v3_ref)):
        turned = vt_ref[...].astype(f32).T.astype(bf16).reshape(blocks, quarter, narrow)
        for g in range(groups):

            @pl.when((v ^ d) == g)
            def _():
                own_ref[:, :, g * narrow : (g + 1) * narrow] = turned

    for t in range(blocks):
        pltpu.make_async_copy(x_ref.at[pl.ds(0, quarter)], buf.at[t], sem_in.at[t]).wait()
        pack[t, :, :feat] = normalize(buf[t])
        pack[t, :, feat:] = own_ref[t]
    spread(pack, pb_ref, out_ref, sem_out)


def send_start(x, vts, pb, my, quarter):
    rows, feat = x.shape
    narrow = vts[0].shape[0]
    width = narrow * len(vts)
    slots = pb.shape[0]
    blocks = rows // BS
    smem = pl.BlockSpec(memory_space=pltpu.SMEM)
    vmem = pl.BlockSpec(memory_space=pltpu.VMEM)
    hbm = pl.BlockSpec(memory_space=pl.ANY)
    return pl.pallas_call(
        send_body,
        out_shape=(
            jax.ShapeDtypeStruct((blocks, quarter, width), bf16),
            jax.ShapeDtypeStruct((slots, quarter, feat + width), bf16),
        ),
        in_specs=[smem, smem, hbm] + [vmem] * len(vts),
        out_specs=(vmem, hbm),
        scratch_shapes=[
            pltpu.VMEM((blocks, quarter, feat), bf16),
            pltpu.VMEM((blocks, quarter, feat + width), bf16),
            pltpu.SemaphoreType.DMA((blocks,)),
            pltpu.SemaphoreType.DMA((slots,)),
        ],
        name="send_start",
    )(my, pb, x, *vts)


LANES = 4


def add_product(out_ref, t, p, first):
    quarters, quarter = out_ref.shape[0], out_ref.shape[2]
    for q in range(quarters):
        piece = p[q * quarter : (q + 1) * quarter]
        if first:
            out_ref[q, t] = piece
        else:
            out_ref[q, t] += piece


def slot_at(sc_ref, s, k):
    return jnp.maximum((s - 1) * LANES + k, 0)


def pairs_first_body(sc_ref, unit_ref, *refs):
    far_refs, (vown_ref, aff_ref, out_ref) = refs[:LANES], refs[LANES:]
    quarter = vown_ref.shape[1]
    feat = unit_ref.shape[1]
    s = pl.program_id(0)

    @pl.when(s == 0)
    def _():
        for t in range(LANES):
            rhs = unit_ref[pl.ds(t * BS + sc_ref[65] * quarter, quarter), :]
            aff = affinity(nt(unit_ref[pl.ds(t * BS, BS), :], rhs), feat)
            aff_ref[t] = aff
            add_product(out_ref, t, jnp.dot(aff, vown_ref[t], preferred_element_type=f32), True)

    @pl.when((s > 0) & ((s - 1) * LANES < sc_ref[64]))
    def _():
        prods = []
        for k in range(LANES):
            at = slot_at(sc_ref, s, k)
            t = sc_ref[32 + at]
            aff = affinity(nt(unit_ref[pl.ds(t * BS, BS), :], far_refs[k][0, :, :feat]), feat)
            aff = jnp.where(at < sc_ref[64], aff, jnp.zeros_like(aff))
            aff_ref[k] = aff
            prods.append((t, jnp.dot(aff, far_refs[k][0, :, feat:], preferred_element_type=f32)))
        for t, p in prods:
            add_product(out_ref, t, p, False)


def pairs_next_body(sc_ref, aff_ref, *refs):
    far_refs, (vown_ref, out_ref) = refs[:LANES], refs[LANES:]
    s = pl.program_id(0)

    @pl.when(s == 0)
    def _():
        for t in range(LANES):
            p = jnp.dot(aff_ref[t], vown_ref[t], preferred_element_type=f32)
            add_product(out_ref, t, p, True)

    @pl.when((s > 0) & ((s - 1) * LANES < sc_ref[64]))
    def _():
        for k in range(LANES):
            t = sc_ref[32 + slot_at(sc_ref, s, k)]
            p = jnp.dot(aff_ref[k], far_refs[k][0], preferred_element_type=f32)
            add_product(out_ref, t, p, False)


def pairs(sc, unit, far, vown, aff=None):
    slots, quarter, far_width = far.shape
    blocks, _, width = vown.shape
    quarters = BS // quarter
    steps = 1 + slots // LANES

    def last_step(sc):
        return (sc[64] + LANES - 1) // LANES

    def slot_map(k):
        def index(s, sc):
            group = jnp.maximum(jnp.minimum(s, last_step(sc)) - 1, 0)
            return (sc[group * LANES + k], 0, 0)

        return index

    out_spec = pl.BlockSpec((quarters, blocks, quarter, width), lambda s, sc: (0, 0, 0, 0))
    out_shape = jax.ShapeDtypeStruct((quarters, blocks, quarter, width), f32)
    far_specs = [pl.BlockSpec((1, quarter, far_width), slot_map(k)) for k in range(LANES)]
    own_spec = pl.BlockSpec((blocks, quarter, width), lambda s, sc: (0, 0, 0))
    aff_spec = pl.BlockSpec((LANES, BS, quarter), lambda s, sc: (jnp.minimum(s, last_step(sc)), 0, 0))
    fars = [far] * LANES
    if aff is None:
        return pl.pallas_call(
            pairs_first_body,
            out_shape=(jax.ShapeDtypeStruct((blocks + slots, BS, quarter), bf16), out_shape),
            grid_spec=pltpu.PrefetchScalarGridSpec(
                num_scalar_prefetch=1,
                grid=(steps,),
                in_specs=[pl.BlockSpec(unit.shape, lambda s, sc: (0, 0))] + far_specs + [own_spec],
                out_specs=(aff_spec, out_spec),
            ),
            name="pairs_first",
        )(sc, unit, *fars, vown)
    return pl.pallas_call(
        pairs_next_body,
        out_shape=out_shape,
        grid_spec=pltpu.PrefetchScalarGridSpec(
            num_scalar_prefetch=1,
            grid=(steps,),
            in_specs=[aff_spec] + far_specs + [own_spec],
            out_specs=out_spec,
        ),
        name="pairs_next",
    )(sc, aff, *fars, vown)


def gram_body(my_ref, parts_ref, prod_ref, *refs):
    piece_refs, full = refs[:-1], refs[-1]
    p = (parts_ref[0] + parts_ref[1]) + (parts_ref[2] + parts_ref[3])
    prod_ref[...] = p
    full[...] = lax.dot_general(
        p, p, (((0,), (0,)), ((), ())), precision=HI, preferred_element_type=f32
    )
    for d, piece in enumerate(piece_refs):
        rows = piece.shape[0]
        piece[...] = full[pl.ds(pl.multiple_of((my_ref[0] ^ d) * rows, rows), rows), :]


def gram(parts, my):
    nvec, rows, width = parts.shape
    vmem = pl.BlockSpec(memory_space=pltpu.VMEM)
    out = pl.pallas_call(
        gram_body,
        out_shape=[jax.ShapeDtypeStruct((rows, width), f32)]
        + [jax.ShapeDtypeStruct((width // nvec, width), f32)] * nvec,
        in_specs=[pl.BlockSpec(memory_space=pltpu.SMEM), vmem],
        out_specs=[vmem] * (nvec + 1),
        scratch_shapes=[pltpu.VMEM((width, width), f32)],
        name="gram",
    )(my, parts)
    return out[0], out[1:]


def lane_splat(x, j):
    return jnp.broadcast_to(x[:, j : j + 1], x.shape)


def row_splat(x, s):
    return jnp.broadcast_to(x[s : s + 1, :], x.shape)


def split3(x):
    high = x.astype(bf16)
    rest = x - high.astype(f32)
    mid = rest.astype(bf16)
    return high, mid, (rest - mid.astype(f32)).astype(bf16)


PANEL = 16


def inverse_factor(a):
    n = a.shape[0]
    row_at = lax.broadcasted_iota(jnp.int32, (PANEL, n), 0)
    square = (n, n)
    on_diag = lax.broadcasted_iota(jnp.int32, square, 0) == lax.broadcasted_iota(jnp.int32, square, 1)
    inv = jnp.where(on_diag, 1.0, 0.0).astype(f32)
    done = []
    for j in range(0, n, PANEL):
        top, itop = a[:PANEL, :], inv[:PANEL, :]
        cols = [lane_splat(top, j + c) for c in range(PANEL)]
        for c in range(PANEL):
            scale = lax.rsqrt(row_splat(cols[c], c))
            below = jnp.where(row_at > c, cols[c] * scale, 0.0)
            for k in range(c + 1, PANEL):
                cols[k] = cols[k] - below * (row_splat(cols[k], c) * scale)
            row, irow = row_splat(top, c) * scale, row_splat(itop, c) * scale
            top = jnp.where(row_at == c, row, top - below * row)
            itop = jnp.where(row_at == c, irow, itop - below * irow)
        done.append(itop)
        if j + PANEL < n:
            h, m, l = split3(top)
            ih, im, il = split3(itop)
            left = jnp.concatenate([h, h, m, h, l, m], axis=0)
            right = jnp.concatenate(
                [jnp.concatenate([h, m, h, l, h, m], axis=0), jnp.concatenate([ih, im, ih, il, ih, im], axis=0)],
                axis=1,
            )
            update = lax.dot_general(left, right, (((0,), (0,)), ((), ())), preferred_element_type=f32)
            update = update[j + PANEL :, :]
            a = a[PANEL:, :] - update[:, :n]
            inv = inv[PANEL:, :] - update[:, n:]
    return jnp.concatenate(done, axis=0)


def whiten(my_ref, chunk_refs, a_ref, w_ref, label_total):
    n = a_ref.shape[0]
    h = n // 2
    rows = chunk_refs[0].shape[0]
    for d, chunk in enumerate(chunk_refs):
        at = pl.multiple_of((my_ref[0] ^ d) * rows, rows)
        a_ref[pl.ds(at, rows), :] = chunk[...] * (1.0 / label_total)
    w11 = inverse_factor(a_ref[:h, :h])
    low = nt(a_ref[h:, :h], w11, precision=HI)
    w22 = inverse_factor(a_ref[h:, h:] - nt(low, low, precision=HI))
    mid = jnp.dot(low, w11, precision=HI, preferred_element_type=f32)
    w_ref[:h, :h] = w11
    w_ref[:h, h:] = jnp.zeros((h, h), f32)
    w_ref[h:, :h] = -jnp.dot(w22, mid, precision=HI, preferred_element_type=f32)
    w_ref[h:, h:] = w22


def step_body(label_total, chunks, my_ref, pb_ref, *refs):
    chunk_refs, (prod_ref, own_ref, out_ref, a_ref, w_ref, sem) = refs[:chunks], refs[chunks:]
    whiten(my_ref, chunk_refs, a_ref, w_ref, label_total)
    blocks, quarter, width = own_ref.shape
    own_ref[...] = nt(prod_ref[...], w_ref[...], precision=HI).astype(bf16).reshape(own_ref.shape)
    spread(own_ref, pb_ref, out_ref, sem)


def step(gram_chunks, prod, my, pb, blocks, quarter, label_total):
    width = prod.shape[1]
    slots = pb.shape[0]
    chunks = len(gram_chunks)
    smem = pl.BlockSpec(memory_space=pltpu.SMEM)
    vmem = pl.BlockSpec(memory_space=pltpu.VMEM)
    return pl.pallas_call(
        functools.partial(step_body, label_total, chunks),
        out_shape=(
            jax.ShapeDtypeStruct((blocks, quarter, width), bf16),
            jax.ShapeDtypeStruct((slots, quarter, width), bf16),
        ),
        in_specs=[smem, smem] + [vmem] * (chunks + 1),
        out_specs=(vmem, pl.BlockSpec(memory_space=pl.ANY)),
        scratch_shapes=[
            pltpu.VMEM((width, width), f32),
            pltpu.VMEM((width, width), f32),
            pltpu.SemaphoreType.DMA((slots,)),
        ],
        name="step",
    )(my, pb, *gram_chunks, prod)


def last_body(label_total, chunks, my_ref, *refs):
    chunk_refs, (prod_ref, out_ref, a_ref, w_ref) = refs[:chunks], refs[chunks:]
    whiten(my_ref, chunk_refs, a_ref, w_ref, label_total)
    quarters, narrow, rows = out_ref.shape
    for q in range(quarters):
        out_ref[q] = nt(w_ref[q * narrow : (q + 1) * narrow, :], prod_ref[...], precision=HI)


def last(gram_chunks, prod, my, quarters, label_total):
    rows, width = prod.shape
    chunks = len(gram_chunks)
    smem = pl.BlockSpec(memory_space=pltpu.SMEM)
    vmem = pl.BlockSpec(memory_space=pltpu.VMEM)
    return pl.pallas_call(
        functools.partial(last_body, label_total, chunks),
        out_shape=jax.ShapeDtypeStruct((quarters, width // quarters, rows), f32),
        in_specs=[smem] + [vmem] * (chunks + 1),
        out_specs=vmem,
        scratch_shapes=[pltpu.VMEM((width, width), f32), pltpu.VMEM((width, width), f32)],
        name="last",
    )(my, *gram_chunks, prod)


def make(mesh):
    nblk, nvec = mesh.shape["blk"], mesh.shape["vec"]

    def swap(x, owner_bits, vec_bits):
        perm = [
            (o * nvec + v, (o ^ owner_bits) * nvec + (v ^ vec_bits))
            for o in range(nblk)
            for v in range(nvec)
        ]
        return lax.ppermute(x, AXES, perm)

    def exchange(x, axis):
        return lax.all_to_all(x, axis, split_axis=0, concat_axis=0, tiled=True)

    def gram_sum(pieces):
        total = pieces[0]
        for d in range(1, nvec):
            total = total + swap(pieces[d], 0, d)
        for shift in (1, 3):
            got = [swap(total, d << shift, 0) for d in (1, 2, 3)]
            total = (total + got[0]) + (got[1] + got[2])
        total = total + swap(total, 1, 0)
        return [total] + [swap(total, 0, d) for d in range(1, nvec)]

    def body(x, basis, pair_block, pair_live):
        rows, feat = x.shape
        narrow = basis.shape[1]
        blocks = rows // BS
        quarter = BS // nvec
        label_total = rows * nblk
        v = lax.axis_index("vec")
        my = v[None].astype(jnp.int32)
        pb, live = pair_block[0], pair_live[0]

        vt = jnp.transpose(basis.T.astype(bf16).reshape(narrow, blocks, nvec, quarter), (2, 0, 1, 3))
        vt = vt.reshape(nvec, narrow, blocks * quarter)
        vts = [lax.dynamic_index_in_dim(vt, v ^ d, 0, keepdims=False) for d in range(nvec)]
        vts = [vts[0]] + [swap(vts[d], 0, d) for d in range(1, nvec)]
        vown, send = send_start(x, vts, pb, my, quarter)
        far = exchange(send, "blk")

        order = jnp.argsort((1 - live) * blocks + pb, stable=True).astype(jnp.int32)
        count = jnp.sum(live)[None].astype(jnp.int32)
        sc = jnp.concatenate([order, jnp.take(pb, order), count, my])
        unit = normalize(x)

        aff, out = pairs(sc, unit, far, vown)
        for it in range(ITERS):
            if it:
                out = pairs(sc, None, far, vown, aff)
            parts = exchange(out.reshape(nvec, blocks * quarter, nvec * narrow), "vec")
            prod, pieces = gram(parts, my)
            sums = gram_sum(pieces)
            if it + 1 < ITERS:
                vown, vsend = step(sums, prod, my, pb, blocks, quarter, label_total)
                far = exchange(vsend, "blk")
        final = exchange(last(sums, prod, my, nvec, label_total), "vec")
        final = final.reshape(nvec, narrow, blocks, quarter)
        return jnp.transpose(final, (2, 0, 3, 1)).reshape(rows, narrow)

    return body


def solution(mesh):
    in_specs = (P("blk", None), P("blk", "vec"), P("blk", None), P("blk", None))
    return jax.shard_map(
        make(mesh), mesh=mesh, in_specs=in_specs, out_specs=P("blk", "vec"), check_vma=False
    )
```

```python
import functools

import jax
import jax.numpy as jnp
from jax import lax
from jax.experimental import pallas as pl
from jax.experimental.pallas import tpu as pltpu
from jax.sharding import PartitionSpec as P

BS = 512
ITERS = 2
SHARPNESS = 5.0
EPSILON = 1e-06
AXES = ("blk", "vec")
HI = lax.Precision.HIGHEST
f32 = jnp.float32
bf16 = jnp.bfloat16


def normalize(features):
    widened = features.astype(f32)
    inv_norm = lax.rsqrt(jnp.mean(widened * widened, axis=-1, keepdims=True) + EPSILON)
    return (widened * inv_norm).astype(bf16)


LOG2E = 1.4426950408889634


def affinity(scores_sum, width):
    bent = scores_sum * (SHARPNESS * LOG2E / width)
    shift = SHARPNESS * LOG2E
    return (jnp.exp2(bent - shift) - jnp.exp2(-shift - bent)).astype(bf16)


def nt(a, b, **kw):
    return lax.dot_general(a, b, (((1,), (1,)), ((), ())), preferred_element_type=f32, **kw)


def spread(src, pb_ref, out_ref, sem):
    slots = out_ref.shape[0]
    for c in range(slots):
        pltpu.make_async_copy(src.at[pb_ref[c]], out_ref.at[c], sem.at[c]).start()
    for c in range(slots):
        pltpu.make_async_copy(src.at[0], out_ref.at[c], sem.at[c]).wait()


def own_quarter_body(my_ref, x_ref, out_ref, buf, sem):
    blocks, quarter, _ = buf.shape
    for t in range(blocks):
        pltpu.make_async_copy(
            x_ref.at[pl.ds(t * BS + my_ref[0] * quarter, quarter)], buf.at[t], sem.at[t]
        ).start()
    for t in range(blocks):
        pltpu.make_async_copy(x_ref.at[pl.ds(0, quarter)], buf.at[t], sem.at[t]).wait()
        out_ref[t] = normalize(buf[t])


def own_quarter(x, my, blocks, quarter):
    feat = x.shape[1]
    return pl.pallas_call(
        own_quarter_body,
        out_shape=jax.ShapeDtypeStruct((blocks, quarter, feat), bf16),
        in_specs=[pl.BlockSpec(memory_space=pltpu.SMEM), pl.BlockSpec(memory_space=pl.ANY)],
        out_specs=pl.BlockSpec(memory_space=pltpu.VMEM),
        scratch_shapes=[pltpu.VMEM((blocks, quarter, feat), bf16), pltpu.SemaphoreType.DMA((blocks,))],
        name="own_quarter",
    )(my, x)


def send_body(my_ref, pb_ref, unit_ref, v0_ref, v1_ref, v2_ref, v3_ref, own_ref, out_ref, pack, sem):
    blocks, quarter, feat = unit_ref.shape
    narrow = v0_ref.shape[0]
    v = my_ref[0]
    for d, vt_ref in enumerate((v0_ref, v1_ref, v2_ref, v3_ref)):
        turned = vt_ref[...].astype(f32).T.astype(bf16).reshape(blocks, quarter, narrow)
        for g in range(4):

            @pl.when((v ^ d) == g)
            def _():
                own_ref[:, :, g * narrow : (g + 1) * narrow] = turned

    for t in range(blocks):
        pack[t, :, :feat] = unit_ref[t]
        pack[t, :, feat:] = own_ref[t]
    spread(pack, pb_ref, out_ref, sem)


def send_start(unit_quarter, vts, pb, my):
    blocks, quarter, feat = unit_quarter.shape
    width = vts[0].shape[0] * len(vts)
    slots = pb.shape[0]
    smem = pl.BlockSpec(memory_space=pltpu.SMEM)
    vmem = pl.BlockSpec(memory_space=pltpu.VMEM)
    return pl.pallas_call(
        send_body,
        out_shape=(
            jax.ShapeDtypeStruct((blocks, quarter, width), bf16),
            jax.ShapeDtypeStruct((slots, quarter, feat + width), bf16),
        ),
        in_specs=[smem, smem, vmem] + [vmem] * len(vts),
        out_specs=(vmem, pl.BlockSpec(memory_space=pl.ANY)),
        scratch_shapes=[
            pltpu.VMEM((blocks, quarter, feat + width), bf16),
            pltpu.SemaphoreType.DMA((slots,)),
        ],
        name="send_start",
    )(my, pb, unit_quarter, *vts)


LANES = 4


def pair_table(pb, live, blocks, entries):
    slots = pb.shape[0]
    on = live > 0
    c = jnp.arange(slots, dtype=jnp.int32)
    same = (pb[:, None] == pb[None, :]) & on[None, :] & (c[None, :] < c[:, None])
    rank = jnp.sum(same.astype(jnp.int32), axis=1)
    t = jnp.arange(blocks, dtype=jnp.int32)
    number = jnp.sum(((pb[None, :] == t[:, None]) & on[None, :]).astype(jnp.int32), axis=1)
    even = (number + 1) // 2 * 2
    end = jnp.sum(jnp.where(t[None, :] <= t[:, None], even[None, :], 0), axis=1)
    start = jnp.sum(jnp.where(pb[:, None] == t[None, :], (end - even)[None, :], 0), axis=1)
    at = jnp.where(on, start + rank, -1)
    j = jnp.arange(entries, dtype=jnp.int32)
    hit = at[None, :] == j[:, None]
    slot = jnp.sum(jnp.where(hit, c[None, :], 0), axis=1)
    use = jnp.sum(hit.astype(jnp.int32), axis=1)
    target = jnp.minimum(jnp.sum((j[:, None] >= end[None, :]).astype(jnp.int32), axis=1), blocks - 1)
    return jnp.concatenate([slot, use, target, end[-1:]])


def entries_of(slots, blocks):
    return -(-(slots - 1 + blocks) // LANES) * LANES


def add_product(out_refs, t, p, first):
    quarter = out_refs[0].shape[1]
    for d, out_ref in enumerate(out_refs):
        piece = p[d * quarter : (d + 1) * quarter]
        if first:
            out_ref[t] = piece
        else:
            out_ref[t] += piece


def pairs_first_body(entries, sc_ref, my_ref, unit_ref, *refs):
    far_refs, vown_ref, aff_ref, out_refs = refs[:LANES], refs[LANES], refs[LANES + 1], refs[LANES + 2 :]
    quarter = vown_ref.shape[1]
    feat = unit_ref.shape[1]
    s = pl.program_id(0)
    v = my_ref[0]

    def target_rows(t):
        return jnp.concatenate(
            [unit_ref[pl.ds(t * BS + (v ^ d) * quarter, quarter), :] for d in range(len(out_refs))], axis=0
        )

    @pl.when(s == 0)
    def _():
        for t in range(LANES):
            rows = target_rows(t)
            aff = affinity(nt(rows, rows[:quarter]), feat)
            aff_ref[t] = aff
            add_product(out_refs, t, jnp.dot(aff, vown_ref[t], preferred_element_type=f32), True)

    @pl.when((s > 0) & ((s - 1) * LANES < sc_ref[3 * entries]))
    def _():
        prods = []
        first = jnp.maximum((s - 1) * LANES, 0)
        for k in range(0, LANES, 2):
            t = sc_ref[2 * entries + first + k]
            rhs = jnp.concatenate([far_refs[k + i][0, :, :feat] for i in range(2)], axis=0)
            vec = jnp.concatenate([far_refs[k + i][0, :, feat:] for i in range(2)], axis=0)
            both = affinity(nt(target_rows(t), rhs), feat)
            affs = []
            for i in range(2):
                aff = both[:, i * quarter : (i + 1) * quarter]
                aff = jnp.where(sc_ref[entries + first + k + i] > 0, aff, jnp.zeros_like(aff))
                aff_ref[k + i] = aff
                affs.append(aff)
            prods.append((t, jnp.dot(jnp.concatenate(affs, axis=1), vec, preferred_element_type=f32)))
        for t, p in prods:
            add_product(out_refs, t, p, False)


def pairs_next_body(entries, sc_ref, my_ref, aff_ref, *refs):
    far_refs, vown_ref, out_refs = refs[:LANES], refs[LANES], refs[LANES + 1 :]
    s = pl.program_id(0)

    @pl.when(s == 0)
    def _():
        for t in range(LANES):
            p = jnp.dot(aff_ref[t], vown_ref[t], preferred_element_type=f32)
            add_product(out_refs, t, p, True)

    @pl.when((s > 0) & ((s - 1) * LANES < sc_ref[3 * entries]))
    def _():
        first = jnp.maximum((s - 1) * LANES, 0)
        for k in range(0, LANES, 2):
            t = sc_ref[2 * entries + first + k]
            aff = jnp.concatenate([aff_ref[k], aff_ref[k + 1]], axis=1)
            vec = jnp.concatenate([far_refs[k][0], far_refs[k + 1][0]], axis=0)
            add_product(out_refs, t, jnp.dot(aff, vec, preferred_element_type=f32), False)


def pairs(sc, my, unit, far, vown, aff=None):
    slots, quarter, far_width = far.shape
    blocks, _, width = vown.shape
    quarters = BS // quarter
    entries = entries_of(slots, blocks)
    steps = 1 + entries // LANES

    def last_step(sc):
        return (sc[3 * entries] + LANES - 1) // LANES

    def slot_map(k):
        def index(s, sc, my):
            group = jnp.maximum(jnp.minimum(s, last_step(sc)) - 1, 0)
            return (sc[group * LANES + k], 0, 0)

        return index

    out_specs = [pl.BlockSpec((blocks, quarter, width), lambda s, sc, my: (0, 0, 0))] * quarters
    out_shapes = [jax.ShapeDtypeStruct((blocks, quarter, width), f32)] * quarters
    far_specs = [pl.BlockSpec((1, quarter, far_width), slot_map(k)) for k in range(LANES)]
    own_spec = pl.BlockSpec((blocks, quarter, width), lambda s, sc, my: (0, 0, 0))
    aff_spec = pl.BlockSpec(
        (LANES, BS, quarter), lambda s, sc, my: (jnp.minimum(s, last_step(sc)), 0, 0)
    )
    fars = [far] * LANES
    if aff is None:
        out = pl.pallas_call(
            functools.partial(pairs_first_body, entries),
            out_shape=[jax.ShapeDtypeStruct((blocks + entries, BS, quarter), bf16)] + out_shapes,
            grid_spec=pltpu.PrefetchScalarGridSpec(
                num_scalar_prefetch=2,
                grid=(steps,),
                in_specs=[pl.BlockSpec(unit.shape, lambda s, sc, my: (0, 0))] + far_specs + [own_spec],
                out_specs=[aff_spec] + out_specs,
            ),
            name="pairs_first",
        )(sc, my, unit, *fars, vown)
        return out[0], out[1:]
    return pl.pallas_call(
        functools.partial(pairs_next_body, entries),
        out_shape=out_shapes,
        grid_spec=pltpu.PrefetchScalarGridSpec(
            num_scalar_prefetch=2,
            grid=(steps,),
            in_specs=[aff_spec] + far_specs + [own_spec],
            out_specs=out_specs,
        ),
        name="pairs_next",
    )(sc, my, aff, *fars, vown)


def gram_body(nvec, my_ref, *refs):
    part_refs, prod_ref, piece_refs, full = refs[:nvec], refs[nvec], refs[nvec + 1 : -1], refs[-1]
    p = (part_refs[0][...] + part_refs[1][...]) + (part_refs[2][...] + part_refs[3][...])
    prod_ref[...] = p
    full[...] = lax.dot_general(
        p, p, (((0,), (0,)), ((), ())), precision=HI, preferred_element_type=f32
    )
    for d, piece in enumerate(piece_refs):
        rows = piece.shape[0]
        piece[...] = full[pl.ds(pl.multiple_of((my_ref[0] ^ d) * rows, rows), rows), :]


def gram(parts, my):
    nvec = len(parts)
    rows, width = parts[0].shape
    vmem = pl.BlockSpec(memory_space=pltpu.VMEM)
    out = pl.pallas_call(
        functools.partial(gram_body, nvec),
        out_shape=[jax.ShapeDtypeStruct((rows, width), f32)]
        + [jax.ShapeDtypeStruct((width // nvec, width), f32)] * nvec,
        in_specs=[pl.BlockSpec(memory_space=pltpu.SMEM)] + [vmem] * nvec,
        out_specs=[vmem] * (nvec + 1),
        scratch_shapes=[pltpu.VMEM((width, width), f32)],
        name="gram",
    )(my, *parts)
    return out[0], out[1:]


def lane_splat(x, j):
    return jnp.broadcast_to(x[:, j : j + 1], x.shape)


def row_splat(x, s):
    return jnp.broadcast_to(x[s : s + 1, :], x.shape)


def split3(x):
    high = x.astype(bf16)
    rest = x - high.astype(f32)
    mid = rest.astype(bf16)
    return high, mid, (rest - mid.astype(f32)).astype(bf16)


PANEL = 16


def inverse_factor(a):
    n = a.shape[0]
    row_at = lax.broadcasted_iota(jnp.int32, (PANEL, n), 0)
    square = (n, n)
    on_diag = lax.broadcasted_iota(jnp.int32, square, 0) == lax.broadcasted_iota(jnp.int32, square, 1)
    inv = jnp.where(on_diag, 1.0, 0.0).astype(f32)
    done = []
    for j in range(0, n, PANEL):
        top, itop = a[:PANEL, :], inv[:PANEL, :]
        cols = [lane_splat(top, j + c) for c in range(PANEL)]
        for c in range(PANEL):
            scale = lax.rsqrt(row_splat(cols[c], c))
            below = jnp.where(row_at > c, cols[c] * scale, 0.0)
            for k in range(c + 1, PANEL):
                cols[k] = cols[k] - below * (row_splat(cols[k], c) * scale)
            row, irow = row_splat(top, c) * scale, row_splat(itop, c) * scale
            top = jnp.where(row_at == c, row, top - below * row)
            itop = jnp.where(row_at == c, irow, itop - below * irow)
        done.append(itop)
        if j + PANEL < n:
            h, m, l = split3(top)
            ih, im, il = split3(itop)
            left = jnp.concatenate([h, h, m, h, l, m], axis=0)
            right = jnp.concatenate(
                [jnp.concatenate([h, m, h, l, h, m], axis=0), jnp.concatenate([ih, im, ih, il, ih, im], axis=0)],
                axis=1,
            )
            update = lax.dot_general(left, right, (((0,), (0,)), ((), ())), preferred_element_type=f32)
            update = update[j + PANEL :, :]
            a = a[PANEL:, :] - update[:, :n]
            inv = inv[PANEL:, :] - update[:, n:]
    return jnp.concatenate(done, axis=0)


def whiten(my_ref, chunk_refs, a_ref, w_ref, label_total):
    n = a_ref.shape[0]
    h = n // 2
    rows = chunk_refs[0].shape[0]
    for d, chunk in enumerate(chunk_refs):
        at = pl.multiple_of((my_ref[0] ^ d) * rows, rows)
        a_ref[pl.ds(at, rows), :] = chunk[...] * (1.0 / label_total)
    w11 = inverse_factor(a_ref[:h, :h])
    low = nt(a_ref[h:, :h], w11, precision=HI)
    w22 = inverse_factor(a_ref[h:, h:] - nt(low, low, precision=HI))
    mid = jnp.dot(low, w11, precision=HI, preferred_element_type=f32)
    w_ref[:h, :h] = w11
    w_ref[:h, h:] = jnp.zeros((h, h), f32)
    w_ref[h:, :h] = -jnp.dot(w22, mid, precision=HI, preferred_element_type=f32)
    w_ref[h:, h:] = w22


def step_body(label_total, chunks, my_ref, pb_ref, *refs):
    chunk_refs, (prod_ref, own_ref, out_ref, a_ref, w_ref, sem) = refs[:chunks], refs[chunks:]
    whiten(my_ref, chunk_refs, a_ref, w_ref, label_total)
    blocks, quarter, width = own_ref.shape
    own_ref[...] = nt(prod_ref[...], w_ref[...], precision=HI).astype(bf16).reshape(own_ref.shape)
    spread(own_ref, pb_ref, out_ref, sem)


def step(gram_chunks, prod, my, pb, blocks, quarter, label_total):
    width = prod.shape[1]
    slots = pb.shape[0]
    chunks = len(gram_chunks)
    smem = pl.BlockSpec(memory_space=pltpu.SMEM)
    vmem = pl.BlockSpec(memory_space=pltpu.VMEM)
    return pl.pallas_call(
        functools.partial(step_body, label_total, chunks),
        out_shape=(
            jax.ShapeDtypeStruct((blocks, quarter, width), bf16),
            jax.ShapeDtypeStruct((slots, quarter, width), bf16),
        ),
        in_specs=[smem, smem] + [vmem] * (chunks + 1),
        out_specs=(vmem, pl.BlockSpec(memory_space=pl.ANY)),
        scratch_shapes=[
            pltpu.VMEM((width, width), f32),
            pltpu.VMEM((width, width), f32),
            pltpu.SemaphoreType.DMA((slots,)),
        ],
        name="step",
    )(my, pb, *gram_chunks, prod)


def last_body(label_total, chunks, my_ref, *refs):
    chunk_refs, (prod_ref, out_ref, a_ref, w_ref) = refs[:chunks], refs[chunks:]
    whiten(my_ref, chunk_refs, a_ref, w_ref, label_total)
    quarters, narrow, rows = out_ref.shape
    for q in range(quarters):
        out_ref[q] = nt(w_ref[q * narrow : (q + 1) * narrow, :], prod_ref[...], precision=HI)


def last(gram_chunks, prod, my, quarters, label_total):
    rows, width = prod.shape
    chunks = len(gram_chunks)
    smem = pl.BlockSpec(memory_space=pltpu.SMEM)
    vmem = pl.BlockSpec(memory_space=pltpu.VMEM)
    return pl.pallas_call(
        functools.partial(last_body, label_total, chunks),
        out_shape=jax.ShapeDtypeStruct((quarters, width // quarters, rows), f32),
        in_specs=[smem] + [vmem] * (chunks + 1),
        out_specs=vmem,
        scratch_shapes=[pltpu.VMEM((width, width), f32), pltpu.VMEM((width, width), f32)],
        name="last",
    )(my, *gram_chunks, prod)


def make(mesh):
    nblk, nvec = mesh.shape["blk"], mesh.shape["vec"]

    def swap(x, owner_bits, vec_bits):
        perm = [
            (o * nvec + v, (o ^ owner_bits) * nvec + (v ^ vec_bits))
            for o in range(nblk)
            for v in range(nvec)
        ]
        return lax.ppermute(x, AXES, perm)

    def exchange(x, axis):
        return lax.all_to_all(x, axis, split_axis=0, concat_axis=0, tiled=True)

    def gram_sum(pieces):
        total = pieces[0]
        for d in range(1, nvec):
            total = total + swap(pieces[d], 0, d)
        for shift in (1, 3):
            got = [swap(total, d << shift, 0) for d in (1, 2, 3)]
            total = (total + got[0]) + (got[1] + got[2])
        total = total + swap(total, 1, 0)
        return [total] + [swap(total, 0, d) for d in range(1, nvec)]

    def body(x, basis, pair_block, pair_live):
        rows, feat = x.shape
        narrow = basis.shape[1]
        blocks = rows // BS
        quarter = BS // nvec
        label_total = rows * nblk
        v = lax.axis_index("vec")
        my = v[None].astype(jnp.int32)
        pb, live = pair_block[0], pair_live[0]

        vt = jnp.transpose(basis.T.astype(bf16).reshape(narrow, blocks, nvec, quarter), (2, 0, 1, 3))
        vt = vt.reshape(nvec, narrow, blocks * quarter)
        vts = [lax.dynamic_index_in_dim(vt, v ^ d, 0, keepdims=False) for d in range(nvec)]
        vts = [vts[0]] + [swap(vts[d], 0, d) for d in range(1, nvec)]
        vown, send = send_start(own_quarter(x, my, blocks, quarter), vts, pb, my)
        far = exchange(send, "blk")

        sc = pair_table(pb, live, blocks, entries_of(nblk, blocks))
        unit = normalize(x)

        aff, out = pairs(sc, my, unit, far, vown)
        for it in range(ITERS):
            if it:
                out = pairs(sc, my, None, far, vown, aff)
            out = [o.reshape(blocks * quarter, nvec * narrow) for o in out]
            parts = [out[0]] + [swap(out[d], 0, d) for d in range(1, nvec)]
            prod, pieces = gram(parts, my)
            sums = gram_sum(pieces)
            if it + 1 < ITERS:
                vown, vsend = step(sums, prod, my, pb, blocks, quarter, label_total)
                far = exchange(vsend, "blk")
        final = exchange(last(sums, prod, my, nvec, label_total), "vec")
        final = final.reshape(nvec, narrow, blocks, quarter)
        return jnp.transpose(final, (2, 0, 3, 1)).reshape(rows, narrow)

    return body


def solution(mesh):
    in_specs = (P("blk", None), P("blk", "vec"), P("blk", None), P("blk", None))
    return jax.shard_map(
        make(mesh), mesh=mesh, in_specs=in_specs, out_specs=P("blk", "vec"), check_vma=False
    )
```

```python
import functools

import jax
import jax.numpy as jnp
from jax import lax
from jax.experimental import pallas as pl
from jax.experimental.pallas import tpu as pltpu
from jax.sharding import PartitionSpec as P

BS = 512
ITERS = 2
SHARPNESS = 5.0
EPSILON = 1e-06
AXES = ("blk", "vec")
HI = lax.Precision.HIGHEST
f32 = jnp.float32
bf16 = jnp.bfloat16


def normalize(features):
    widened = features.astype(f32)
    inv_norm = lax.rsqrt(jnp.mean(widened * widened, axis=-1, keepdims=True) + EPSILON)
    return (widened * inv_norm).astype(bf16)


LOG2E = 1.4426950408889634


def affinity(scores_sum, width):
    bent = scores_sum * (SHARPNESS * LOG2E / width)
    shift = SHARPNESS * LOG2E
    return (jnp.exp2(bent - shift) - jnp.exp2(-shift - bent)).astype(bf16)


def nt(a, b, **kw):
    return lax.dot_general(a, b, (((1,), (1,)), ((), ())), preferred_element_type=f32, **kw)


def spread(src, pb_ref, out_ref, sem):
    slots = out_ref.shape[0]
    for c in range(slots):
        pltpu.make_async_copy(src.at[pb_ref[c]], out_ref.at[c], sem.at[c]).start()
    for c in range(slots):
        pltpu.make_async_copy(src.at[0], out_ref.at[c], sem.at[c]).wait()


def own_quarter_body(my_ref, x_ref, out_ref, buf, sem):
    blocks, quarter, _ = buf.shape
    for t in range(blocks):
        pltpu.make_async_copy(
            x_ref.at[pl.ds(t * BS + my_ref[0] * quarter, quarter)], buf.at[t], sem.at[t]
        ).start()
    for t in range(blocks):
        pltpu.make_async_copy(x_ref.at[pl.ds(0, quarter)], buf.at[t], sem.at[t]).wait()
        out_ref[t] = normalize(buf[t])


def own_quarter(x, my, blocks, quarter):
    feat = x.shape[1]
    return pl.pallas_call(
        own_quarter_body,
        out_shape=jax.ShapeDtypeStruct((blocks, quarter, feat), bf16),
        in_specs=[pl.BlockSpec(memory_space=pltpu.SMEM), pl.BlockSpec(memory_space=pl.ANY)],
        out_specs=pl.BlockSpec(memory_space=pltpu.VMEM),
        scratch_shapes=[pltpu.VMEM((blocks, quarter, feat), bf16), pltpu.SemaphoreType.DMA((blocks,))],
        name="own_quarter",
    )(my, x)


def send_body(my_ref, unit_ref, v0_ref, v1_ref, v2_ref, v3_ref, own_ref, *pack_refs):
    blocks, quarter, feat = unit_ref.shape
    narrow = v0_ref.shape[0]
    v = my_ref[0]
    for d, vt_ref in enumerate((v0_ref, v1_ref, v2_ref, v3_ref)):
        turned = vt_ref[...].astype(f32).T.astype(bf16).reshape(blocks, quarter, narrow)
        for g in range(4):

            @pl.when((v ^ d) == g)
            def _():
                own_ref[:, :, g * narrow : (g + 1) * narrow] = turned

    half = quarter // 2
    for h, pack in enumerate(pack_refs):
        rows = slice(h * half, (h + 1) * half)
        for t in range(blocks):
            pack[t, :, :feat] = unit_ref[t, rows]
            pack[t, :, feat:] = own_ref[t, rows]


def send_start(unit_quarter, vts, my):
    blocks, quarter, feat = unit_quarter.shape
    width = vts[0].shape[0] * len(vts)
    vmem = pl.BlockSpec(memory_space=pltpu.VMEM)
    out = pl.pallas_call(
        send_body,
        out_shape=[jax.ShapeDtypeStruct((blocks, quarter, width), bf16)]
        + [jax.ShapeDtypeStruct((blocks, quarter // 2, feat + width), bf16)] * 2,
        in_specs=[pl.BlockSpec(memory_space=pltpu.SMEM), vmem] + [vmem] * len(vts),
        out_specs=[vmem] * 3,
        name="send_start",
    )(my, unit_quarter, *vts)
    return out[0], out[1:]


SHIFT = {"z": 3, "y": 1}
LINES = (("z", "y"), ("y", "z"))
NEAR = 4
SIDE = 8


def offset(axis, o):
    return (o >> 1) << SHIFT[axis] | (o & 1)


def relay_body(at_ref, *refs):
    pb_refs, has_refs = refs[: 2 * NEAR], refs[2 * NEAR : 4 * NEAR]
    out_refs, sem = refs[4 * NEAR : -1], refs[-1]
    owner = at_ref[0]

    def copy(h, o, d, block):
        return pltpu.make_async_copy(
            has_refs[h * NEAR + d].at[block], out_refs[h * SIDE + o].at[d], sem.at[h, o, d]
        )

    places = [(h, o, d) for h in range(2) for o in range(SIDE) for d in range(NEAR)]
    for h, o, d in places:
        copy(h, o, d, pb_refs[h * NEAR + d][0, owner ^ offset(LINES[h][1], o)]).start()
    for h, o, d in places:
        copy(h, o, d, 0).wait()


def relay(pbs, has, owner):
    blocks, half, width = has[0].shape
    hbm = pl.BlockSpec(memory_space=pl.ANY)
    smem = pl.BlockSpec(memory_space=pltpu.SMEM)
    return pl.pallas_call(
        relay_body,
        out_shape=[jax.ShapeDtypeStruct((NEAR, half, width), bf16)] * (2 * SIDE),
        in_specs=[smem] * (1 + len(pbs)) + [hbm] * len(has),
        out_specs=[hbm] * (2 * SIDE),
        scratch_shapes=[pltpu.SemaphoreType.DMA((2, SIDE, NEAR))],
        name="relay",
    )(owner, *pbs, *has)


LANES = 4


def pair_table(pb, live, owner, blocks, entries):
    slots = pb.shape[0]
    on = live > 0
    c = jnp.arange(slots, dtype=jnp.int32)
    same = (pb[:, None] == pb[None, :]) & on[None, :] & (c[None, :] < c[:, None])
    rank = jnp.sum(same.astype(jnp.int32), axis=1)
    t = jnp.arange(blocks, dtype=jnp.int32)
    number = jnp.sum(((pb[None, :] == t[:, None]) & on[None, :]).astype(jnp.int32), axis=1)
    even = (number + 1) // 2 * 2
    end = jnp.sum(jnp.where(t[None, :] <= t[:, None], even[None, :], 0), axis=1)
    start = jnp.sum(jnp.where(pb[:, None] == t[None, :], (end - even)[None, :], 0), axis=1)
    at = jnp.where(on, start + rank, -1)
    j = jnp.arange(entries, dtype=jnp.int32)
    hit = at[None, :] == j[:, None]
    slot = jnp.sum(jnp.where(hit, c[None, :], 0), axis=1)
    use = jnp.sum(hit.astype(jnp.int32), axis=1)
    target = jnp.minimum(jnp.sum((j[:, None] >= end[None, :]).astype(jnp.int32), axis=1), blocks - 1)
    by_offset = jnp.sum(jnp.where((owner ^ c)[:, None] == c[None, :], at[None, :], 0), axis=1)
    return jnp.concatenate([slot, use, target, end[-1:], by_offset])


def entries_of(slots, blocks):
    return -(-(slots - 1 + blocks) // LANES) * LANES


def add_product(out_refs, t, p, first):
    quarter = out_refs[0].shape[1]
    for d, out_ref in enumerate(out_refs):
        piece = p[d * quarter : (d + 1) * quarter]
        if first:
            out_ref[t] = piece
        else:
            out_ref[t] += piece


def pairs_first_body(entries, sc_ref, my_ref, unit_ref, *refs):
    far_refs, refs = refs[: 2 * SIDE], refs[2 * SIDE :]
    vown_ref, aff_ref, out_refs, (buf, sem) = refs[0], refs[1], refs[2:-2], refs[-2:]
    quarter = vown_ref.shape[1]
    half = quarter // 2
    feat = unit_ref.shape[1]
    s = pl.program_id(0)
    v = my_ref[0]

    def copy(h, side, line, entry):
        return pltpu.make_async_copy(
            far_refs[h * SIDE + side].at[line], buf.at[entry, pl.ds(h * half, half)], sem.at[h, entry]
        )

    def target_rows(t):
        return jnp.concatenate(
            [unit_ref[pl.ds(t * BS + (v ^ d) * quarter, quarter), :] for d in range(len(out_refs))], axis=0
        )

    @pl.when(s == 0)
    def _():
        for o in range(1, NEAR * NEAR * 2):
            z, y, core = o >> 3, (o >> 1) & 3, o & 1
            entry = sc_ref[3 * entries + 1 + o]

            @pl.when(entry >= 0)
            def _():
                copy(0, 2 * y + core, z, entry).start()
                copy(1, 2 * z + core, y, entry).start()

        for t in range(LANES):
            rows = target_rows(t)
            aff = affinity(nt(rows, rows[:quarter]), feat)
            aff_ref[t] = aff
            add_product(out_refs, t, jnp.dot(aff, vown_ref[t], preferred_element_type=f32), True)

    @pl.when((s > 0) & ((s - 1) * LANES < sc_ref[3 * entries]))
    def _():
        prods = []
        first = jnp.maximum((s - 1) * LANES, 0)
        for k in range(LANES):

            @pl.when(sc_ref[entries + first + k] > 0)
            def _():
                copy(0, 0, 0, first + k).wait()
                copy(1, 0, 0, first + k).wait()

        for k in range(0, LANES, 2):
            t = sc_ref[2 * entries + first + k]
            rhs = jnp.concatenate([buf[first + k + i, :, :feat] for i in range(2)], axis=0)
            both = affinity(nt(target_rows(t), rhs), feat)
            affs, vecs = [], []
            for i in range(2):
                used = sc_ref[entries + first + k + i] > 0
                aff = both[:, i * quarter : (i + 1) * quarter]
                aff = jnp.where(used, aff, jnp.zeros_like(aff))
                vec = buf[first + k + i, :, feat:]
                vecs.append(jnp.where(used, vec, jnp.zeros_like(vec)))
                aff_ref[k + i] = aff
                affs.append(aff)
            p = jnp.dot(
                jnp.concatenate(affs, axis=1), jnp.concatenate(vecs, axis=0), preferred_element_type=f32
            )
            prods.append((t, p))
        for t, p in prods:
            add_product(out_refs, t, p, False)


def pairs_next_body(entries, sc_ref, my_ref, aff_ref, *refs):
    far_refs, vown_ref, out_refs = refs[:LANES], refs[LANES], refs[LANES + 1 :]
    s = pl.program_id(0)

    @pl.when(s == 0)
    def _():
        for t in range(LANES):
            p = jnp.dot(aff_ref[t], vown_ref[t], preferred_element_type=f32)
            add_product(out_refs, t, p, True)

    @pl.when((s > 0) & ((s - 1) * LANES < sc_ref[3 * entries]))
    def _():
        first = jnp.maximum((s - 1) * LANES, 0)
        for k in range(0, LANES, 2):
            t = sc_ref[2 * entries + first + k]
            aff = jnp.concatenate([aff_ref[k], aff_ref[k + 1]], axis=1)
            vec = jnp.concatenate([far_refs[k][0], far_refs[k + 1][0]], axis=0)
            add_product(out_refs, t, jnp.dot(aff, vec, preferred_element_type=f32), False)


def last_step(sc, entries):
    return (sc[3 * entries] + LANES - 1) // LANES


def pair_specs(blocks, quarter, width, entries):
    quarters = BS // quarter
    whole = lambda s, sc, my: (0, 0, 0)
    aff_spec = pl.BlockSpec(
        (LANES, BS, quarter), lambda s, sc, my: (jnp.minimum(s, last_step(sc, entries)), 0, 0)
    )
    own_spec = pl.BlockSpec((blocks, quarter, width), whole)
    out_shapes = [jax.ShapeDtypeStruct((blocks, quarter, width), f32)] * quarters
    return aff_spec, own_spec, [own_spec] * quarters, out_shapes


def pairs_first(sc, my, unit, fars, vown, entries):
    blocks, quarter, width = vown.shape
    far_width = fars[0].shape[2]
    aff_spec, own_spec, out_specs, out_shapes = pair_specs(blocks, quarter, width, entries)
    out = pl.pallas_call(
        functools.partial(pairs_first_body, entries),
        out_shape=[jax.ShapeDtypeStruct((blocks + entries, BS, quarter), bf16)] + out_shapes,
        grid_spec=pltpu.PrefetchScalarGridSpec(
            num_scalar_prefetch=2,
            grid=(1 + entries // LANES,),
            in_specs=[pl.BlockSpec(unit.shape, lambda s, sc, my: (0, 0))]
            + [pl.BlockSpec(memory_space=pl.ANY)] * len(fars)
            + [own_spec],
            out_specs=[aff_spec] + out_specs,
            scratch_shapes=[
                pltpu.VMEM((entries, quarter, far_width), bf16),
                pltpu.SemaphoreType.DMA((2, entries)),
            ],
        ),
        name="pairs_first",
    )(sc, my, unit, *fars, vown)
    return out[0], out[1:]


def pairs_next(sc, my, far, vown, aff, entries):
    blocks, quarter, width = vown.shape
    aff_spec, own_spec, out_specs, out_shapes = pair_specs(blocks, quarter, width, entries)

    def slot_map(k):
        def index(s, sc, my):
            group = jnp.maximum(jnp.minimum(s, last_step(sc, entries)) - 1, 0)
            return (sc[group * LANES + k], 0, 0)

        return index

    return pl.pallas_call(
        functools.partial(pairs_next_body, entries),
        out_shape=out_shapes,
        grid_spec=pltpu.PrefetchScalarGridSpec(
            num_scalar_prefetch=2,
            grid=(1 + entries // LANES,),
            in_specs=[aff_spec]
            + [pl.BlockSpec((1, quarter, width), slot_map(k)) for k in range(LANES)]
            + [own_spec],
            out_specs=out_specs,
        ),
        name="pairs_next",
    )(sc, my, aff, *[far] * LANES, vown)


def gram_body(nvec, my_ref, *refs):
    part_refs, prod_ref, piece_refs, full = refs[:nvec], refs[nvec], refs[nvec + 1 : -1], refs[-1]
    p = (part_refs[0][...] + part_refs[1][...]) + (part_refs[2][...] + part_refs[3][...])
    prod_ref[...] = p
    full[...] = lax.dot_general(
        p, p, (((0,), (0,)), ((), ())), precision=HI, preferred_element_type=f32
    )
    for d, piece in enumerate(piece_refs):
        rows = piece.shape[0]
        piece[...] = full[pl.ds(pl.multiple_of((my_ref[0] ^ d) * rows, rows), rows), :]


def gram(parts, my):
    nvec = len(parts)
    rows, width = parts[0].shape
    vmem = pl.BlockSpec(memory_space=pltpu.VMEM)
    out = pl.pallas_call(
        functools.partial(gram_body, nvec),
        out_shape=[jax.ShapeDtypeStruct((rows, width), f32)]
        + [jax.ShapeDtypeStruct((width // nvec, width), f32)] * nvec,
        in_specs=[pl.BlockSpec(memory_space=pltpu.SMEM)] + [vmem] * nvec,
        out_specs=[vmem] * (nvec + 1),
        scratch_shapes=[pltpu.VMEM((width, width), f32)],
        name="gram",
    )(my, *parts)
    return out[0], out[1:]


def lane_splat(x, j):
    return jnp.broadcast_to(x[:, j : j + 1], x.shape)


def row_splat(x, s):
    return jnp.broadcast_to(x[s : s + 1, :], x.shape)


def split3(x):
    high = x.astype(bf16)
    rest = x - high.astype(f32)
    mid = rest.astype(bf16)
    return high, mid, (rest - mid.astype(f32)).astype(bf16)


PANEL = 16


def inverse_factor(a):
    n = a.shape[0]
    row_at = lax.broadcasted_iota(jnp.int32, (PANEL, n), 0)
    square = (n, n)
    on_diag = lax.broadcasted_iota(jnp.int32, square, 0) == lax.broadcasted_iota(jnp.int32, square, 1)
    inv = jnp.where(on_diag, 1.0, 0.0).astype(f32)
    done = []
    for j in range(0, n, PANEL):
        top, itop = a[:PANEL, :], inv[:PANEL, :]
        cols = [lane_splat(top, j + c) for c in range(PANEL)]
        for c in range(PANEL):
            scale = lax.rsqrt(row_splat(cols[c], c))
            below = jnp.where(row_at > c, cols[c] * scale, 0.0)
            for k in range(c + 1, PANEL):
                cols[k] = cols[k] - below * (row_splat(cols[k], c) * scale)
            row, irow = row_splat(top, c) * scale, row_splat(itop, c) * scale
            top = jnp.where(row_at == c, row, top - below * row)
            itop = jnp.where(row_at == c, irow, itop - below * irow)
        done.append(itop)
        if j + PANEL < n:
            h, m, l = split3(top)
            ih, im, il = split3(itop)
            left = jnp.concatenate([h, h, m, h, l, m], axis=0)
            right = jnp.concatenate(
                [jnp.concatenate([h, m, h, l, h, m], axis=0), jnp.concatenate([ih, im, ih, il, ih, im], axis=0)],
                axis=1,
            )
            update = lax.dot_general(left, right, (((0,), (0,)), ((), ())), preferred_element_type=f32)
            update = update[j + PANEL :, :]
            a = a[PANEL:, :] - update[:, :n]
            inv = inv[PANEL:, :] - update[:, n:]
    return jnp.concatenate(done, axis=0)


def whiten(my_ref, chunk_refs, a_ref, w_ref, label_total):
    n = a_ref.shape[0]
    h = n // 2
    rows = chunk_refs[0].shape[0]
    for d, chunk in enumerate(chunk_refs):
        at = pl.multiple_of((my_ref[0] ^ d) * rows, rows)
        a_ref[pl.ds(at, rows), :] = chunk[...] * (1.0 / label_total)
    w11 = inverse_factor(a_ref[:h, :h])
    low = nt(a_ref[h:, :h], w11, precision=HI)
    w22 = inverse_factor(a_ref[h:, h:] - nt(low, low, precision=HI))
    mid = jnp.dot(low, w11, precision=HI, preferred_element_type=f32)
    w_ref[:h, :h] = w11
    w_ref[:h, h:] = jnp.zeros((h, h), f32)
    w_ref[h:, :h] = -jnp.dot(w22, mid, precision=HI, preferred_element_type=f32)
    w_ref[h:, h:] = w22


def step_body(label_total, chunks, my_ref, pb_ref, *refs):
    chunk_refs, (prod_ref, own_ref, out_ref, a_ref, w_ref, sem) = refs[:chunks], refs[chunks:]
    whiten(my_ref, chunk_refs, a_ref, w_ref, label_total)
    blocks, quarter, width = own_ref.shape
    own_ref[...] = nt(prod_ref[...], w_ref[...], precision=HI).astype(bf16).reshape(own_ref.shape)
    spread(own_ref, pb_ref, out_ref, sem)


def step(gram_chunks, prod, my, pb, blocks, quarter, label_total):
    width = prod.shape[1]
    slots = pb.shape[0]
    chunks = len(gram_chunks)
    smem = pl.BlockSpec(memory_space=pltpu.SMEM)
    vmem = pl.BlockSpec(memory_space=pltpu.VMEM)
    return pl.pallas_call(
        functools.partial(step_body, label_total, chunks),
        out_shape=(
            jax.ShapeDtypeStruct((blocks, quarter, width), bf16),
            jax.ShapeDtypeStruct((slots, quarter, width), bf16),
        ),
        in_specs=[smem, smem] + [vmem] * (chunks + 1),
        out_specs=(vmem, pl.BlockSpec(memory_space=pl.ANY)),
        scratch_shapes=[
            pltpu.VMEM((width, width), f32),
            pltpu.VMEM((width, width), f32),
            pltpu.SemaphoreType.DMA((slots,)),
        ],
        name="step",
    )(my, pb, *gram_chunks, prod)


def last_body(label_total, chunks, my_ref, *refs):
    chunk_refs, (prod_ref, out_ref, a_ref, w_ref) = refs[:chunks], refs[chunks:]
    whiten(my_ref, chunk_refs, a_ref, w_ref, label_total)
    quarters, narrow, rows = out_ref.shape
    for q in range(quarters):
        out_ref[q] = nt(w_ref[q * narrow : (q + 1) * narrow, :], prod_ref[...], precision=HI)


def last(gram_chunks, prod, my, quarters, label_total):
    rows, width = prod.shape
    chunks = len(gram_chunks)
    smem = pl.BlockSpec(memory_space=pltpu.SMEM)
    vmem = pl.BlockSpec(memory_space=pltpu.VMEM)
    return pl.pallas_call(
        functools.partial(last_body, label_total, chunks),
        out_shape=jax.ShapeDtypeStruct((quarters, width // quarters, rows), f32),
        in_specs=[smem] + [vmem] * (chunks + 1),
        out_specs=vmem,
        scratch_shapes=[pltpu.VMEM((width, width), f32), pltpu.VMEM((width, width), f32)],
        name="last",
    )(my, *gram_chunks, prod)


def make(mesh):
    nblk, nvec = mesh.shape["blk"], mesh.shape["vec"]

    def swap(x, owner_bits, vec_bits):
        perm = [
            (o * nvec + v, (o ^ owner_bits) * nvec + (v ^ vec_bits))
            for o in range(nblk)
            for v in range(nvec)
        ]
        return lax.ppermute(x, AXES, perm)

    def exchange(x, axis):
        return lax.all_to_all(x, axis, split_axis=0, concat_axis=0, tiled=True)

    def gram_sum(pieces):
        total = pieces[0]
        for d in range(1, nvec):
            total = total + swap(pieces[d], 0, d)
        for shift in (1, 3):
            got = [swap(total, d << shift, 0) for d in (1, 2, 3)]
            total = (total + got[0]) + (got[1] + got[2])
        total = total + swap(total, 1, 0)
        return [total] + [swap(total, 0, d) for d in range(1, nvec)]

    def body(x, basis, pair_block, pair_live):
        rows, feat = x.shape
        narrow = basis.shape[1]
        blocks = rows // BS
        quarter = BS // nvec
        label_total = rows * nblk
        v = lax.axis_index("vec")
        my = v[None].astype(jnp.int32)
        pb, live = pair_block[0], pair_live[0]

        vt = jnp.transpose(basis.T.astype(bf16).reshape(narrow, blocks, nvec, quarter), (2, 0, 1, 3))
        vt = vt.reshape(nvec, narrow, blocks * quarter)
        vts = [lax.dynamic_index_in_dim(vt, v ^ d, 0, keepdims=False) for d in range(nvec)]
        vts = [vts[0]] + [swap(vts[d], 0, d) for d in range(1, nvec)]
        owner = lax.axis_index("blk").astype(jnp.int32)
        pbs = [
            pair_block if d == 0 else swap(pair_block, d << SHIFT[line], 0)
            for line, _ in LINES
            for d in range(NEAR)
        ]
        vown, packs = send_start(own_quarter(x, my, blocks, quarter), vts, my)
        has = [
            packs[h] if d == 0 else swap(packs[h], d << SHIFT[line], 0)
            for h, (line, _) in enumerate(LINES)
            for d in range(NEAR)
        ]
        sends = relay(pbs, has, owner[None])
        fars = [
            sends[h * SIDE + o] if o == 0 else swap(sends[h * SIDE + o], offset(axis, o), 0)
            for h, (_, axis) in enumerate(LINES)
            for o in range(SIDE)
        ]

        entries = entries_of(nblk, blocks)
        sc = pair_table(pb, live, owner, blocks, entries)
        unit = normalize(x)

        aff, out = pairs_first(sc, my, unit, fars, vown, entries)
        for it in range(ITERS):
            if it:
                out = pairs_next(sc, my, far, vown, aff, entries)
            out = [o.reshape(blocks * quarter, nvec * narrow) for o in out]
            parts = [out[0]] + [swap(out[d], 0, d) for d in range(1, nvec)]
            prod, pieces = gram(parts, my)
            sums = gram_sum(pieces)
            if it + 1 < ITERS:
                vown, vsend = step(sums, prod, my, pb, blocks, quarter, label_total)
                far = exchange(vsend, "blk")
        final = exchange(last(sums, prod, my, nvec, label_total), "vec")
        final = final.reshape(nvec, narrow, blocks, quarter)
        return jnp.transpose(final, (2, 0, 3, 1)).reshape(rows, narrow)

    return body


def solution(mesh):
    in_specs = (P("blk", None), P("blk", "vec"), P("blk", None), P("blk", None))
    return jax.shard_map(
        make(mesh), mesh=mesh, in_specs=in_specs, out_specs=P("blk", "vec"), check_vma=False
    )
```

```python
import functools

import jax
import jax.numpy as jnp
from jax import lax
from jax.experimental import pallas as pl
from jax.experimental.pallas import tpu as pltpu
from jax.sharding import PartitionSpec as P

BS = 512
ITERS = 2
SHARPNESS = 5.0
EPSILON = 1e-06
AXES = ("blk", "vec")
HI = lax.Precision.HIGHEST
f32 = jnp.float32
bf16 = jnp.bfloat16


def normalize(features):
    widened = features.astype(f32)
    inv_norm = lax.rsqrt(jnp.mean(widened * widened, axis=-1, keepdims=True) + EPSILON)
    return (widened * inv_norm).astype(bf16)


LOG2E = 1.4426950408889634


def affinity(scores_sum, width):
    bent = scores_sum * (SHARPNESS * LOG2E / width)
    shift = SHARPNESS * LOG2E
    return (jnp.exp2(bent - shift) - jnp.exp2(-shift - bent)).astype(bf16)


def nt(a, b, **kw):
    return lax.dot_general(a, b, (((1,), (1,)), ((), ())), preferred_element_type=f32, **kw)


def spread(src, pb_ref, out_ref, sem):
    slots = out_ref.shape[0]
    for c in range(slots):
        pltpu.make_async_copy(src.at[pb_ref[c]], out_ref.at[c], sem.at[c]).start()
    for c in range(slots):
        pltpu.make_async_copy(src.at[0], out_ref.at[c], sem.at[c]).wait()


def own_quarter_body(my_ref, x_ref, out_ref, buf, sem):
    blocks, quarter, _ = buf.shape
    for t in range(blocks):
        pltpu.make_async_copy(
            x_ref.at[pl.ds(t * BS + my_ref[0] * quarter, quarter)], buf.at[t], sem.at[t]
        ).start()
    for t in range(blocks):
        pltpu.make_async_copy(x_ref.at[pl.ds(0, quarter)], buf.at[t], sem.at[t]).wait()
        out_ref[t] = normalize(buf[t])


def own_quarter(x, my, blocks, quarter):
    feat = x.shape[1]
    return pl.pallas_call(
        own_quarter_body,
        out_shape=jax.ShapeDtypeStruct((blocks, quarter, feat), bf16),
        in_specs=[pl.BlockSpec(memory_space=pltpu.SMEM), pl.BlockSpec(memory_space=pl.ANY)],
        out_specs=pl.BlockSpec(memory_space=pltpu.VMEM),
        scratch_shapes=[pltpu.VMEM((blocks, quarter, feat), bf16), pltpu.SemaphoreType.DMA((blocks,))],
        name="own_quarter",
    )(my, x)


def send_body(my_ref, unit_ref, v0_ref, v1_ref, v2_ref, v3_ref, own_ref, *pack_refs):
    blocks, quarter, feat = unit_ref.shape
    narrow = v0_ref.shape[0]
    v = my_ref[0]
    for d, vt_ref in enumerate((v0_ref, v1_ref, v2_ref, v3_ref)):
        turned = vt_ref[...].astype(f32).T.astype(bf16).reshape(blocks, quarter, narrow)
        for g in range(4):

            @pl.when((v ^ d) == g)
            def _():
                own_ref[:, :, g * narrow : (g + 1) * narrow] = turned

    half = quarter // 2
    for h, pack in enumerate(pack_refs):
        rows = slice(h * half, (h + 1) * half)
        for t in range(blocks):
            pack[t, :, :feat] = unit_ref[t, rows]
            pack[t, :, feat:] = own_ref[t, rows]


def send_start(unit_quarter, vts, my):
    blocks, quarter, feat = unit_quarter.shape
    width = vts[0].shape[0] * len(vts)
    vmem = pl.BlockSpec(memory_space=pltpu.VMEM)
    out = pl.pallas_call(
        send_body,
        out_shape=[jax.ShapeDtypeStruct((blocks, quarter, width), bf16)]
        + [jax.ShapeDtypeStruct((blocks, quarter // 2, feat + width), bf16)] * 2,
        in_specs=[pl.BlockSpec(memory_space=pltpu.SMEM), vmem] + [vmem] * len(vts),
        out_specs=[vmem] * 3,
        name="send_start",
    )(my, unit_quarter, *vts)
    return out[0], out[1:]


SHIFT = {"z": 3, "y": 1}
LINES = (("z", "y"), ("y", "z"))
NEAR = 4
SIDE = 8
STEPS = (0, 1, 3, 2)
FORWARD = (0, 4, 5, 2, 3, 6, 7, 1)


def near_at(h, d):
    return 2 * STEPS.index(d) + h


def side_at(h, o):
    return 2 * FORWARD.index(o) + h


def offset(axis, o):
    return (o >> 1) << SHIFT[axis] | (o & 1)


def relay_body(at_ref, *refs):
    pb_refs, has_refs = refs[: 2 * NEAR], refs[2 * NEAR : 4 * NEAR]
    out_refs, sem = refs[4 * NEAR : -1], refs[-1]
    owner = at_ref[0]

    def copy(h, o, d, block):
        return pltpu.make_async_copy(
            has_refs[near_at(h, d)].at[block], out_refs[side_at(h, o)].at[d], sem.at[h, o, d]
        )

    places = [(h, o, d) for h in range(2) for o in range(SIDE) for d in range(NEAR)]
    for h, o, d in places:
        copy(h, o, d, pb_refs[near_at(h, d)][0, owner ^ offset(LINES[h][1], o)]).start()
    for h, o, d in places:
        copy(h, o, d, 0).wait()


def relay(pbs, has, owner):
    blocks, half, width = has[0].shape
    hbm = pl.BlockSpec(memory_space=pl.ANY)
    smem = pl.BlockSpec(memory_space=pltpu.SMEM)
    return pl.pallas_call(
        relay_body,
        out_shape=[jax.ShapeDtypeStruct((NEAR, half, width), bf16)] * (2 * SIDE),
        in_specs=[smem] * (1 + len(pbs)) + [pl.BlockSpec(memory_space=pltpu.VMEM)] * len(has),
        out_specs=[hbm] * (2 * SIDE),
        scratch_shapes=[pltpu.SemaphoreType.DMA((2, SIDE, NEAR))],
        name="relay",
    )(owner, *pbs, *has)


LANES = 4


def pair_table(pb, live, owner, blocks, entries):
    slots = pb.shape[0]
    on = live > 0
    c = jnp.arange(slots, dtype=jnp.int32)
    same = (pb[:, None] == pb[None, :]) & on[None, :] & (c[None, :] < c[:, None])
    rank = jnp.sum(same.astype(jnp.int32), axis=1)
    t = jnp.arange(blocks, dtype=jnp.int32)
    number = jnp.sum(((pb[None, :] == t[:, None]) & on[None, :]).astype(jnp.int32), axis=1)
    even = (number + 1) // 2 * 2
    end = jnp.sum(jnp.where(t[None, :] <= t[:, None], even[None, :], 0), axis=1)
    start = jnp.sum(jnp.where(pb[:, None] == t[None, :], (end - even)[None, :], 0), axis=1)
    at = jnp.where(on, start + rank, -1)
    j = jnp.arange(entries, dtype=jnp.int32)
    hit = at[None, :] == j[:, None]
    slot = jnp.sum(jnp.where(hit, c[None, :], 0), axis=1)
    use = jnp.sum(hit.astype(jnp.int32), axis=1)
    target = jnp.minimum(jnp.sum((j[:, None] >= end[None, :]).astype(jnp.int32), axis=1), blocks - 1)
    by_offset = jnp.sum(jnp.where((owner ^ c)[:, None] == c[None, :], at[None, :], 0), axis=1)
    return jnp.concatenate([slot, use, target, end[-1:], by_offset])


def entries_of(slots, blocks):
    return -(-(slots - 1 + blocks) // LANES) * LANES


def add_product(out_refs, t, p, first):
    quarter = out_refs[0].shape[1]
    for d, out_ref in enumerate(out_refs):
        piece = p[d * quarter : (d + 1) * quarter]
        if first:
            out_ref[t] = piece
        else:
            out_ref[t] += piece


def pairs_first_body(entries, sc_ref, my_ref, unit_ref, *refs):
    far_refs, refs = refs[: 2 * SIDE], refs[2 * SIDE :]
    vown_ref, aff_ref, out_refs, (buf, sem) = refs[0], refs[1], refs[2:-2], refs[-2:]
    quarter = vown_ref.shape[1]
    half = quarter // 2
    feat = unit_ref.shape[1]
    s = pl.program_id(0)
    v = my_ref[0]

    def copy(h, side, line, entry):
        return pltpu.make_async_copy(
            far_refs[side_at(h, side)].at[line], buf.at[entry, pl.ds(h * half, half)], sem.at[h, entry]
        )

    def target_rows(t):
        return jnp.concatenate(
            [unit_ref[pl.ds(t * BS + (v ^ d) * quarter, quarter), :] for d in range(len(out_refs))], axis=0
        )

    def fetch(low, high):
        for o in range(1, NEAR * NEAR * 2):
            z, y, core = o >> 3, (o >> 1) & 3, o & 1
            entry = sc_ref[3 * entries + 1 + o]

            @pl.when((entry >= low) & (entry < high))
            def _():
                copy(0, 2 * y + core, z, entry).start()
                copy(1, 2 * z + core, y, entry).start()

    @pl.when(s == 0)
    def _():
        fetch(0, 3 * LANES)
        fetch(3 * LANES, entries)
        for t in range(LANES):
            rows = target_rows(t)
            aff = affinity(nt(rows, rows[:quarter]), feat)
            aff_ref[t] = aff
            add_product(out_refs, t, jnp.dot(aff, vown_ref[t], preferred_element_type=f32), True)

    @pl.when((s > 0) & ((s - 1) * LANES < sc_ref[3 * entries]))
    def _():
        prods = []
        first = jnp.maximum((s - 1) * LANES, 0)
        for k in range(LANES):

            @pl.when(sc_ref[entries + first + k] > 0)
            def _():
                copy(0, 0, 0, first + k).wait()
                copy(1, 0, 0, first + k).wait()

        for k in range(0, LANES, 2):
            t = sc_ref[2 * entries + first + k]
            rhs = jnp.concatenate([buf[first + k + i, :, :feat] for i in range(2)], axis=0)
            both = affinity(nt(target_rows(t), rhs), feat)
            affs, vecs = [], []
            for i in range(2):
                used = sc_ref[entries + first + k + i] > 0
                aff = both[:, i * quarter : (i + 1) * quarter]
                aff = jnp.where(used, aff, jnp.zeros_like(aff))
                vec = buf[first + k + i, :, feat:]
                vecs.append(jnp.where(used, vec, jnp.zeros_like(vec)))
                aff_ref[k + i] = aff
                affs.append(aff)
            p = jnp.dot(
                jnp.concatenate(affs, axis=1), jnp.concatenate(vecs, axis=0), preferred_element_type=f32
            )
            prods.append((t, p))
        for t, p in prods:
            add_product(out_refs, t, p, False)


def pairs_next_body(entries, sc_ref, my_ref, aff_ref, *refs):
    far_refs, vown_ref, out_refs = refs[:LANES], refs[LANES], refs[LANES + 1 :]
    s = pl.program_id(0)

    @pl.when(s == 0)
    def _():
        for t in range(LANES):
            p = jnp.dot(aff_ref[t], vown_ref[t], preferred_element_type=f32)
            add_product(out_refs, t, p, True)

    @pl.when((s > 0) & ((s - 1) * LANES < sc_ref[3 * entries]))
    def _():
        first = jnp.maximum((s - 1) * LANES, 0)
        for k in range(0, LANES, 2):
            t = sc_ref[2 * entries + first + k]
            aff = jnp.concatenate([aff_ref[k], aff_ref[k + 1]], axis=1)
            vec = jnp.concatenate([far_refs[k][0], far_refs[k + 1][0]], axis=0)
            add_product(out_refs, t, jnp.dot(aff, vec, preferred_element_type=f32), False)


def last_step(sc, entries):
    return (sc[3 * entries] + LANES - 1) // LANES


def pair_specs(blocks, quarter, width, entries):
    quarters = BS // quarter
    whole = lambda s, sc, my: (0, 0, 0)
    aff_spec = pl.BlockSpec(
        (LANES, BS, quarter), lambda s, sc, my: (jnp.minimum(s, last_step(sc, entries)), 0, 0)
    )
    own_spec = pl.BlockSpec((blocks, quarter, width), whole)
    out_shapes = [jax.ShapeDtypeStruct((blocks, quarter, width), f32)] * quarters
    return aff_spec, own_spec, [own_spec] * quarters, out_shapes


def pairs_first(sc, my, unit, fars, vown, entries):
    blocks, quarter, width = vown.shape
    far_width = fars[0].shape[2]
    aff_spec, own_spec, out_specs, out_shapes = pair_specs(blocks, quarter, width, entries)
    out = pl.pallas_call(
        functools.partial(pairs_first_body, entries),
        out_shape=[jax.ShapeDtypeStruct((blocks + entries, BS, quarter), bf16)] + out_shapes,
        grid_spec=pltpu.PrefetchScalarGridSpec(
            num_scalar_prefetch=2,
            grid=(1 + entries // LANES,),
            in_specs=[pl.BlockSpec(unit.shape, lambda s, sc, my: (0, 0))]
            + [pl.BlockSpec(memory_space=pl.ANY)] * len(fars)
            + [own_spec],
            out_specs=[aff_spec] + out_specs,
            scratch_shapes=[
                pltpu.VMEM((entries, quarter, far_width), bf16),
                pltpu.SemaphoreType.DMA((2, entries)),
            ],
        ),
        name="pairs_first",
    )(sc, my, unit, *fars, vown)
    return out[0], out[1:]


def pairs_next(sc, my, far, vown, aff, entries):
    blocks, quarter, width = vown.shape
    aff_spec, own_spec, out_specs, out_shapes = pair_specs(blocks, quarter, width, entries)

    def slot_map(k):
        def index(s, sc, my):
            group = jnp.maximum(jnp.minimum(s, last_step(sc, entries)) - 1, 0)
            return (sc[group * LANES + k], 0, 0)

        return index

    return pl.pallas_call(
        functools.partial(pairs_next_body, entries),
        out_shape=out_shapes,
        grid_spec=pltpu.PrefetchScalarGridSpec(
            num_scalar_prefetch=2,
            grid=(1 + entries // LANES,),
            in_specs=[aff_spec]
            + [pl.BlockSpec((1, quarter, width), slot_map(k)) for k in range(LANES)]
            + [own_spec],
            out_specs=out_specs,
        ),
        name="pairs_next",
    )(sc, my, aff, *[far] * LANES, vown)


def gram_body(nvec, my_ref, *refs):
    part_refs, prod_ref, piece_refs, full = refs[:nvec], refs[nvec], refs[nvec + 1 : -1], refs[-1]
    p = (part_refs[0][...] + part_refs[1][...]) + (part_refs[2][...] + part_refs[3][...])
    prod_ref[...] = p
    full[...] = lax.dot_general(
        p, p, (((0,), (0,)), ((), ())), precision=HI, preferred_element_type=f32
    )
    for d, piece in enumerate(piece_refs):
        rows = piece.shape[0]
        piece[...] = full[pl.ds(pl.multiple_of((my_ref[0] ^ d) * rows, rows), rows), :]


def gram(parts, my):
    nvec = len(parts)
    rows, width = parts[0].shape
    vmem = pl.BlockSpec(memory_space=pltpu.VMEM)
    out = pl.pallas_call(
        functools.partial(gram_body, nvec),
        out_shape=[jax.ShapeDtypeStruct((rows, width), f32)]
        + [jax.ShapeDtypeStruct((width // nvec, width), f32)] * nvec,
        in_specs=[pl.BlockSpec(memory_space=pltpu.SMEM)] + [vmem] * nvec,
        out_specs=[vmem] * (nvec + 1),
        scratch_shapes=[pltpu.VMEM((width, width), f32)],
        name="gram",
    )(my, *parts)
    return out[0], out[1:]


def lane_splat(x, j):
    return jnp.broadcast_to(x[:, j : j + 1], x.shape)


def row_splat(x, s):
    return jnp.broadcast_to(x[s : s + 1, :], x.shape)


def split3(x):
    high = x.astype(bf16)
    rest = x - high.astype(f32)
    mid = rest.astype(bf16)
    return high, mid, (rest - mid.astype(f32)).astype(bf16)


PANEL = 16


def inverse_factor(a):
    n = a.shape[0]
    row_at = lax.broadcasted_iota(jnp.int32, (PANEL, n), 0)
    square = (n, n)
    on_diag = lax.broadcasted_iota(jnp.int32, square, 0) == lax.broadcasted_iota(jnp.int32, square, 1)
    inv = jnp.where(on_diag, 1.0, 0.0).astype(f32)
    done = []
    for j in range(0, n, PANEL):
        top, itop = a[:PANEL, :], inv[:PANEL, :]
        cols = [lane_splat(top, j + c) for c in range(PANEL)]
        for c in range(PANEL):
            scale = lax.rsqrt(row_splat(cols[c], c))
            below = jnp.where(row_at > c, cols[c] * scale, 0.0)
            for k in range(c + 1, PANEL):
                cols[k] = cols[k] - below * (row_splat(cols[k], c) * scale)
            row, irow = row_splat(top, c) * scale, row_splat(itop, c) * scale
            top = jnp.where(row_at == c, row, top - below * row)
            itop = jnp.where(row_at == c, irow, itop - below * irow)
        done.append(itop)
        if j + PANEL < n:
            h, m, l = split3(top)
            ih, im, il = split3(itop)
            left = jnp.concatenate([h, h, m, h, l, m], axis=0)
            right = jnp.concatenate(
                [jnp.concatenate([h, m, h, l, h, m], axis=0), jnp.concatenate([ih, im, ih, il, ih, im], axis=0)],
                axis=1,
            )
            update = lax.dot_general(left, right, (((0,), (0,)), ((), ())), preferred_element_type=f32)
            update = update[j + PANEL :, :]
            a = a[PANEL:, :] - update[:, :n]
            inv = inv[PANEL:, :] - update[:, n:]
    return jnp.concatenate(done, axis=0)


def whiten(my_ref, chunk_refs, a_ref, w_ref, label_total):
    n = a_ref.shape[0]
    h = n // 2
    rows = chunk_refs[0].shape[0]
    for d, chunk in enumerate(chunk_refs):
        at = pl.multiple_of((my_ref[0] ^ d) * rows, rows)
        a_ref[pl.ds(at, rows), :] = chunk[...] * (1.0 / label_total)

    def half(i, _):
        at = pl.multiple_of(i * h, h)
        w = inverse_factor(a_ref[pl.ds(at, h), :h])
        w_ref[pl.ds(at, h), h:] = w

        @pl.when(i == 0)
        def _():
            low = nt(a_ref[h:, :h], w, precision=HI)
            w_ref[:h, :h] = jnp.dot(low, w, precision=HI, preferred_element_type=f32)
            a_ref[h:, :h] = a_ref[h:, h:] - nt(low, low, precision=HI)

        return 0

    lax.fori_loop(0, 2, half, 0)
    w11, w22, mid = w_ref[:h, h:], w_ref[h:, h:], w_ref[:h, :h]
    w_ref[h:, :h] = -jnp.dot(w22, mid, precision=HI, preferred_element_type=f32)
    w_ref[:h, :h] = w11
    w_ref[:h, h:] = jnp.zeros((h, h), f32)


def step_body(label_total, chunks, my_ref, pb_ref, *refs):
    chunk_refs, (prod_ref, own_ref, out_ref, a_ref, w_ref, sem) = refs[:chunks], refs[chunks:]
    whiten(my_ref, chunk_refs, a_ref, w_ref, label_total)
    blocks, quarter, width = own_ref.shape
    own_ref[...] = nt(prod_ref[...], w_ref[...], precision=HI).astype(bf16).reshape(own_ref.shape)
    spread(own_ref, pb_ref, out_ref, sem)


def step(gram_chunks, prod, my, pb, blocks, quarter, label_total):
    width = prod.shape[1]
    slots = pb.shape[0]
    chunks = len(gram_chunks)
    smem = pl.BlockSpec(memory_space=pltpu.SMEM)
    vmem = pl.BlockSpec(memory_space=pltpu.VMEM)
    return pl.pallas_call(
        functools.partial(step_body, label_total, chunks),
        out_shape=(
            jax.ShapeDtypeStruct((blocks, quarter, width), bf16),
            jax.ShapeDtypeStruct((slots, quarter, width), bf16),
        ),
        in_specs=[smem, smem] + [vmem] * (chunks + 1),
        out_specs=(vmem, pl.BlockSpec(memory_space=pl.ANY)),
        scratch_shapes=[
            pltpu.VMEM((width, width), f32),
            pltpu.VMEM((width, width), f32),
            pltpu.SemaphoreType.DMA((slots,)),
        ],
        name="step",
    )(my, pb, *gram_chunks, prod)


def last_body(label_total, chunks, my_ref, *refs):
    chunk_refs, (prod_ref, out_ref, a_ref, w_ref) = refs[:chunks], refs[chunks:]
    whiten(my_ref, chunk_refs, a_ref, w_ref, label_total)
    quarters, narrow, rows = out_ref.shape
    for q in range(quarters):
        out_ref[q] = nt(w_ref[q * narrow : (q + 1) * narrow, :], prod_ref[...], precision=HI)


def last(gram_chunks, prod, my, quarters, label_total):
    rows, width = prod.shape
    chunks = len(gram_chunks)
    smem = pl.BlockSpec(memory_space=pltpu.SMEM)
    vmem = pl.BlockSpec(memory_space=pltpu.VMEM)
    return pl.pallas_call(
        functools.partial(last_body, label_total, chunks),
        out_shape=jax.ShapeDtypeStruct((quarters, width // quarters, rows), f32),
        in_specs=[smem] + [vmem] * (chunks + 1),
        out_specs=vmem,
        scratch_shapes=[pltpu.VMEM((width, width), f32), pltpu.VMEM((width, width), f32)],
        name="last",
    )(my, *gram_chunks, prod)


def make(mesh):
    nblk, nvec = mesh.shape["blk"], mesh.shape["vec"]

    def swap(x, owner_bits, vec_bits):
        perm = [
            (o * nvec + v, (o ^ owner_bits) * nvec + (v ^ vec_bits))
            for o in range(nblk)
            for v in range(nvec)
        ]
        return lax.ppermute(x, AXES, perm)

    def exchange(x, axis):
        return lax.all_to_all(x, axis, split_axis=0, concat_axis=0, tiled=True)

    def gram_sum(pieces):
        total = pieces[0]
        for d in range(1, nvec):
            total = total + swap(pieces[d], 0, d)
        for shift in (1, 3):
            got = [swap(total, d << shift, 0) for d in (1, 2, 3)]
            total = (total + got[0]) + (got[1] + got[2])
        total = total + swap(total, 1, 0)
        return [total] + [swap(total, 0, d) for d in range(1, nvec)]

    def body(x, basis, pair_block, pair_live):
        rows, feat = x.shape
        narrow = basis.shape[1]
        blocks = rows // BS
        quarter = BS // nvec
        label_total = rows * nblk
        v = lax.axis_index("vec")
        my = v[None].astype(jnp.int32)
        pb, live = pair_block[0], pair_live[0]

        vt = jnp.transpose(basis.T.astype(bf16).reshape(narrow, blocks, nvec, quarter), (2, 0, 1, 3))
        vt = vt.reshape(nvec, narrow, blocks * quarter)
        vts = [lax.dynamic_index_in_dim(vt, v ^ d, 0, keepdims=False) for d in range(nvec)]
        vts = [vts[0]] + [swap(vts[d], 0, d) for d in range(1, nvec)]
        owner = lax.axis_index("blk").astype(jnp.int32)
        vown, packs = send_start(own_quarter(x, my, blocks, quarter), vts, my)
        pair_late, packs = lax.optimization_barrier((pair_block, packs))
        def along(x, h, d):
            return x if d == 0 else swap(x, d << SHIFT[LINES[h][0]], 0)

        has = [along(packs[h], h, d) for d in STEPS for h in range(2)]
        pbs = [along(pair_late, h, d) for d in STEPS for h in range(2)]
        sends = relay(pbs, has, owner[None])
        fars = [
            sends[side_at(h, o)] if o == 0 else swap(sends[side_at(h, o)], offset(LINES[h][1], o), 0)
            for o in FORWARD
            for h in range(2)
        ]

        entries = entries_of(nblk, blocks)
        sc = pair_table(pb, live, owner, blocks, entries)
        unit = normalize(x)

        aff, out = pairs_first(sc, my, unit, fars, vown, entries)
        for it in range(ITERS):
            if it:
                out = pairs_next(sc, my, far, vown, aff, entries)
            out = [o.reshape(blocks * quarter, nvec * narrow) for o in out]
            parts = [out[0]] + [swap(out[d], 0, d) for d in range(1, nvec)]
            prod, pieces = gram(parts, my)
            sums = gram_sum(pieces)
            if it + 1 < ITERS:
                vown, vsend = step(sums, prod, my, pb, blocks, quarter, label_total)
                far = exchange(vsend, "blk")
        final = exchange(last(sums, prod, my, nvec, label_total), "vec")
        final = final.reshape(nvec, narrow, blocks, quarter)
        return jnp.transpose(final, (2, 0, 3, 1)).reshape(rows, narrow)

    return body


def solution(mesh):
    in_specs = (P("blk", None), P("blk", "vec"), P("blk", None), P("blk", None))
    return jax.shard_map(
        make(mesh), mesh=mesh, in_specs=in_specs, out_specs=P("blk", "vec"), check_vma=False
    )
```

```python
import functools

import jax
import jax.numpy as jnp
from jax import lax
from jax.experimental import pallas as pl
from jax.experimental.pallas import tpu as pltpu
from jax.sharding import PartitionSpec as P

BS = 512
ITERS = 2
SHARPNESS = 5.0
EPSILON = 1e-06
AXES = ("blk", "vec")
HI = lax.Precision.HIGHEST
f32 = jnp.float32
bf16 = jnp.bfloat16


def normalize(features):
    widened = features.astype(f32)
    inv_norm = lax.rsqrt(jnp.mean(widened * widened, axis=-1, keepdims=True) + EPSILON)
    return (widened * inv_norm).astype(bf16)


LOG2E = 1.4426950408889634


def affinity(scores_sum, width):
    bent = scores_sum * (SHARPNESS * LOG2E / width)
    shift = SHARPNESS * LOG2E
    return (jnp.exp2(bent - shift) - jnp.exp2(-shift - bent)).astype(bf16)


def nt(a, b, **kw):
    return lax.dot_general(a, b, (((1,), (1,)), ((), ())), preferred_element_type=f32, **kw)


def spread(src, pb_ref, out_ref, sem):
    slots = out_ref.shape[0]
    for c in range(slots):
        pltpu.make_async_copy(src.at[pb_ref[c]], out_ref.at[c], sem.at[c]).start()
    for c in range(slots):
        pltpu.make_async_copy(src.at[0], out_ref.at[c], sem.at[c]).wait()


def own_quarter_body(my_ref, x_ref, *refs):
    half_refs, (buf, sem) = refs[:2], refs[2:]
    blocks, quarter, _ = buf.shape
    half = quarter // 2
    for t in range(blocks):
        pltpu.make_async_copy(
            x_ref.at[pl.ds(t * BS + my_ref[0] * quarter, quarter)], buf.at[t], sem.at[t]
        ).start()
    for t in range(blocks):
        pltpu.make_async_copy(x_ref.at[pl.ds(0, quarter)], buf.at[t], sem.at[t]).wait()
        unit = normalize(buf[t])
        for h, out_ref in enumerate(half_refs):
            out_ref[t] = unit[h * half : (h + 1) * half]


def own_quarter(x, my, blocks, quarter):
    feat = x.shape[1]
    vmem = pl.BlockSpec(memory_space=pltpu.VMEM)
    return pl.pallas_call(
        own_quarter_body,
        out_shape=[jax.ShapeDtypeStruct((blocks, quarter // 2, feat), bf16)] * 2,
        in_specs=[pl.BlockSpec(memory_space=pltpu.SMEM), pl.BlockSpec(memory_space=pl.ANY)],
        out_specs=[vmem] * 2,
        scratch_shapes=[pltpu.VMEM((blocks, quarter, feat), bf16), pltpu.SemaphoreType.DMA((blocks,))],
        name="own_quarter",
    )(my, x)


NOTE = 16


def send_body(my_ref, pb_ref, v0_ref, v1_ref, v2_ref, v3_ref, own_ref, *pack_refs):
    blocks, quarter, _ = own_ref.shape
    narrow = v0_ref.shape[0]
    v = my_ref[0]
    for d, vt_ref in enumerate((v0_ref, v1_ref, v2_ref, v3_ref)):
        turned = vt_ref[...].astype(f32).T.astype(bf16).reshape(blocks, quarter, narrow)
        for g in range(4):

            @pl.when((v ^ d) == g)
            def _():
                own_ref[:, :, g * narrow : (g + 1) * narrow] = turned

    half = quarter // 2
    for h, pack in enumerate(pack_refs):
        pack[:, :half] = own_ref[:, h * half : (h + 1) * half]
        pack[:, half:] = jnp.zeros((blocks, NOTE, pack.shape[2]), bf16)
        pack[0, half:, :128] = pb_ref[...].astype(bf16)


def send_start(vts, pb, my, blocks, quarter):
    width = vts[0].shape[0] * len(vts)
    vmem = pl.BlockSpec(memory_space=pltpu.VMEM)
    note = jnp.broadcast_to(jnp.pad(pb.astype(f32), (0, 128 - pb.shape[0])), (NOTE, 128))
    out = pl.pallas_call(
        send_body,
        out_shape=[jax.ShapeDtypeStruct((blocks, quarter, width), bf16)]
        + [jax.ShapeDtypeStruct((blocks, quarter // 2 + NOTE, width), bf16)] * 2,
        in_specs=[pl.BlockSpec(memory_space=pltpu.SMEM), vmem] + [vmem] * len(vts),
        out_specs=[vmem] * 3,
        name="send_start",
    )(my, note, *vts)
    return out[0], out[1:]


SHIFT = {"z": 3, "y": 1}
LINES = (("z", "y"), ("y", "z"))
NEAR = 4
SIDE = 8
STEPS = (0, 1, 3, 2)
FORWARD = (0, 4, 5, 2, 3, 6, 7, 1)


def near_at(h, d):
    return 2 * STEPS.index(d) + h


def side_at(h, o):
    return 2 * FORWARD.index(o) + h


def offset(axis, o):
    return (o >> 1) << SHIFT[axis] | (o & 1)


def relay_body(at_ref, *refs):
    feat_refs, vec_refs = refs[: 2 * NEAR], refs[2 * NEAR : 4 * NEAR]
    out_refs, (notes, pbs, sem_note, sem) = refs[4 * NEAR : -4], refs[-4:]
    owner = at_ref[0]
    _, half, feat = feat_refs[0].shape
    width = vec_refs[0].shape[2]
    for i, vec in enumerate(vec_refs):
        notes[i : i + 1] = vec[0, half:, :128].astype(f32)[:1].astype(jnp.int32)
    note_copy = pltpu.make_async_copy(notes, pbs, sem_note)
    note_copy.start()
    note_copy.wait()

    def copies(h, o, d, block):
        out = out_refs[side_at(h, o)]
        i = near_at(h, d)
        return (
            pltpu.make_async_copy(feat_refs[i].at[block], out.at[d, :, pl.ds(0, feat)], sem.at[0, h, o, d]),
            pltpu.make_async_copy(
                vec_refs[i].at[block, pl.ds(0, half)], out.at[d, :, pl.ds(feat, width)], sem.at[1, h, o, d]
            ),
        )

    places = [(h, o, d) for o in FORWARD for h in range(2) for d in range(NEAR)]
    for h, o, d in places:
        for copy in copies(h, o, d, pbs[near_at(h, d), owner ^ offset(LINES[h][1], o)]):
            copy.start()
    for h, o, d in places:
        for copy in copies(h, o, d, 0):
            copy.wait()


def relay(feats, vecs, owner):
    _, half, feat = feats[0].shape
    hbm = pl.BlockSpec(memory_space=pl.ANY)
    vmem = pl.BlockSpec(memory_space=pltpu.VMEM)
    shape = jax.ShapeDtypeStruct((NEAR, half, feat + vecs[0].shape[2]), bf16)
    return pl.pallas_call(
        relay_body,
        out_shape=[shape] * (2 * SIDE),
        in_specs=[pl.BlockSpec(memory_space=pltpu.SMEM)] + [vmem] * (len(feats) + len(vecs)),
        out_specs=[hbm] * (2 * SIDE),
        scratch_shapes=[
            pltpu.VMEM((2 * NEAR, 128), jnp.int32),
            pltpu.SMEM((2 * NEAR, 128), jnp.int32),
            pltpu.SemaphoreType.DMA(()),
            pltpu.SemaphoreType.DMA((2, 2, SIDE, NEAR)),
        ],
        name="relay",
    )(owner, *feats, *vecs)


LANES = 4


def pair_table(pb, live, owner, blocks, entries):
    slots = pb.shape[0]
    on = live > 0
    c = jnp.arange(slots, dtype=jnp.int32)
    same = (pb[:, None] == pb[None, :]) & on[None, :] & (c[None, :] < c[:, None])
    rank = jnp.sum(same.astype(jnp.int32), axis=1)
    t = jnp.arange(blocks, dtype=jnp.int32)
    number = jnp.sum(((pb[None, :] == t[:, None]) & on[None, :]).astype(jnp.int32), axis=1)
    even = (number + 1) // 2 * 2
    end = jnp.sum(jnp.where(t[None, :] <= t[:, None], even[None, :], 0), axis=1)
    start = jnp.sum(jnp.where(pb[:, None] == t[None, :], (end - even)[None, :], 0), axis=1)
    at = jnp.where(on, start + rank, -1)
    j = jnp.arange(entries, dtype=jnp.int32)
    hit = at[None, :] == j[:, None]
    slot = jnp.sum(jnp.where(hit, c[None, :], 0), axis=1)
    use = jnp.sum(hit.astype(jnp.int32), axis=1)
    target = jnp.minimum(jnp.sum((j[:, None] >= end[None, :]).astype(jnp.int32), axis=1), blocks - 1)
    by_offset = jnp.sum(jnp.where((owner ^ c)[:, None] == c[None, :], at[None, :], 0), axis=1)
    return jnp.concatenate([slot, use, target, end[-1:], by_offset])


def entries_of(slots, blocks):
    return -(-(slots - 1 + blocks) // LANES) * LANES


def add_product(out_refs, t, p, first):
    quarter = out_refs[0].shape[1]
    for d, out_ref in enumerate(out_refs):
        piece = p[d * quarter : (d + 1) * quarter]
        if first:
            out_ref[t] = piece
        else:
            out_ref[t] += piece


def pairs_first_body(entries, sc_ref, my_ref, unit_ref, *refs):
    far_refs, refs = refs[: 2 * SIDE], refs[2 * SIDE :]
    vown_ref, aff_ref, out_refs, (buf, sem) = refs[0], refs[1], refs[2:-2], refs[-2:]
    quarter = vown_ref.shape[1]
    half = quarter // 2
    feat = unit_ref.shape[1]
    s = pl.program_id(0)
    v = my_ref[0]

    def copy(h, side, line, entry):
        return pltpu.make_async_copy(
            far_refs[side_at(h, side)].at[line], buf.at[entry, pl.ds(h * half, half)], sem.at[h, entry]
        )

    def target_rows(t):
        return jnp.concatenate(
            [unit_ref[pl.ds(t * BS + (v ^ d) * quarter, quarter), :] for d in range(len(out_refs))], axis=0
        )

    def fetch(low, high):
        for o in range(1, NEAR * NEAR * 2):
            z, y, core = o >> 3, (o >> 1) & 3, o & 1
            entry = sc_ref[3 * entries + 1 + o]

            @pl.when((entry >= low) & (entry < high))
            def _():
                copy(0, 2 * y + core, z, entry).start()
                copy(1, 2 * z + core, y, entry).start()

    @pl.when(s == 0)
    def _():
        fetch(0, 3 * LANES)
        fetch(3 * LANES, entries)
        for t in range(LANES):
            rows = target_rows(t)
            aff = affinity(nt(rows, rows[:quarter]), feat)
            aff_ref[t] = aff
            add_product(out_refs, t, jnp.dot(aff, vown_ref[t], preferred_element_type=f32), True)

    @pl.when((s > 0) & ((s - 1) * LANES < sc_ref[3 * entries]))
    def _():
        prods = []
        first = jnp.maximum((s - 1) * LANES, 0)
        for k in range(LANES):

            @pl.when(sc_ref[entries + first + k] > 0)
            def _():
                copy(0, 0, 0, first + k).wait()
                copy(1, 0, 0, first + k).wait()

        for k in range(0, LANES, 2):
            t = sc_ref[2 * entries + first + k]
            rhs = jnp.concatenate([buf[first + k + i, :, :feat] for i in range(2)], axis=0)
            both = affinity(nt(target_rows(t), rhs), feat)
            affs, vecs = [], []
            for i in range(2):
                used = sc_ref[entries + first + k + i] > 0
                aff = both[:, i * quarter : (i + 1) * quarter]
                aff = jnp.where(used, aff, jnp.zeros_like(aff))
                vec = buf[first + k + i, :, feat:]
                vecs.append(jnp.where(used, vec, jnp.zeros_like(vec)))
                aff_ref[k + i] = aff
                affs.append(aff)
            p = jnp.dot(
                jnp.concatenate(affs, axis=1), jnp.concatenate(vecs, axis=0), preferred_element_type=f32
            )
            prods.append((t, p))
        for t, p in prods:
            add_product(out_refs, t, p, False)


def pairs_next_body(entries, sc_ref, my_ref, aff_ref, *refs):
    far_refs, vown_ref, out_refs = refs[:LANES], refs[LANES], refs[LANES + 1 :]
    s = pl.program_id(0)

    @pl.when(s == 0)
    def _():
        for t in range(LANES):
            p = jnp.dot(aff_ref[t], vown_ref[t], preferred_element_type=f32)
            add_product(out_refs, t, p, True)

    @pl.when((s > 0) & ((s - 1) * LANES < sc_ref[3 * entries]))
    def _():
        first = jnp.maximum((s - 1) * LANES, 0)
        for k in range(0, LANES, 2):
            t = sc_ref[2 * entries + first + k]
            aff = jnp.concatenate([aff_ref[k], aff_ref[k + 1]], axis=1)
            vec = jnp.concatenate([far_refs[k][0], far_refs[k + 1][0]], axis=0)
            add_product(out_refs, t, jnp.dot(aff, vec, preferred_element_type=f32), False)


def last_step(sc, entries):
    return (sc[3 * entries] + LANES - 1) // LANES


def pair_specs(blocks, quarter, width, entries):
    quarters = BS // quarter
    whole = lambda s, sc, my: (0, 0, 0)
    aff_spec = pl.BlockSpec(
        (LANES, BS, quarter), lambda s, sc, my: (jnp.minimum(s, last_step(sc, entries)), 0, 0)
    )
    own_spec = pl.BlockSpec((blocks, quarter, width), whole)
    out_shapes = [jax.ShapeDtypeStruct((blocks, quarter, width), f32)] * quarters
    return aff_spec, own_spec, [own_spec] * quarters, out_shapes


def pairs_first(sc, my, unit, fars, vown, entries):
    blocks, quarter, width = vown.shape
    far_width = fars[0].shape[2]
    aff_spec, own_spec, out_specs, out_shapes = pair_specs(blocks, quarter, width, entries)
    out = pl.pallas_call(
        functools.partial(pairs_first_body, entries),
        out_shape=[jax.ShapeDtypeStruct((blocks + entries, BS, quarter), bf16)] + out_shapes,
        grid_spec=pltpu.PrefetchScalarGridSpec(
            num_scalar_prefetch=2,
            grid=(1 + entries // LANES,),
            in_specs=[pl.BlockSpec(unit.shape, lambda s, sc, my: (0, 0))]
            + [pl.BlockSpec(memory_space=pl.ANY)] * len(fars)
            + [own_spec],
            out_specs=[aff_spec] + out_specs,
            scratch_shapes=[
                pltpu.VMEM((entries, quarter, far_width), bf16),
                pltpu.SemaphoreType.DMA((2, entries)),
            ],
        ),
        name="pairs_first",
    )(sc, my, unit, *fars, vown)
    return out[0], out[1:]


def pairs_next(sc, my, far, vown, aff, entries):
    blocks, quarter, width = vown.shape
    aff_spec, own_spec, out_specs, out_shapes = pair_specs(blocks, quarter, width, entries)

    def slot_map(k):
        def index(s, sc, my):
            group = jnp.maximum(jnp.minimum(s, last_step(sc, entries)) - 1, 0)
            return (sc[group * LANES + k], 0, 0)

        return index

    return pl.pallas_call(
        functools.partial(pairs_next_body, entries),
        out_shape=out_shapes,
        grid_spec=pltpu.PrefetchScalarGridSpec(
            num_scalar_prefetch=2,
            grid=(1 + entries // LANES,),
            in_specs=[aff_spec]
            + [pl.BlockSpec((1, quarter, width), slot_map(k)) for k in range(LANES)]
            + [own_spec],
            out_specs=out_specs,
        ),
        name="pairs_next",
    )(sc, my, aff, *[far] * LANES, vown)


def gram_body(nvec, my_ref, *refs):
    part_refs, prod_ref, piece_refs, full = refs[:nvec], refs[nvec], refs[nvec + 1 : -1], refs[-1]
    p = (part_refs[0][...] + part_refs[1][...]) + (part_refs[2][...] + part_refs[3][...])
    prod_ref[...] = p
    full[...] = lax.dot_general(
        p, p, (((0,), (0,)), ((), ())), precision=HI, preferred_element_type=f32
    )
    for d, piece in enumerate(piece_refs):
        rows = piece.shape[0]
        piece[...] = full[pl.ds(pl.multiple_of((my_ref[0] ^ d) * rows, rows), rows), :]


def gram(parts, my):
    nvec = len(parts)
    rows, width = parts[0].shape
    vmem = pl.BlockSpec(memory_space=pltpu.VMEM)
    out = pl.pallas_call(
        functools.partial(gram_body, nvec),
        out_shape=[jax.ShapeDtypeStruct((rows, width), f32)]
        + [jax.ShapeDtypeStruct((width // nvec, width), f32)] * nvec,
        in_specs=[pl.BlockSpec(memory_space=pltpu.SMEM)] + [vmem] * nvec,
        out_specs=[vmem] * (nvec + 1),
        scratch_shapes=[pltpu.VMEM((width, width), f32)],
        name="gram",
    )(my, *parts)
    return out[0], out[1:]


def lane_splat(x, j):
    return jnp.broadcast_to(x[:, j : j + 1], x.shape)


def row_splat(x, s):
    return jnp.broadcast_to(x[s : s + 1, :], x.shape)


def split3(x):
    high = x.astype(bf16)
    rest = x - high.astype(f32)
    mid = rest.astype(bf16)
    return high, mid, (rest - mid.astype(f32)).astype(bf16)


PANEL = 16


def inverse_factor(a):
    n = a.shape[0]
    row_at = lax.broadcasted_iota(jnp.int32, (PANEL, n), 0)
    square = (n, n)
    on_diag = lax.broadcasted_iota(jnp.int32, square, 0) == lax.broadcasted_iota(jnp.int32, square, 1)
    inv = jnp.where(on_diag, 1.0, 0.0).astype(f32)
    done = []
    for j in range(0, n, PANEL):
        top, itop = a[:PANEL, :], inv[:PANEL, :]
        cols = [lane_splat(top, j + c) for c in range(PANEL)]
        for c in range(PANEL):
            scale = lax.rsqrt(row_splat(cols[c], c))
            below = jnp.where(row_at > c, cols[c] * scale, 0.0)
            for k in range(c + 1, PANEL):
                cols[k] = cols[k] - below * (row_splat(cols[k], c) * scale)
            row, irow = row_splat(top, c) * scale, row_splat(itop, c) * scale
            top = jnp.where(row_at == c, row, top - below * row)
            itop = jnp.where(row_at == c, irow, itop - below * irow)
        done.append(itop)
        if j + PANEL < n:
            h, m, l = split3(top)
            ih, im, il = split3(itop)
            left = jnp.concatenate([h, h, m, h, l, m], axis=0)
            right = jnp.concatenate(
                [jnp.concatenate([h, m, h, l, h, m], axis=0), jnp.concatenate([ih, im, ih, il, ih, im], axis=0)],
                axis=1,
            )
            update = lax.dot_general(left, right, (((0,), (0,)), ((), ())), preferred_element_type=f32)
            update = update[j + PANEL :, :]
            a = a[PANEL:, :] - update[:, :n]
            inv = inv[PANEL:, :] - update[:, n:]
    return jnp.concatenate(done, axis=0)


def whiten(my_ref, chunk_refs, a_ref, w_ref, label_total):
    n = a_ref.shape[0]
    h = n // 2
    rows = chunk_refs[0].shape[0]
    for d, chunk in enumerate(chunk_refs):
        at = pl.multiple_of((my_ref[0] ^ d) * rows, rows)
        a_ref[pl.ds(at, rows), :] = chunk[...] * (1.0 / label_total)

    def half(i, _):
        at = pl.multiple_of(i * h, h)
        w = inverse_factor(a_ref[pl.ds(at, h), :h])
        w_ref[pl.ds(at, h), h:] = w

        @pl.when(i == 0)
        def _():
            low = nt(a_ref[h:, :h], w, precision=HI)
            w_ref[:h, :h] = jnp.dot(low, w, precision=HI, preferred_element_type=f32)
            a_ref[h:, :h] = a_ref[h:, h:] - nt(low, low, precision=HI)

        return 0

    lax.fori_loop(0, 2, half, 0)
    w11, w22, mid = w_ref[:h, h:], w_ref[h:, h:], w_ref[:h, :h]
    w_ref[h:, :h] = -jnp.dot(w22, mid, precision=HI, preferred_element_type=f32)
    w_ref[:h, :h] = w11
    w_ref[:h, h:] = jnp.zeros((h, h), f32)


def step_body(label_total, chunks, my_ref, pb_ref, *refs):
    chunk_refs, (prod_ref, own_ref, out_ref, a_ref, w_ref, sem) = refs[:chunks], refs[chunks:]
    whiten(my_ref, chunk_refs, a_ref, w_ref, label_total)
    blocks, quarter, width = own_ref.shape
    own_ref[...] = nt(prod_ref[...], w_ref[...], precision=HI).astype(bf16).reshape(own_ref.shape)
    spread(own_ref, pb_ref, out_ref, sem)


def step(gram_chunks, prod, my, pb, blocks, quarter, label_total):
    width = prod.shape[1]
    slots = pb.shape[0]
    chunks = len(gram_chunks)
    smem = pl.BlockSpec(memory_space=pltpu.SMEM)
    vmem = pl.BlockSpec(memory_space=pltpu.VMEM)
    return pl.pallas_call(
        functools.partial(step_body, label_total, chunks),
        out_shape=(
            jax.ShapeDtypeStruct((blocks, quarter, width), bf16),
            jax.ShapeDtypeStruct((slots, quarter, width), bf16),
        ),
        in_specs=[smem, smem] + [vmem] * (chunks + 1),
        out_specs=(vmem, pl.BlockSpec(memory_space=pl.ANY)),
        scratch_shapes=[
            pltpu.VMEM((width, width), f32),
            pltpu.VMEM((width, width), f32),
            pltpu.SemaphoreType.DMA((slots,)),
        ],
        name="step",
    )(my, pb, *gram_chunks, prod)


def last_body(label_total, chunks, my_ref, *refs):
    chunk_refs, (prod_ref, out_ref, a_ref, w_ref) = refs[:chunks], refs[chunks:]
    whiten(my_ref, chunk_refs, a_ref, w_ref, label_total)
    quarters, narrow, rows = out_ref.shape
    for q in range(quarters):
        out_ref[q] = nt(w_ref[q * narrow : (q + 1) * narrow, :], prod_ref[...], precision=HI)


def last(gram_chunks, prod, my, quarters, label_total):
    rows, width = prod.shape
    chunks = len(gram_chunks)
    smem = pl.BlockSpec(memory_space=pltpu.SMEM)
    vmem = pl.BlockSpec(memory_space=pltpu.VMEM)
    return pl.pallas_call(
        functools.partial(last_body, label_total, chunks),
        out_shape=jax.ShapeDtypeStruct((quarters, width // quarters, rows), f32),
        in_specs=[smem] + [vmem] * (chunks + 1),
        out_specs=vmem,
        scratch_shapes=[pltpu.VMEM((width, width), f32), pltpu.VMEM((width, width), f32)],
        name="last",
    )(my, *gram_chunks, prod)


def make(mesh):
    nblk, nvec = mesh.shape["blk"], mesh.shape["vec"]

    def swap(x, owner_bits, vec_bits):
        perm = [
            (o * nvec + v, (o ^ owner_bits) * nvec + (v ^ vec_bits))
            for o in range(nblk)
            for v in range(nvec)
        ]
        return lax.ppermute(x, AXES, perm)

    def exchange(x, axis):
        return lax.all_to_all(x, axis, split_axis=0, concat_axis=0, tiled=True)

    def gram_sum(pieces):
        total = pieces[0]
        for d in range(1, nvec):
            total = total + swap(pieces[d], 0, d)
        for shift in (1, 3):
            got = [swap(total, d << shift, 0) for d in (1, 2, 3)]
            total = (total + got[0]) + (got[1] + got[2])
        total = total + swap(total, 1, 0)
        return [total] + [swap(total, 0, d) for d in range(1, nvec)]

    def body(x, basis, pair_block, pair_live):
        rows, feat = x.shape
        narrow = basis.shape[1]
        blocks = rows // BS
        quarter = BS // nvec
        label_total = rows * nblk
        v = lax.axis_index("vec")
        my = v[None].astype(jnp.int32)
        pb, live = pair_block[0], pair_live[0]

        owner = lax.axis_index("blk").astype(jnp.int32)
        units = own_quarter(x, my, blocks, quarter)
        basis, units = lax.optimization_barrier((basis, units))

        def along(x, h, d):
            return x if d == 0 else swap(x, d << SHIFT[LINES[h][0]], 0)

        feats = [along(units[h], h, d) for d in STEPS for h in range(2)]
        vt = jnp.transpose(basis.T.astype(bf16).reshape(narrow, blocks, nvec, quarter), (2, 0, 1, 3))
        vt = vt.reshape(nvec, narrow, blocks * quarter)
        vts = [lax.dynamic_index_in_dim(vt, v ^ d, 0, keepdims=False) for d in range(nvec)]
        vts = [vts[0]] + [swap(vts[d], 0, d) for d in range(1, nvec)]
        vown, packs = send_start(vts, pb, my, blocks, quarter)
        (pb, live), packs = lax.optimization_barrier(((pb, live), packs))
        vecs = [along(packs[h], h, d) for d in STEPS for h in range(2)]
        sends = relay(feats, vecs, owner[None])
        fars = [
            sends[side_at(h, o)] if o == 0 else swap(sends[side_at(h, o)], offset(LINES[h][1], o), 0)
            for o in FORWARD
            for h in range(2)
        ]

        entries = entries_of(nblk, blocks)
        sc = pair_table(pb, live, owner, blocks, entries)
        unit = normalize(x)

        aff, out = pairs_first(sc, my, unit, fars, vown, entries)
        for it in range(ITERS):
            if it:
                out = pairs_next(sc, my, far, vown, aff, entries)
            out = [o.reshape(blocks * quarter, nvec * narrow) for o in out]
            parts = [out[0]] + [swap(out[d], 0, d) for d in range(1, nvec)]
            prod, pieces = gram(parts, my)
            sums = gram_sum(pieces)
            if it + 1 < ITERS:
                vown, vsend = step(sums, prod, my, pb, blocks, quarter, label_total)
                far = exchange(vsend, "blk")
        final = exchange(last(sums, prod, my, nvec, label_total), "vec")
        final = final.reshape(nvec, narrow, blocks, quarter)
        return jnp.transpose(final, (2, 0, 3, 1)).reshape(rows, narrow)

    return body


def solution(mesh):
    in_specs = (P("blk", None), P("blk", "vec"), P("blk", None), P("blk", None))
    return jax.shard_map(
        make(mesh), mesh=mesh, in_specs=in_specs, out_specs=P("blk", "vec"), check_vma=False
    )
```

```python
import functools

import jax
import jax.numpy as jnp
from jax import lax
from jax.experimental import pallas as pl
from jax.experimental.pallas import tpu as pltpu
from jax.sharding import PartitionSpec as P

BS = 512
ITERS = 2
SHARPNESS = 5.0
EPSILON = 1e-06
AXES = ("blk", "vec")
HI = lax.Precision.HIGHEST
f32 = jnp.float32
bf16 = jnp.bfloat16


def normalize(features):
    widened = features.astype(f32)
    inv_norm = lax.rsqrt(jnp.mean(widened * widened, axis=-1, keepdims=True) + EPSILON)
    return (widened * inv_norm).astype(bf16)


LOG2E = 1.4426950408889634


def affinity(scores_sum, width):
    bent = scores_sum * (SHARPNESS * LOG2E / width)
    shift = SHARPNESS * LOG2E
    return (jnp.exp2(bent - shift) - jnp.exp2(-shift - bent)).astype(bf16)


def nt(a, b, **kw):
    return lax.dot_general(a, b, (((1,), (1,)), ((), ())), preferred_element_type=f32, **kw)


def spread(src, pb_ref, out_ref, sem):
    slots = out_ref.shape[0]
    for c in range(slots):
        pltpu.make_async_copy(src.at[pb_ref[c]], out_ref.at[c], sem.at[c]).start()
    for c in range(slots):
        pltpu.make_async_copy(src.at[0], out_ref.at[c], sem.at[c]).wait()


def own_quarter_body(my_ref, x_ref, *refs):
    half_refs, (buf, sem) = refs[:2], refs[2:]
    blocks, quarter, _ = buf.shape
    half = quarter // 2
    for t in range(blocks):
        pltpu.make_async_copy(
            x_ref.at[pl.ds(t * BS + my_ref[0] * quarter, quarter)], buf.at[t], sem.at[t]
        ).start()
    for t in range(blocks):
        pltpu.make_async_copy(x_ref.at[pl.ds(0, quarter)], buf.at[t], sem.at[t]).wait()
        unit = normalize(buf[t])
        for h, out_ref in enumerate(half_refs):
            out_ref[t] = unit[h * half : (h + 1) * half]


def own_quarter(x, my, blocks, quarter):
    feat = x.shape[1]
    vmem = pl.BlockSpec(memory_space=pltpu.VMEM)
    return pl.pallas_call(
        own_quarter_body,
        out_shape=[jax.ShapeDtypeStruct((blocks, quarter // 2, feat), bf16)] * 2,
        in_specs=[pl.BlockSpec(memory_space=pltpu.SMEM), pl.BlockSpec(memory_space=pl.ANY)],
        out_specs=[vmem] * 2,
        scratch_shapes=[pltpu.VMEM((blocks, quarter, feat), bf16), pltpu.SemaphoreType.DMA((blocks,))],
        name="own_quarter",
    )(my, x)


def cut_body(my_ref, basis_ref, *out_refs):
    quarter = BS // len(out_refs)
    for d, out_ref in enumerate(out_refs):
        for t in range(basis_ref.shape[1] // BS):
            at = pl.multiple_of(t * BS + (my_ref[0] ^ d) * quarter, quarter)
            out_ref[:, t * quarter : (t + 1) * quarter] = basis_ref[:, pl.ds(at, quarter)].astype(bf16)


def cut_start(basis_t, my, nvec):
    narrow, rows = basis_t.shape
    vmem = pl.BlockSpec(memory_space=pltpu.VMEM)
    return pl.pallas_call(
        cut_body,
        out_shape=[jax.ShapeDtypeStruct((narrow, rows // nvec), bf16)] * nvec,
        in_specs=[pl.BlockSpec(memory_space=pltpu.SMEM), vmem],
        out_specs=[vmem] * nvec,
        name="cut_start",
    )(my, basis_t)


NOTE = 16


def send_body(my_ref, pb_ref, v0_ref, v1_ref, v2_ref, v3_ref, own_ref, *pack_refs):
    blocks, quarter, _ = own_ref.shape
    narrow = v0_ref.shape[0]
    v = my_ref[0]
    for d, vt_ref in enumerate((v0_ref, v1_ref, v2_ref, v3_ref)):
        turned = vt_ref[...].astype(f32).T.astype(bf16).reshape(blocks, quarter, narrow)
        for g in range(4):

            @pl.when((v ^ d) == g)
            def _():
                own_ref[:, :, g * narrow : (g + 1) * narrow] = turned

    half = quarter // 2
    for h, pack in enumerate(pack_refs):
        pack[:, :half] = own_ref[:, h * half : (h + 1) * half]
        pack[:, half:] = jnp.zeros((blocks, NOTE, pack.shape[2]), bf16)
        pack[0, half:, :128] = pb_ref[...].astype(bf16)


def send_start(vts, pb, my, blocks, quarter):
    width = vts[0].shape[0] * len(vts)
    vmem = pl.BlockSpec(memory_space=pltpu.VMEM)
    note = jnp.broadcast_to(jnp.pad(pb.astype(f32), (0, 128 - pb.shape[0])), (NOTE, 128))
    out = pl.pallas_call(
        send_body,
        out_shape=[jax.ShapeDtypeStruct((blocks, quarter, width), bf16)]
        + [jax.ShapeDtypeStruct((blocks, quarter // 2 + NOTE, width), bf16)] * 2,
        in_specs=[pl.BlockSpec(memory_space=pltpu.SMEM), vmem] + [vmem] * len(vts),
        out_specs=[vmem] * 3,
        name="send_start",
    )(my, note, *vts)
    return out[0], out[1:]


SHIFT = {"z": 3, "y": 1}
LINES = (("z", "y"), ("y", "z"))
NEAR = 4
SIDE = 8
STEPS = (0, 1, 3, 2)
FORWARD = (0, 4, 5, 2, 3, 6, 7, 1)


def near_at(h, d):
    return 2 * STEPS.index(d) + h


def side_at(h, o):
    return 2 * FORWARD.index(o) + h


def offset(axis, o):
    return (o >> 1) << SHIFT[axis] | (o & 1)


def relay_body(at_ref, *refs):
    feat_refs, vec_refs = refs[: 2 * NEAR], refs[2 * NEAR : 4 * NEAR]
    out_refs, (notes, pbs, sem_note, sem) = refs[4 * NEAR : -4], refs[-4:]
    owner = at_ref[0]
    _, half, feat = feat_refs[0].shape
    width = vec_refs[0].shape[2]
    for i, vec in enumerate(vec_refs):
        notes[i : i + 1] = vec[0, half:, :128].astype(f32)[:1].astype(jnp.int32)
    note_copy = pltpu.make_async_copy(notes, pbs, sem_note)
    note_copy.start()
    note_copy.wait()

    def copies(h, o, d, block):
        out = out_refs[side_at(h, o)]
        i = near_at(h, d)
        return (
            pltpu.make_async_copy(feat_refs[i].at[block], out.at[d, :, pl.ds(0, feat)], sem.at[0, h, o, d]),
            pltpu.make_async_copy(
                vec_refs[i].at[block, pl.ds(0, half)], out.at[d, :, pl.ds(feat, width)], sem.at[1, h, o, d]
            ),
        )

    places = [(h, o, d) for o in FORWARD for h in range(2) for d in range(NEAR)]
    for h, o, d in places:
        for copy in copies(h, o, d, pbs[near_at(h, d), owner ^ offset(LINES[h][1], o)]):
            copy.start()
    for h, o, d in places:
        for copy in copies(h, o, d, 0):
            copy.wait()


def relay(feats, vecs, owner):
    _, half, feat = feats[0].shape
    hbm = pl.BlockSpec(memory_space=pl.ANY)
    vmem = pl.BlockSpec(memory_space=pltpu.VMEM)
    shape = jax.ShapeDtypeStruct((NEAR, half, feat + vecs[0].shape[2]), bf16)
    return pl.pallas_call(
        relay_body,
        out_shape=[shape] * (2 * SIDE),
        in_specs=[pl.BlockSpec(memory_space=pltpu.SMEM)] + [vmem] * (len(feats) + len(vecs)),
        out_specs=[hbm] * (2 * SIDE),
        scratch_shapes=[
            pltpu.VMEM((2 * NEAR, 128), jnp.int32),
            pltpu.SMEM((2 * NEAR, 128), jnp.int32),
            pltpu.SemaphoreType.DMA(()),
            pltpu.SemaphoreType.DMA((2, 2, SIDE, NEAR)),
        ],
        name="relay",
    )(owner, *feats, *vecs)


LANES = 4


def pair_table(pb, live, owner, blocks, entries):
    slots = pb.shape[0]
    on = live > 0
    c = jnp.arange(slots, dtype=jnp.int32)
    same = (pb[:, None] == pb[None, :]) & on[None, :] & (c[None, :] < c[:, None])
    rank = jnp.sum(same.astype(jnp.int32), axis=1)
    t = jnp.arange(blocks, dtype=jnp.int32)
    number = jnp.sum(((pb[None, :] == t[:, None]) & on[None, :]).astype(jnp.int32), axis=1)
    even = (number + 1) // 2 * 2
    end = jnp.sum(jnp.where(t[None, :] <= t[:, None], even[None, :], 0), axis=1)
    start = jnp.sum(jnp.where(pb[:, None] == t[None, :], (end - even)[None, :], 0), axis=1)
    at = jnp.where(on, start + rank, -1)
    j = jnp.arange(entries, dtype=jnp.int32)
    hit = at[None, :] == j[:, None]
    slot = jnp.sum(jnp.where(hit, c[None, :], 0), axis=1)
    use = jnp.sum(hit.astype(jnp.int32), axis=1)
    target = jnp.minimum(jnp.sum((j[:, None] >= end[None, :]).astype(jnp.int32), axis=1), blocks - 1)
    by_offset = jnp.sum(jnp.where((owner ^ c)[:, None] == c[None, :], at[None, :], 0), axis=1)
    return jnp.concatenate([slot, use, target, end[-1:], by_offset])


def entries_of(slots, blocks):
    return -(-(slots - 1 + blocks) // LANES) * LANES


def add_product(out_refs, t, p, first):
    quarter = out_refs[0].shape[1]
    for d, out_ref in enumerate(out_refs):
        piece = p[d * quarter : (d + 1) * quarter]
        if first:
            out_ref[t] = piece
        else:
            out_ref[t] += piece


def pairs_first_body(entries, sc_ref, my_ref, unit_ref, *refs):
    far_refs, refs = refs[: 2 * SIDE], refs[2 * SIDE :]
    vown_ref, aff_ref, out_refs, (buf, sem) = refs[0], refs[1], refs[2:-2], refs[-2:]
    quarter = vown_ref.shape[1]
    half = quarter // 2
    feat = unit_ref.shape[1]
    s = pl.program_id(0)
    v = my_ref[0]

    def copy(h, side, line, entry):
        return pltpu.make_async_copy(
            far_refs[side_at(h, side)].at[line], buf.at[entry, pl.ds(h * half, half)], sem.at[h, entry]
        )

    def target_rows(t):
        return jnp.concatenate(
            [unit_ref[pl.ds(t * BS + (v ^ d) * quarter, quarter), :] for d in range(len(out_refs))], axis=0
        )

    def fetch(low, high):
        for o in range(1, NEAR * NEAR * 2):
            z, y, core = o >> 3, (o >> 1) & 3, o & 1
            entry = sc_ref[3 * entries + 1 + o]

            @pl.when((entry >= low) & (entry < high))
            def _():
                copy(0, 2 * y + core, z, entry).start()
                copy(1, 2 * z + core, y, entry).start()

    @pl.when(s == 0)
    def _():
        fetch(0, 3 * LANES)
        fetch(3 * LANES, entries)
        for t in range(LANES):
            rows = target_rows(t)
            aff = affinity(nt(rows, rows[:quarter]), feat)
            aff_ref[t] = aff
            add_product(out_refs, t, jnp.dot(aff, vown_ref[t], preferred_element_type=f32), True)

    @pl.when((s > 0) & ((s - 1) * LANES < sc_ref[3 * entries]))
    def _():
        prods = []
        first = jnp.maximum((s - 1) * LANES, 0)
        for k in range(LANES):

            @pl.when(sc_ref[entries + first + k] > 0)
            def _():
                copy(0, 0, 0, first + k).wait()
                copy(1, 0, 0, first + k).wait()

        for k in range(0, LANES, 2):
            t = sc_ref[2 * entries + first + k]
            rhs = jnp.concatenate([buf[first + k + i, :, :feat] for i in range(2)], axis=0)
            both = affinity(nt(target_rows(t), rhs), feat)
            affs, vecs = [], []
            for i in range(2):
                used = sc_ref[entries + first + k + i] > 0
                aff = both[:, i * quarter : (i + 1) * quarter]
                aff = jnp.where(used, aff, jnp.zeros_like(aff))
                vec = buf[first + k + i, :, feat:]
                vecs.append(jnp.where(used, vec, jnp.zeros_like(vec)))
                aff_ref[k + i] = aff
                affs.append(aff)
            p = jnp.dot(
                jnp.concatenate(affs, axis=1), jnp.concatenate(vecs, axis=0), preferred_element_type=f32
            )
            prods.append((t, p))
        for t, p in prods:
            add_product(out_refs, t, p, False)


def pairs_next_body(entries, sc_ref, my_ref, aff_ref, *refs):
    far_refs, vown_ref, out_refs = refs[:LANES], refs[LANES], refs[LANES + 1 :]
    s = pl.program_id(0)

    @pl.when(s == 0)
    def _():
        for t in range(LANES):
            p = jnp.dot(aff_ref[t], vown_ref[t], preferred_element_type=f32)
            add_product(out_refs, t, p, True)

    @pl.when((s > 0) & ((s - 1) * LANES < sc_ref[3 * entries]))
    def _():
        first = jnp.maximum((s - 1) * LANES, 0)
        for k in range(0, LANES, 2):
            t = sc_ref[2 * entries + first + k]
            aff = jnp.concatenate([aff_ref[k], aff_ref[k + 1]], axis=1)
            vec = jnp.concatenate([far_refs[k][0], far_refs[k + 1][0]], axis=0)
            add_product(out_refs, t, jnp.dot(aff, vec, preferred_element_type=f32), False)


def last_step(sc, entries):
    return (sc[3 * entries] + LANES - 1) // LANES


def pair_specs(blocks, quarter, width, entries):
    quarters = BS // quarter
    whole = lambda s, sc, my: (0, 0, 0)
    aff_spec = pl.BlockSpec(
        (LANES, BS, quarter), lambda s, sc, my: (jnp.minimum(s, last_step(sc, entries)), 0, 0)
    )
    own_spec = pl.BlockSpec((blocks, quarter, width), whole)
    out_shapes = [jax.ShapeDtypeStruct((blocks, quarter, width), f32)] * quarters
    return aff_spec, own_spec, [own_spec] * quarters, out_shapes


def pairs_first(sc, my, unit, fars, vown, entries):
    blocks, quarter, width = vown.shape
    far_width = fars[0].shape[2]
    aff_spec, own_spec, out_specs, out_shapes = pair_specs(blocks, quarter, width, entries)
    out = pl.pallas_call(
        functools.partial(pairs_first_body, entries),
        out_shape=[jax.ShapeDtypeStruct((blocks + entries, BS, quarter), bf16)] + out_shapes,
        grid_spec=pltpu.PrefetchScalarGridSpec(
            num_scalar_prefetch=2,
            grid=(1 + entries // LANES,),
            in_specs=[pl.BlockSpec(unit.shape, lambda s, sc, my: (0, 0))]
            + [pl.BlockSpec(memory_space=pl.ANY)] * len(fars)
            + [own_spec],
            out_specs=[aff_spec] + out_specs,
            scratch_shapes=[
                pltpu.VMEM((entries, quarter, far_width), bf16),
                pltpu.SemaphoreType.DMA((2, entries)),
            ],
        ),
        name="pairs_first",
    )(sc, my, unit, *fars, vown)
    return out[0], out[1:]


def pairs_next(sc, my, far, vown, aff, entries):
    blocks, quarter, width = vown.shape
    aff_spec, own_spec, out_specs, out_shapes = pair_specs(blocks, quarter, width, entries)

    def slot_map(k):
        def index(s, sc, my):
            group = jnp.maximum(jnp.minimum(s, last_step(sc, entries)) - 1, 0)
            return (sc[group * LANES + k], 0, 0)

        return index

    return pl.pallas_call(
        functools.partial(pairs_next_body, entries),
        out_shape=out_shapes,
        grid_spec=pltpu.PrefetchScalarGridSpec(
            num_scalar_prefetch=2,
            grid=(1 + entries // LANES,),
            in_specs=[aff_spec]
            + [pl.BlockSpec((1, quarter, width), slot_map(k)) for k in range(LANES)]
            + [own_spec],
            out_specs=out_specs,
        ),
        name="pairs_next",
    )(sc, my, aff, *[far] * LANES, vown)


def gram_body(nvec, my_ref, *refs):
    part_refs, prod_ref, piece_refs, full = refs[:nvec], refs[nvec], refs[nvec + 1 : -1], refs[-1]
    p = (part_refs[0][...] + part_refs[1][...]) + (part_refs[2][...] + part_refs[3][...])
    prod_ref[...] = p
    full[...] = lax.dot_general(
        p, p, (((0,), (0,)), ((), ())), precision=HI, preferred_element_type=f32
    )
    for d, piece in enumerate(piece_refs):
        rows = piece.shape[0]
        piece[...] = full[pl.ds(pl.multiple_of((my_ref[0] ^ d) * rows, rows), rows), :]


def gram(parts, my):
    nvec = len(parts)
    rows, width = parts[0].shape
    vmem = pl.BlockSpec(memory_space=pltpu.VMEM)
    out = pl.pallas_call(
        functools.partial(gram_body, nvec),
        out_shape=[jax.ShapeDtypeStruct((rows, width), f32)]
        + [jax.ShapeDtypeStruct((width // nvec, width), f32)] * nvec,
        in_specs=[pl.BlockSpec(memory_space=pltpu.SMEM)] + [vmem] * nvec,
        out_specs=[vmem] * (nvec + 1),
        scratch_shapes=[pltpu.VMEM((width, width), f32)],
        name="gram",
    )(my, *parts)
    return out[0], out[1:]


def lane_splat(x, j):
    return jnp.broadcast_to(x[:, j : j + 1], x.shape)


def row_splat(x, s):
    return jnp.broadcast_to(x[s : s + 1, :], x.shape)


def split3(x):
    high = x.astype(bf16)
    rest = x - high.astype(f32)
    mid = rest.astype(bf16)
    return high, mid, (rest - mid.astype(f32)).astype(bf16)


PANEL = 16


def inverse_factor(a):
    n = a.shape[0]
    row_at = lax.broadcasted_iota(jnp.int32, (PANEL, n), 0)
    square = (n, n)
    on_diag = lax.broadcasted_iota(jnp.int32, square, 0) == lax.broadcasted_iota(jnp.int32, square, 1)
    inv = jnp.where(on_diag, 1.0, 0.0).astype(f32)
    done = []
    for j in range(0, n, PANEL):
        top, itop = a[:PANEL, :], inv[:PANEL, :]
        cols = [lane_splat(top, j + c) for c in range(PANEL)]
        for c in range(PANEL):
            scale = lax.rsqrt(row_splat(cols[c], c))
            below = jnp.where(row_at > c, cols[c] * scale, 0.0)
            for k in range(c + 1, PANEL):
                cols[k] = cols[k] - below * (row_splat(cols[k], c) * scale)
            row, irow = row_splat(top, c) * scale, row_splat(itop, c) * scale
            top = jnp.where(row_at == c, row, top - below * row)
            itop = jnp.where(row_at == c, irow, itop - below * irow)
        done.append(itop)
        if j + PANEL < n:
            h, m, l = split3(top)
            ih, im, il = split3(itop)
            left = jnp.concatenate([h, h, m, h, l, m], axis=0)
            right = jnp.concatenate(
                [jnp.concatenate([h, m, h, l, h, m], axis=0), jnp.concatenate([ih, im, ih, il, ih, im], axis=0)],
                axis=1,
            )
            update = lax.dot_general(left, right, (((0,), (0,)), ((), ())), preferred_element_type=f32)
            update = update[j + PANEL :, :]
            a = a[PANEL:, :] - update[:, :n]
            inv = inv[PANEL:, :] - update[:, n:]
    return jnp.concatenate(done, axis=0)


def whiten(my_ref, chunk_refs, a_ref, w_ref, label_total):
    n = a_ref.shape[0]
    h = n // 2
    rows = chunk_refs[0].shape[0]
    for d, chunk in enumerate(chunk_refs):
        at = pl.multiple_of((my_ref[0] ^ d) * rows, rows)
        a_ref[pl.ds(at, rows), :] = chunk[...] * (1.0 / label_total)

    def half(i, _):
        at = pl.multiple_of(i * h, h)
        w = inverse_factor(a_ref[pl.ds(at, h), :h])
        w_ref[pl.ds(at, h), h:] = w

        @pl.when(i == 0)
        def _():
            low = nt(a_ref[h:, :h], w, precision=HI)
            w_ref[:h, :h] = jnp.dot(low, w, precision=HI, preferred_element_type=f32)
            a_ref[h:, :h] = a_ref[h:, h:] - nt(low, low, precision=HI)

        return 0

    lax.fori_loop(0, 2, half, 0)
    w11, w22, mid = w_ref[:h, h:], w_ref[h:, h:], w_ref[:h, :h]
    w_ref[h:, :h] = -jnp.dot(w22, mid, precision=HI, preferred_element_type=f32)
    w_ref[:h, :h] = w11
    w_ref[:h, h:] = jnp.zeros((h, h), f32)


def step_body(label_total, chunks, my_ref, pb_ref, *refs):
    chunk_refs, (prod_ref, own_ref, out_ref, a_ref, w_ref, sem) = refs[:chunks], refs[chunks:]
    whiten(my_ref, chunk_refs, a_ref, w_ref, label_total)
    blocks, quarter, width = own_ref.shape
    own_ref[...] = nt(prod_ref[...], w_ref[...], precision=HI).astype(bf16).reshape(own_ref.shape)
    spread(own_ref, pb_ref, out_ref, sem)


def step(gram_chunks, prod, my, pb, blocks, quarter, label_total):
    width = prod.shape[1]
    slots = pb.shape[0]
    chunks = len(gram_chunks)
    smem = pl.BlockSpec(memory_space=pltpu.SMEM)
    vmem = pl.BlockSpec(memory_space=pltpu.VMEM)
    return pl.pallas_call(
        functools.partial(step_body, label_total, chunks),
        out_shape=(
            jax.ShapeDtypeStruct((blocks, quarter, width), bf16),
            jax.ShapeDtypeStruct((slots, quarter, width), bf16),
        ),
        in_specs=[smem, smem] + [vmem] * (chunks + 1),
        out_specs=(vmem, pl.BlockSpec(memory_space=pl.ANY)),
        scratch_shapes=[
            pltpu.VMEM((width, width), f32),
            pltpu.VMEM((width, width), f32),
            pltpu.SemaphoreType.DMA((slots,)),
        ],
        name="step",
    )(my, pb, *gram_chunks, prod)


def last_body(label_total, chunks, my_ref, *refs):
    chunk_refs, prod_refs, (out_ref, a_ref, w_ref) = refs[:chunks], refs[chunks:-3], refs[-3:]
    whiten(my_ref, chunk_refs, a_ref, w_ref, label_total)
    narrow, rows = out_ref.shape
    quarter = BS // len(prod_refs)
    v = my_ref[0]
    w = w_ref[pl.ds(pl.multiple_of(v * narrow, narrow), narrow), :]
    for d, prod_ref in enumerate(prod_refs):
        piece = nt(w, prod_ref[...], precision=HI)
        for t in range(rows // BS):
            at = pl.multiple_of(t * BS + (v ^ d) * quarter, quarter)
            out_ref[:, pl.ds(at, quarter)] = piece[:, t * quarter : (t + 1) * quarter]


def last(gram_chunks, prods, my, label_total):
    rows, width = prods[0].shape
    chunks = len(gram_chunks)
    smem = pl.BlockSpec(memory_space=pltpu.SMEM)
    vmem = pl.BlockSpec(memory_space=pltpu.VMEM)
    return pl.pallas_call(
        functools.partial(last_body, label_total, chunks),
        out_shape=jax.ShapeDtypeStruct((width // len(prods), rows * len(prods)), f32),
        in_specs=[smem] + [vmem] * (chunks + len(prods)),
        out_specs=vmem,
        scratch_shapes=[pltpu.VMEM((width, width), f32), pltpu.VMEM((width, width), f32)],
        name="last",
    )(my, *gram_chunks, *prods)


def make(mesh):
    nblk, nvec = mesh.shape["blk"], mesh.shape["vec"]

    def swap(x, owner_bits, vec_bits):
        perm = [
            (o * nvec + v, (o ^ owner_bits) * nvec + (v ^ vec_bits))
            for o in range(nblk)
            for v in range(nvec)
        ]
        return lax.ppermute(x, AXES, perm)

    def exchange(x, axis):
        return lax.all_to_all(x, axis, split_axis=0, concat_axis=0, tiled=True)

    def gram_sum(pieces, prod, gather):
        total = pieces[0]
        for d in range(1, nvec):
            total = total + swap(pieces[d], 0, d)
        prods = [prod]
        if gather:
            total, prod = lax.optimization_barrier((total, prod))
            prods = [prod] + [swap(prod, 0, d) for d in range(1, nvec)]
        for shift in (1, 3):
            got = [swap(total, d << shift, 0) for d in (1, 2, 3)]
            total = (total + got[0]) + (got[1] + got[2])
        total = total + swap(total, 1, 0)
        return [total] + [swap(total, 0, d) for d in range(1, nvec)], prods

    def body(x, basis, pair_block, pair_live):
        rows, feat = x.shape
        narrow = basis.shape[1]
        blocks = rows // BS
        quarter = BS // nvec
        label_total = rows * nblk
        v = lax.axis_index("vec")
        my = v[None].astype(jnp.int32)
        pb, live = pair_block[0], pair_live[0]

        owner = lax.axis_index("blk").astype(jnp.int32)
        cuts = cut_start(basis.T, my, nvec)
        x, cuts = lax.optimization_barrier((x, cuts))
        units = own_quarter(x, my, blocks, quarter)

        def along(x, h, d):
            return x if d == 0 else swap(x, d << SHIFT[LINES[h][0]], 0)

        feats = [along(units[h], h, d) for d in STEPS for h in range(2)]
        vts = [cuts[0]] + [swap(cuts[d], 0, d) for d in range(1, nvec)]
        vown, packs = send_start(vts, pb, my, blocks, quarter)
        vecs = [along(packs[h], h, d) for d in STEPS for h in range(2)]
        sends = relay(feats, vecs, owner[None])
        fars = [
            sends[side_at(h, o)] if o == 0 else swap(sends[side_at(h, o)], offset(LINES[h][1], o), 0)
            for o in FORWARD
            for h in range(2)
        ]

        (x, pb_late, live), fars[2] = lax.optimization_barrier(((x, pb, live), fars[2]))
        entries = entries_of(nblk, blocks)
        sc = pair_table(pb_late, live, owner, blocks, entries)
        unit = normalize(x)

        aff, out = pairs_first(sc, my, unit, fars, vown, entries)
        for it in range(ITERS):
            if it:
                out = pairs_next(sc, my, far, vown, aff, entries)
            out = [o.reshape(blocks * quarter, nvec * narrow) for o in out]
            parts = [out[0]] + [swap(out[d], 0, d) for d in range(1, nvec)]
            prod, pieces = gram(parts, my)
            sums, prods = gram_sum(pieces, prod, it + 1 == ITERS)
            if it + 1 < ITERS:
                vown, vsend = step(sums, prod, my, pb, blocks, quarter, label_total)
                far = exchange(vsend, "blk")
        return last(sums, prods, my, label_total).T

    return body


def solution(mesh):
    in_specs = (P("blk", None), P("blk", "vec"), P("blk", None), P("blk", None))
    return jax.shard_map(
        make(mesh), mesh=mesh, in_specs=in_specs, out_specs=P("blk", "vec"), check_vma=False
    )
```

```python
import functools

import jax
import jax.numpy as jnp
from jax import lax
from jax.experimental import pallas as pl
from jax.experimental.pallas import tpu as pltpu
from jax.sharding import PartitionSpec as P


BS = 512
ITERS = 2
SHARPNESS = 5.0
EPSILON = 1e-06
AXES = ("blk", "vec")
HI = lax.Precision.HIGHEST
f32 = jnp.float32
bf16 = jnp.bfloat16


def normalize(features):
    widened = features.astype(f32)
    inv_norm = lax.rsqrt(jnp.mean(widened * widened, axis=-1, keepdims=True) + EPSILON)
    return (widened * inv_norm).astype(bf16)


LOG2E = 1.4426950408889634


def affinity(scores_sum, width):
    bent = scores_sum * (SHARPNESS * LOG2E / width)
    shift = SHARPNESS * LOG2E
    return (jnp.exp2(bent - shift) - jnp.exp2(-shift - bent)).astype(bf16)


def nt(a, b, **kw):
    return lax.dot_general(a, b, (((1,), (1,)), ((), ())), preferred_element_type=f32, **kw)


def spread(src, pb_ref, out_ref, sem):
    slots = out_ref.shape[0]
    for c in range(slots):
        pltpu.make_async_copy(src.at[pb_ref[c]], out_ref.at[c], sem.at[c]).start()
    for c in range(slots):
        pltpu.make_async_copy(src.at[0], out_ref.at[c], sem.at[c]).wait()


def own_quarter_body(my_ref, x_ref, *refs):
    half_refs, (buf, sem) = refs[:2], refs[2:]
    blocks, quarter, _ = buf.shape
    half = quarter // 2
    for t in range(blocks):
        pltpu.make_async_copy(
            x_ref.at[pl.ds(t * BS + my_ref[0] * quarter, quarter)], buf.at[t], sem.at[t]
        ).start()
    for t in range(blocks):
        pltpu.make_async_copy(x_ref.at[pl.ds(0, quarter)], buf.at[t], sem.at[t]).wait()
        unit = normalize(buf[t])
        for h, out_ref in enumerate(half_refs):
            out_ref[t] = unit[h * half : (h + 1) * half]


def own_quarter(x, my, blocks, quarter):
    feat = x.shape[1]
    vmem = pl.BlockSpec(memory_space=pltpu.VMEM)
    return pl.pallas_call(
        own_quarter_body,
        out_shape=[jax.ShapeDtypeStruct((blocks, quarter // 2, feat), bf16)] * 2,
        in_specs=[pl.BlockSpec(memory_space=pltpu.SMEM), pl.BlockSpec(memory_space=pl.ANY)],
        out_specs=[vmem] * 2,
        scratch_shapes=[pltpu.VMEM((blocks, quarter, feat), bf16), pltpu.SemaphoreType.DMA((blocks,))],
        name="own_quarter",
    )(my, x)


def cut_body(my_ref, basis_ref, *out_refs):
    quarter = BS // len(out_refs)
    for d, out_ref in enumerate(out_refs):
        for t in range(basis_ref.shape[1] // BS):
            at = pl.multiple_of(t * BS + (my_ref[0] ^ d) * quarter, quarter)
            out_ref[:, t * quarter : (t + 1) * quarter] = basis_ref[:, pl.ds(at, quarter)].astype(bf16)


def cut_start(basis_t, my, nvec):
    narrow, rows = basis_t.shape
    vmem = pl.BlockSpec(memory_space=pltpu.VMEM)
    return pl.pallas_call(
        cut_body,
        out_shape=[jax.ShapeDtypeStruct((narrow, rows // nvec), bf16)] * nvec,
        in_specs=[pl.BlockSpec(memory_space=pltpu.SMEM), vmem],
        out_specs=[vmem] * nvec,
        name="cut_start",
    )(my, basis_t)


NOTE = 16


def send_body(my_ref, pb_ref, v0_ref, v1_ref, v2_ref, v3_ref, own_ref, *refs):
    pack_refs, turned = refs[:2], refs[2]
    blocks, quarter, _ = own_ref.shape
    narrow = v0_ref.shape[0]
    for d, vt_ref in enumerate((v0_ref, v1_ref, v2_ref, v3_ref)):
        turned[my_ref[0] ^ d] = vt_ref[...].astype(f32).T.astype(bf16).reshape(blocks, quarter, narrow)
    own_ref[...] = jnp.concatenate([turned[g] for g in range(4)], axis=2)
    half = quarter // 2
    for h, pack in enumerate(pack_refs):
        pack[:, :half] = own_ref[:, h * half : (h + 1) * half]
        pack[:, half:] = jnp.zeros((blocks, NOTE, pack.shape[2]), bf16)
        pack[0, half:, :128] = pb_ref[...].astype(bf16)


def send_start(vts, pb, my, blocks, quarter):
    width = vts[0].shape[0] * len(vts)
    vmem = pl.BlockSpec(memory_space=pltpu.VMEM)
    note = jnp.broadcast_to(jnp.pad(pb.astype(f32), (0, 128 - pb.shape[0])), (NOTE, 128))
    out = pl.pallas_call(
        send_body,
        out_shape=[jax.ShapeDtypeStruct((blocks, quarter, width), bf16)]
        + [jax.ShapeDtypeStruct((blocks, quarter // 2 + NOTE, width), bf16)] * 2,
        in_specs=[pl.BlockSpec(memory_space=pltpu.SMEM), vmem] + [vmem] * len(vts),
        out_specs=[vmem] * 3,
        scratch_shapes=[pltpu.VMEM((len(vts), blocks, quarter, width // len(vts)), bf16)],
        name="send_start",
    )(my, note, *vts)
    return out[0], out[1:]


SHIFT = {"z": 3, "y": 1}
LINES = (("z", "y"), ("y", "z"))
NEAR = 4
SIDE = 8
STEPS = (0, 1, 3, 2)
FORWARD = (0, 4, 5, 2, 3, 6, 7, 1)


def near_at(h, d):
    return 2 * STEPS.index(d) + h


def side_at(h, o):
    return 2 * FORWARD.index(o) + h


def offset(axis, o):
    return (o >> 1) << SHIFT[axis] | (o & 1)


def relay_body(at_ref, *refs):
    feat_refs, vec_refs = refs[: 2 * NEAR], refs[2 * NEAR : 4 * NEAR]
    out_refs, (notes, pbs, sem_note, sem) = refs[4 * NEAR : -4], refs[-4:]
    owner = at_ref[0]
    _, half, feat = feat_refs[0].shape
    width = vec_refs[0].shape[2]
    for i, vec in enumerate(vec_refs):
        notes[i : i + 1] = vec[0, half:, :128].astype(f32)[:1].astype(jnp.int32)
    note_copy = pltpu.make_async_copy(notes, pbs, sem_note)
    note_copy.start()
    note_copy.wait()

    def copies(h, o, d, block):
        out = out_refs[side_at(h, o)]
        i = near_at(h, d)
        return (
            pltpu.make_async_copy(feat_refs[i].at[block], out.at[d, :, pl.ds(0, feat)], sem.at[h, o]),
            pltpu.make_async_copy(
                vec_refs[i].at[block, pl.ds(0, half)], out.at[d, :, pl.ds(feat, width)], sem.at[h, o]
            ),
        )

    places = [(h, o, d) for o in FORWARD for h in range(2) for d in range(NEAR)]
    for h, o, d in places:
        for copy in copies(h, o, d, pbs[near_at(h, d), owner ^ offset(LINES[h][1], o)]):
            copy.start()
    for h in range(2):
        for o in range(SIDE):
            out = out_refs[side_at(h, o)]
            pltpu.make_async_copy(out, out, sem.at[h, o]).wait()


def relay(feats, vecs, owner):
    _, half, feat = feats[0].shape
    hbm = pl.BlockSpec(memory_space=pl.ANY)
    vmem = pl.BlockSpec(memory_space=pltpu.VMEM)
    shape = jax.ShapeDtypeStruct((NEAR, half, feat + vecs[0].shape[2]), bf16)
    return pl.pallas_call(
        relay_body,
        out_shape=[shape] * (2 * SIDE),
        in_specs=[pl.BlockSpec(memory_space=pltpu.SMEM)] + [vmem] * (len(feats) + len(vecs)),
        out_specs=[hbm] * (2 * SIDE),
        scratch_shapes=[
            pltpu.VMEM((2 * NEAR, 128), jnp.int32),
            pltpu.SMEM((2 * NEAR, 128), jnp.int32),
            pltpu.SemaphoreType.DMA(()),
            pltpu.SemaphoreType.DMA((2, SIDE)),
        ],
        name="relay",
    )(owner, *feats, *vecs)


LANES = 4
HALF = 2


def pair_table(pb, live, owner, blocks, entries):
    slots = pb.shape[0]
    on = live > 0
    c = jnp.arange(slots, dtype=jnp.int32)
    same = (pb[:, None] == pb[None, :]) & on[None, :] & (c[None, :] < c[:, None])
    rank = jnp.sum(same.astype(jnp.int32), axis=1)
    t = jnp.arange(blocks, dtype=jnp.int32)
    number = jnp.sum(((pb[None, :] == t[:, None]) & on[None, :]).astype(jnp.int32), axis=1)
    even = (number + 1) // 2 * 2
    plain = jnp.sum(jnp.where(t[None, :] <= t[:, None], even[None, :], 0), axis=1)
    middle = jnp.sum(jnp.where(t < HALF, even, 0))
    pad = -middle % LANES
    end = plain + jnp.where(t >= HALF - 1, pad, 0)
    begin = plain - even + jnp.where(t >= HALF, pad, 0)
    start = jnp.sum(jnp.where(pb[:, None] == t[None, :], begin[None, :], 0), axis=1)
    at = jnp.where(on, start + rank, -1)
    j = jnp.arange(entries, dtype=jnp.int32)
    hit = at[None, :] == j[:, None]
    slot = jnp.sum(jnp.where(hit, c[None, :], 0), axis=1)
    use = jnp.sum(hit.astype(jnp.int32), axis=1)
    target = jnp.minimum(jnp.sum((j[:, None] >= end[None, :]).astype(jnp.int32), axis=1), blocks - 1)
    by_offset = jnp.sum(jnp.where((owner ^ c)[:, None] == c[None, :], at[None, :], 0), axis=1)
    return jnp.concatenate([slot, use, target, end[-1:], by_offset, (middle + pad)[None]])


def entries_of(slots, blocks):
    return -(-(slots - 1 + blocks) // LANES) * LANES


def add_product(out_refs, t, p, first):
    quarter = out_refs[0].shape[1]
    for d, out_ref in enumerate(out_refs):
        piece = p[d * quarter : (d + 1) * quarter]
        if first:
            out_ref[t] = piece
        else:
            out_ref[t] += piece


def entry_range(sc, entries, slots, part):
    middle = sc[3 * entries + 1 + slots]
    return (0, middle) if part == 0 else (middle, sc[3 * entries])


def pairs_first_body(entries, part, sc_ref, my_ref, unit_ref, *refs):
    far_refs, refs = refs[: 2 * SIDE], refs[2 * SIDE :]
    vown_ref, aff_ref, out_refs, (buf, sem) = refs[0], refs[1], refs[2:-2], refs[-2:]
    quarter = vown_ref.shape[1]
    half = quarter // 2
    feat = unit_ref.shape[1]
    slots = NEAR * NEAR * 2
    s = pl.program_id(0)
    v = my_ref[0]
    low, high = entry_range(sc_ref, entries, slots, part)

    def copy(h, side, line, entry):
        return pltpu.make_async_copy(
            far_refs[side_at(h, side)].at[line], buf.at[entry, pl.ds(h * half, half)], sem.at[h, entry]
        )

    def target_rows(t):
        return jnp.concatenate(
            [unit_ref[pl.ds(t * BS + (v ^ d) * quarter, quarter), :] for d in range(len(out_refs))], axis=0
        )

    @pl.when(s == 0)
    def _():
        for o in range(1, slots):
            z, y, core = o >> 3, (o >> 1) & 3, o & 1
            entry = sc_ref[3 * entries + 1 + o]

            @pl.when((entry >= low) & (entry < high))
            def _():
                copy(0, 2 * y + core, z, entry).start()
                copy(1, 2 * z + core, y, entry).start()

        def own(t, _):
            rows = target_rows(t)
            aff = affinity(nt(rows, rows[:quarter]), feat)
            aff_ref[t] = aff
            p = jnp.dot(aff, vown_ref[part * HALF + t], preferred_element_type=f32)
            add_product(out_refs, t, p, True)
            return 0

        lax.fori_loop(0, HALF, own, 0)

    @pl.when((s > 0) & (low + (s - 1) * LANES < high))
    def _():
        first = jnp.clip(low + (s - 1) * LANES, 0, entries - LANES)

        def two(i, _):
            at = first + 2 * i
            used = [sc_ref[entries + at + k] > 0 for k in range(2)]
            for k in range(2):

                @pl.when(used[k])
                def _():
                    copy(0, 0, 0, at + k).wait()
                    copy(1, 0, 0, at + k).wait()

            t = jnp.clip(sc_ref[2 * entries + at] - part * HALF, 0, HALF - 1)
            rhs = jnp.concatenate([buf[at + k, :, :feat] for k in range(2)], axis=0)
            both = affinity(nt(target_rows(t), rhs), feat)
            affs, vecs = [], []
            for k in range(2):
                aff = both[:, k * quarter : (k + 1) * quarter]
                aff = jnp.where(used[k], aff, jnp.zeros_like(aff))
                vec = buf[at + k, :, feat:]
                vecs.append(jnp.where(used[k], vec, jnp.zeros_like(vec)))
                aff_ref[2 * i + k] = aff
                affs.append(aff)
            p = jnp.dot(
                jnp.concatenate(affs, axis=1), jnp.concatenate(vecs, axis=0), preferred_element_type=f32
            )
            add_product(out_refs, t, p, False)
            return 0

        lax.fori_loop(0, LANES // 2, two, 0)


def pairs_next_body(entries, part, sc_ref, my_ref, aff_ref, *refs):
    far_refs, vown_ref, out_refs = refs[:LANES], refs[LANES], refs[LANES + 1 :]
    s = pl.program_id(0)
    low, high = entry_range(sc_ref, entries, NEAR * NEAR * 2, part)

    @pl.when(s == 0)
    def _():
        def own(t, _):
            p = jnp.dot(aff_ref[t], vown_ref[part * HALF + t], preferred_element_type=f32)
            add_product(out_refs, t, p, True)
            return 0

        lax.fori_loop(0, HALF, own, 0)

    @pl.when((s > 0) & (low + (s - 1) * LANES < high))
    def _():
        first = jnp.clip(low + (s - 1) * LANES, 0, entries - LANES)
        for k in range(0, LANES, 2):
            t = jnp.clip(sc_ref[2 * entries + first + k] - part * HALF, 0, HALF - 1)
            aff = jnp.concatenate([aff_ref[k], aff_ref[k + 1]], axis=1)
            vec = jnp.concatenate([far_refs[k][0], far_refs[k + 1][0]], axis=0)
            add_product(out_refs, t, jnp.dot(aff, vec, preferred_element_type=f32), False)


def pair_specs(blocks, quarter, width, entries, part):
    quarters = BS // quarter
    whole = lambda s, sc, my: (0, 0, 0)

    def last_step(sc):
        low, high = entry_range(sc, entries, NEAR * NEAR * 2, part)
        return (high - low + LANES - 1) // LANES

    def slot_map(k):
        def index(s, sc, my):
            low, _ = entry_range(sc, entries, NEAR * NEAR * 2, part)
            first = low + jnp.maximum(jnp.minimum(s, last_step(sc)) - 1, 0) * LANES
            return (sc[jnp.minimum(first, entries - LANES) + k], 0, 0)

        return index

    aff_spec = pl.BlockSpec((LANES, BS, quarter), lambda s, sc, my: (jnp.minimum(s, last_step(sc)), 0, 0))
    own_spec = pl.BlockSpec((blocks, quarter, width), whole)
    out_spec = pl.BlockSpec((HALF, quarter, width), whole)
    out_shapes = [jax.ShapeDtypeStruct((HALF, quarter, width), f32)] * quarters
    far_specs = [pl.BlockSpec((1, quarter, width), slot_map(k)) for k in range(LANES)]
    return aff_spec, own_spec, far_specs, [out_spec] * quarters, out_shapes


def pairs_first(sc, my, unit, fars, vown, entries, part):
    blocks, quarter, width = vown.shape
    far_width = fars[0].shape[2]
    aff_spec, own_spec, _, out_specs, out_shapes = pair_specs(blocks, quarter, width, entries, part)
    out = pl.pallas_call(
        functools.partial(pairs_first_body, entries, part),
        out_shape=[jax.ShapeDtypeStruct((LANES + entries, BS, quarter), bf16)] + out_shapes,
        grid_spec=pltpu.PrefetchScalarGridSpec(
            num_scalar_prefetch=2,
            grid=(1 + entries // LANES,),
            in_specs=[pl.BlockSpec((HALF * BS, unit.shape[1]), lambda s, sc, my: (part, 0))]
            + [pl.BlockSpec(memory_space=pl.ANY)] * len(fars)
            + [own_spec],
            out_specs=[aff_spec] + out_specs,
            scratch_shapes=[
                pltpu.VMEM((entries, quarter, far_width), bf16),
                pltpu.SemaphoreType.DMA((2, entries)),
            ],
        ),
        cost_estimate=pl.CostEstimate(flops=6 * 10**9, bytes_accessed=12 * 2**20, transcendentals=2 * 10**6),
    )(sc, my, unit, *fars, vown)
    return out[0], out[1:]


def pairs_next(sc, my, far, vown, aff, entries, part):
    blocks, quarter, width = vown.shape
    aff_spec, own_spec, far_specs, out_specs, out_shapes = pair_specs(blocks, quarter, width, entries, part)
    return pl.pallas_call(
        functools.partial(pairs_next_body, entries, part),
        out_shape=out_shapes,
        grid_spec=pltpu.PrefetchScalarGridSpec(
            num_scalar_prefetch=2,
            grid=(1 + entries // LANES,),
            in_specs=[aff_spec] + far_specs + [own_spec],
            out_specs=out_specs,
        ),
        cost_estimate=pl.CostEstimate(flops=2 * 10**9, bytes_accessed=12 * 2**20, transcendentals=0),
    )(sc, my, aff, *[far] * LANES, vown)


def gram_body(nvec, my_ref, *refs):
    part_refs, prod_ref, piece_refs, full = refs[:nvec], refs[nvec], refs[nvec + 1 : -1], refs[-1]
    rows = part_refs[0].shape[0]
    for i in range(0, nvec, 4):
        a, b, c, d = (r[...] for r in part_refs[i : i + 4])
        prod_ref[(i // 4) * rows : (i // 4 + 1) * rows] = (a + b) + (c + d)
    p = prod_ref[...]
    full[...] = lax.dot_general(
        p, p, (((0,), (0,)), ((), ())), precision=HI, preferred_element_type=f32
    )
    for d, piece in enumerate(piece_refs):
        rows = piece.shape[0]
        piece[...] = full[pl.ds(pl.multiple_of((my_ref[0] ^ d) * rows, rows), rows), :]


def gram(parts, my, nvec):
    rows, width = parts[0].shape
    vmem = pl.BlockSpec(memory_space=pltpu.VMEM)
    out = pl.pallas_call(
        functools.partial(gram_body, len(parts)),
        out_shape=[jax.ShapeDtypeStruct((rows * len(parts) // nvec, width), f32)]
        + [jax.ShapeDtypeStruct((width // nvec, width), f32)] * nvec,
        in_specs=[pl.BlockSpec(memory_space=pltpu.SMEM)] + [vmem] * len(parts),
        out_specs=[vmem] * (nvec + 1),
        scratch_shapes=[pltpu.VMEM((width, width), f32)],
        name="gram",
    )(my, *parts)
    return out[0], out[1:]


def lane_splat(x, j):
    return jnp.broadcast_to(x[:, j : j + 1], x.shape)


def row_splat(x, s):
    return jnp.broadcast_to(x[s : s + 1, :], x.shape)


def split3(x):
    high = x.astype(bf16)
    rest = x - high.astype(f32)
    mid = rest.astype(bf16)
    return high, mid, (rest - mid.astype(f32)).astype(bf16)


PANEL = 16


def inverse_factor(a):
    n = a.shape[0]
    row_at = lax.broadcasted_iota(jnp.int32, (PANEL, n), 0)
    square = (n, n)
    on_diag = lax.broadcasted_iota(jnp.int32, square, 0) == lax.broadcasted_iota(jnp.int32, square, 1)
    inv = jnp.where(on_diag, 1.0, 0.0).astype(f32)
    done = []
    for j in range(0, n, PANEL):
        top, itop = a[:PANEL, :], inv[:PANEL, :]
        cols = [lane_splat(top, j + c) for c in range(PANEL)]
        for c in range(PANEL):
            scale = lax.rsqrt(row_splat(cols[c], c))
            below = jnp.where(row_at > c, cols[c] * scale, 0.0)
            for k in range(c + 1, PANEL):
                cols[k] = cols[k] - below * (row_splat(cols[k], c) * scale)
            row, irow = row_splat(top, c) * scale, row_splat(itop, c) * scale
            top = jnp.where(row_at == c, row, top - below * row)
            itop = jnp.where(row_at == c, irow, itop - below * irow)
        done.append(itop)
        if j + PANEL < n:
            h, m, l = split3(top)
            ih, im, il = split3(itop)
            left = jnp.concatenate([h, h, m, h, l, m], axis=0)
            right = jnp.concatenate(
                [jnp.concatenate([h, m, h, l, h, m], axis=0), jnp.concatenate([ih, im, ih, il, ih, im], axis=0)],
                axis=1,
            )
            update = lax.dot_general(left, right, (((0,), (0,)), ((), ())), preferred_element_type=f32)
            update = update[j + PANEL :, :]
            a = a[PANEL:, :] - update[:, :n]
            inv = inv[PANEL:, :] - update[:, n:]
    return jnp.concatenate(done, axis=0)


def whiten(my_ref, chunk_refs, a_ref, w_ref, label_total):
    n = a_ref.shape[0]
    h = n // 2
    rows = chunk_refs[0].shape[0]
    for d, chunk in enumerate(chunk_refs):
        at = pl.multiple_of((my_ref[0] ^ d) * rows, rows)
        a_ref[pl.ds(at, rows), :] = chunk[...] * (1.0 / label_total)

    def half(i, _):
        at = pl.multiple_of(i * h, h)
        w = inverse_factor(a_ref[pl.ds(at, h), :h])
        w_ref[pl.ds(at, h), h:] = w

        @pl.when(i == 0)
        def _():
            low = nt(a_ref[h:, :h], w, precision=HI)
            w_ref[:h, :h] = jnp.dot(low, w, precision=HI, preferred_element_type=f32)
            a_ref[h:, :h] = a_ref[h:, h:] - nt(low, low, precision=HI)

        return 0

    lax.fori_loop(0, 2, half, 0)
    w11, w22, mid = w_ref[:h, h:], w_ref[h:, h:], w_ref[:h, :h]
    w_ref[h:, :h] = -jnp.dot(w22, mid, precision=HI, preferred_element_type=f32)
    w_ref[:h, :h] = w11
    w_ref[:h, h:] = jnp.zeros((h, h), f32)


def step_body(label_total, chunks, my_ref, pb_ref, *refs):
    chunk_refs, (prod_ref, own_ref, out_ref, a_ref, w_ref, sem) = refs[:chunks], refs[chunks:]
    whiten(my_ref, chunk_refs, a_ref, w_ref, label_total)
    own_ref[...] = nt(prod_ref[...], w_ref[...], precision=HI).astype(bf16).reshape(own_ref.shape)
    spread(own_ref, pb_ref, out_ref, sem)


def step(gram_chunks, prod, my, pb, blocks, quarter, label_total):
    width = prod.shape[1]
    slots = pb.shape[0]
    chunks = len(gram_chunks)
    smem = pl.BlockSpec(memory_space=pltpu.SMEM)
    vmem = pl.BlockSpec(memory_space=pltpu.VMEM)
    return pl.pallas_call(
        functools.partial(step_body, label_total, chunks),
        out_shape=(
            jax.ShapeDtypeStruct((blocks, quarter, width), bf16),
            jax.ShapeDtypeStruct((slots, quarter, width), bf16),
        ),
        in_specs=[smem, smem] + [vmem] * (chunks + 1),
        out_specs=(vmem, pl.BlockSpec(memory_space=pl.ANY)),
        scratch_shapes=[
            pltpu.VMEM((width, width), f32),
            pltpu.VMEM((width, width), f32),
            pltpu.SemaphoreType.DMA((slots,)),
        ],
        name="step",
    )(my, pb, *gram_chunks, prod)


def last_body(label_total, chunks, my_ref, *refs):
    chunk_refs, prod_refs, (out_ref, a_ref, w_ref) = refs[:chunks], refs[chunks:-3], refs[-3:]
    whiten(my_ref, chunk_refs, a_ref, w_ref, label_total)
    narrow, rows = out_ref.shape
    quarter = BS // len(prod_refs)
    v = my_ref[0]
    w = w_ref[pl.ds(pl.multiple_of(v * narrow, narrow), narrow), :]
    for d, prod_ref in enumerate(prod_refs):
        piece = nt(w, prod_ref[...], precision=HI)
        for t in range(rows // BS):
            at = pl.multiple_of(t * BS + (v ^ d) * quarter, quarter)
            out_ref[:, pl.ds(at, quarter)] = piece[:, t * quarter : (t + 1) * quarter]


def last(gram_chunks, prods, my, label_total):
    rows, width = prods[0].shape
    chunks = len(gram_chunks)
    smem = pl.BlockSpec(memory_space=pltpu.SMEM)
    vmem = pl.BlockSpec(memory_space=pltpu.VMEM)
    return pl.pallas_call(
        functools.partial(last_body, label_total, chunks),
        out_shape=jax.ShapeDtypeStruct((width // len(prods), rows * len(prods)), f32),
        in_specs=[smem] + [vmem] * (chunks + len(prods)),
        out_specs=vmem,
        scratch_shapes=[pltpu.VMEM((width, width), f32), pltpu.VMEM((width, width), f32)],
        name="last",
    )(my, *gram_chunks, *prods)


def make(mesh):
    nblk, nvec = mesh.shape["blk"], mesh.shape["vec"]

    def swap(x, owner_bits, vec_bits):
        perm = [
            (o * nvec + v, (o ^ owner_bits) * nvec + (v ^ vec_bits))
            for o in range(nblk)
            for v in range(nvec)
        ]
        return lax.ppermute(x, AXES, perm)

    def exchange(x, axis):
        return lax.all_to_all(x, axis, split_axis=0, concat_axis=0, tiled=True)

    def gram_sum(pieces, prod, gather):
        total = pieces[0]
        for d in range(1, nvec):
            total = total + swap(pieces[d], 0, d)
        prods = [prod]
        if gather:
            total, prod = lax.optimization_barrier((total, prod))
            prods = [prod] + [swap(prod, 0, d) for d in range(1, nvec)]
        for shift in (1, 3):
            got = [swap(total, d << shift, 0) for d in (1, 2, 3)]
            total = (total + got[0]) + (got[1] + got[2])
        total = total + swap(total, 1, 0)
        return [total] + [swap(total, 0, d) for d in range(1, nvec)], prods

    def body(x, basis, pair_block, pair_live):
        rows, _ = x.shape
        narrow = basis.shape[1]
        blocks = rows // BS
        quarter = BS // nvec
        label_total = rows * nblk
        v = lax.axis_index("vec")
        my = v[None].astype(jnp.int32)
        pb, live = pair_block[0], pair_live[0]

        owner = lax.axis_index("blk").astype(jnp.int32)
        cuts = cut_start(basis.T, my, nvec)
        x, cuts = lax.optimization_barrier((x, cuts))
        vts = [cuts[0]] + [swap(cuts[d], 0, d) for d in range(1, nvec)]
        units = own_quarter(x, my, blocks, quarter)
        units, vts = lax.optimization_barrier((units, vts))

        def along(x, h, d):
            return x if d == 0 else swap(x, d << SHIFT[LINES[h][0]], 0)

        feats = [along(units[h], h, d) for d in STEPS for h in range(2)]
        vown, packs = send_start(vts, pb, my, blocks, quarter)
        vecs = [along(packs[h], h, d) for d in STEPS for h in range(2)]
        sends = relay(feats, vecs, owner[None])
        fars = [
            sends[side_at(h, o)] if o == 0 else swap(sends[side_at(h, o)], offset(LINES[h][1], o), 0)
            for o in FORWARD
            for h in range(2)
        ]

        (x, pb_late, live), fars[2] = lax.optimization_barrier(((x, pb, live), fars[2]))
        entries = entries_of(nblk, blocks)
        sc = pair_table(pb_late, live, owner, blocks, entries)
        unit = normalize(x)

        affs = [None] * (blocks // HALF)
        for it in range(ITERS):
            parts = []
            for part in range(len(affs)):
                if it:
                    out = pairs_next(sc, my, far, vown, affs[part], entries, part)
                else:
                    affs[part], out = pairs_first(sc, my, unit, fars, vown, entries, part)
                sc, out = lax.optimization_barrier((sc, list(out)))
                out = [o.reshape(HALF * quarter, nvec * narrow) for o in out]
                parts.append(out[0])
                for d in range(1, nvec):
                    parts.append(swap(out[d], 0, d))
            prod, pieces = gram(parts, my, nvec)
            sums, prods = gram_sum(pieces, prod, it + 1 == ITERS)
            if it + 1 < ITERS:
                vown, vsend = step(sums, prod, my, pb, blocks, quarter, label_total)
                far = exchange(vsend, "blk")
        return last(sums, prods, my, label_total).T

    return body


def solution(mesh):
    in_specs = (P("blk", None), P("blk", "vec"), P("blk", None), P("blk", None))
    return jax.shard_map(
        make(mesh), mesh=mesh, in_specs=in_specs, out_specs=P("blk", "vec"), check_vma=False
    )
```

```python
import functools

import jax
import jax.numpy as jnp
from jax import lax
from jax.experimental import pallas as pl
from jax.experimental.pallas import tpu as pltpu
from jax.sharding import PartitionSpec as P


BS = 512
ITERS = 2
SHARPNESS = 5.0
EPSILON = 1e-06
AXES = ("blk", "vec")
HI = lax.Precision.HIGHEST
f32 = jnp.float32
bf16 = jnp.bfloat16


def normalize(features):
    widened = features.astype(f32)
    inv_norm = lax.rsqrt(jnp.mean(widened * widened, axis=-1, keepdims=True) + EPSILON)
    return (widened * inv_norm).astype(bf16)


LOG2E = 1.4426950408889634


def affinity(scores_sum, width):
    bent = scores_sum * (SHARPNESS * LOG2E / width)
    shift = SHARPNESS * LOG2E
    return (jnp.exp2(bent - shift) - jnp.exp2(-shift - bent)).astype(bf16)


def nt(a, b, **kw):
    return lax.dot_general(a, b, (((1,), (1,)), ((), ())), preferred_element_type=f32, **kw)


def spread(src, pb_ref, out_ref, sem):
    slots = out_ref.shape[0]
    for c in range(slots):
        pltpu.make_async_copy(src.at[pb_ref[c]], out_ref.at[c], sem.at[c]).start()
    for c in range(slots):
        pltpu.make_async_copy(src.at[0], out_ref.at[c], sem.at[c]).wait()


def own_quarter_body(my_ref, x_ref, *refs):
    half_refs, (buf, sem) = refs[:2], refs[2:]
    blocks, quarter, _ = buf.shape
    half = quarter // 2
    for t in range(blocks):
        pltpu.make_async_copy(
            x_ref.at[pl.ds(t * BS + my_ref[0] * quarter, quarter)], buf.at[t], sem.at[t]
        ).start()
    for t in range(blocks):
        pltpu.make_async_copy(x_ref.at[pl.ds(0, quarter)], buf.at[t], sem.at[t]).wait()
        unit = normalize(buf[t])
        for h, out_ref in enumerate(half_refs):
            out_ref[t] = unit[h * half : (h + 1) * half]


def own_quarter(x, my, blocks, quarter):
    feat = x.shape[1]
    vmem = pl.BlockSpec(memory_space=pltpu.VMEM)
    return pl.pallas_call(
        own_quarter_body,
        out_shape=[jax.ShapeDtypeStruct((blocks, quarter // 2, feat), bf16)] * 2,
        in_specs=[pl.BlockSpec(memory_space=pltpu.SMEM), pl.BlockSpec(memory_space=pl.ANY)],
        out_specs=[vmem] * 2,
        scratch_shapes=[pltpu.VMEM((blocks, quarter, feat), bf16), pltpu.SemaphoreType.DMA((blocks,))],
        name="own_quarter",
    )(my, x)


def cut_body(my_ref, basis_ref, *out_refs):
    quarter = BS // len(out_refs)
    for d, out_ref in enumerate(out_refs):
        for t in range(basis_ref.shape[1] // BS):
            at = pl.multiple_of(t * BS + (my_ref[0] ^ d) * quarter, quarter)
            out_ref[:, t * quarter : (t + 1) * quarter] = basis_ref[:, pl.ds(at, quarter)].astype(bf16)


def cut_start(basis_t, my, nvec):
    narrow, rows = basis_t.shape
    vmem = pl.BlockSpec(memory_space=pltpu.VMEM)
    return pl.pallas_call(
        cut_body,
        out_shape=[jax.ShapeDtypeStruct((narrow, rows // nvec), bf16)] * nvec,
        in_specs=[pl.BlockSpec(memory_space=pltpu.SMEM), vmem],
        out_specs=[vmem] * nvec,
        name="cut_start",
    )(my, basis_t)


NOTE = 16


def send_body(my_ref, pb_ref, v0_ref, v1_ref, v2_ref, v3_ref, own_ref, *refs):
    pack_refs, turned = refs[:2], refs[2]
    blocks, quarter, _ = own_ref.shape
    narrow = v0_ref.shape[0]
    for d, vt_ref in enumerate((v0_ref, v1_ref, v2_ref, v3_ref)):
        turned[my_ref[0] ^ d] = vt_ref[...].astype(f32).T.astype(bf16).reshape(blocks, quarter, narrow)
    own_ref[...] = jnp.concatenate([turned[g] for g in range(4)], axis=2)
    half = quarter // 2
    for h, pack in enumerate(pack_refs):
        pack[:, :half] = own_ref[:, h * half : (h + 1) * half]
        pack[:, half:] = jnp.zeros((blocks, NOTE, pack.shape[2]), bf16)
        pack[0, half:, :128] = pb_ref[...].astype(bf16)


def send_start(vts, pb, my, blocks, quarter):
    width = vts[0].shape[0] * len(vts)
    vmem = pl.BlockSpec(memory_space=pltpu.VMEM)
    note = jnp.broadcast_to(jnp.pad(pb.astype(f32), (0, 128 - pb.shape[0])), (NOTE, 128))
    out = pl.pallas_call(
        send_body,
        out_shape=[jax.ShapeDtypeStruct((blocks, quarter, width), bf16)]
        + [jax.ShapeDtypeStruct((blocks, quarter // 2 + NOTE, width), bf16)] * 2,
        in_specs=[pl.BlockSpec(memory_space=pltpu.SMEM), vmem] + [vmem] * len(vts),
        out_specs=[vmem] * 3,
        scratch_shapes=[pltpu.VMEM((len(vts), blocks, quarter, width // len(vts)), bf16)],
        name="send_start",
    )(my, note, *vts)
    return out[0], out[1:]


SHIFT = {"z": 3, "y": 1}
LINES = (("z", "y"), ("y", "z"))
NEAR = 4
SIDE = 8
STEPS = (0, 1, 3, 2)
FORWARD = (0, 4, 5, 2, 3, 6, 7, 1)


def near_at(h, d):
    return 2 * STEPS.index(d) + h


def side_at(h, o):
    return 2 * FORWARD.index(o) + h


def offset(axis, o):
    return (o >> 1) << SHIFT[axis] | (o & 1)


def relay_body(at_ref, *refs):
    feat_refs, vec_refs = refs[: 2 * NEAR], refs[2 * NEAR : 4 * NEAR]
    out_refs, (notes, pbs, sem_note, sem) = refs[4 * NEAR : -4], refs[-4:]
    owner = at_ref[0]
    _, half, feat = feat_refs[0].shape
    width = vec_refs[0].shape[2]
    for i, vec in enumerate(vec_refs):
        notes[i : i + 1] = vec[0, half:, :128].astype(f32)[:1].astype(jnp.int32)
    note_copy = pltpu.make_async_copy(notes, pbs, sem_note)
    note_copy.start()
    note_copy.wait()

    def copies(h, o, d, block):
        out = out_refs[side_at(h, o)]
        i = near_at(h, d)
        return (
            pltpu.make_async_copy(feat_refs[i].at[block], out.at[d, :, pl.ds(0, feat)], sem.at[h, o]),
            pltpu.make_async_copy(
                vec_refs[i].at[block, pl.ds(0, half)], out.at[d, :, pl.ds(feat, width)], sem.at[h, o]
            ),
        )

    places = [(h, o, d) for o in FORWARD for h in range(2) for d in range(NEAR)]
    for h, o, d in places:
        for copy in copies(h, o, d, pbs[near_at(h, d), owner ^ offset(LINES[h][1], o)]):
            copy.start()
    for h in range(2):
        for o in range(SIDE):
            out = out_refs[side_at(h, o)]
            pltpu.make_async_copy(out, out, sem.at[h, o]).wait()


def relay(feats, vecs, owner):
    _, half, feat = feats[0].shape
    hbm = pl.BlockSpec(memory_space=pl.ANY)
    vmem = pl.BlockSpec(memory_space=pltpu.VMEM)
    shape = jax.ShapeDtypeStruct((NEAR, half, feat + vecs[0].shape[2]), bf16)
    return pl.pallas_call(
        relay_body,
        out_shape=[shape] * (2 * SIDE),
        in_specs=[pl.BlockSpec(memory_space=pltpu.SMEM)] + [vmem] * (len(feats) + len(vecs)),
        out_specs=[hbm] * (2 * SIDE),
        scratch_shapes=[
            pltpu.VMEM((2 * NEAR, 128), jnp.int32),
            pltpu.SMEM((2 * NEAR, 128), jnp.int32),
            pltpu.SemaphoreType.DMA(()),
            pltpu.SemaphoreType.DMA((2, SIDE)),
        ],
        name="relay",
    )(owner, *feats, *vecs)


LANES = 4
HALF = 2


def pair_table(pb, live, owner, blocks, entries):
    slots = pb.shape[0]
    on = live > 0
    c = jnp.arange(slots, dtype=jnp.int32)
    same = (pb[:, None] == pb[None, :]) & on[None, :] & (c[None, :] < c[:, None])
    rank = jnp.sum(same.astype(jnp.int32), axis=1)
    t = jnp.arange(blocks, dtype=jnp.int32)
    number = jnp.sum(((pb[None, :] == t[:, None]) & on[None, :]).astype(jnp.int32), axis=1)
    even = (number + 1) // 2 * 2
    plain = jnp.sum(jnp.where(t[None, :] <= t[:, None], even[None, :], 0), axis=1)
    middle = jnp.sum(jnp.where(t < HALF, even, 0))
    pad = -middle % LANES
    end = plain + jnp.where(t >= HALF - 1, pad, 0)
    begin = plain - even + jnp.where(t >= HALF, pad, 0)
    start = jnp.sum(jnp.where(pb[:, None] == t[None, :], begin[None, :], 0), axis=1)
    at = jnp.where(on, start + rank, -1)
    j = jnp.arange(entries, dtype=jnp.int32)
    hit = at[None, :] == j[:, None]
    slot = jnp.sum(jnp.where(hit, c[None, :], 0), axis=1)
    use = jnp.sum(hit.astype(jnp.int32), axis=1)
    target = jnp.minimum(jnp.sum((j[:, None] >= end[None, :]).astype(jnp.int32), axis=1), blocks - 1)
    by_offset = jnp.sum(jnp.where((owner ^ c)[:, None] == c[None, :], at[None, :], 0), axis=1)
    return jnp.concatenate([slot, use, target, end[-1:], by_offset, (middle + pad)[None]])


def entries_of(slots, blocks):
    return -(-(slots - 1 + blocks) // LANES) * LANES


def add_product(out_refs, t, p, first):
    quarter = out_refs[0].shape[1]
    for d, out_ref in enumerate(out_refs):
        piece = p[d * quarter : (d + 1) * quarter]
        if first:
            out_ref[t] = piece
        else:
            out_ref[t] += piece


def entry_range(sc, entries, slots, part):
    middle = sc[3 * entries + 1 + slots]
    return (0, middle) if part == 0 else (middle, sc[3 * entries])


def pairs_first_body(entries, part, sc_ref, my_ref, unit_ref, *refs):
    far_refs, refs = refs[: 2 * SIDE], refs[2 * SIDE :]
    vown_ref, aff_ref, out_refs, (buf, sem) = refs[0], refs[1], refs[2:-2], refs[-2:]
    quarter = vown_ref.shape[1]
    half = quarter // 2
    feat = unit_ref.shape[1]
    slots = NEAR * NEAR * 2
    s = pl.program_id(0)
    v = my_ref[0]
    low, high = entry_range(sc_ref, entries, slots, part)

    def copy(h, side, line, entry):
        return pltpu.make_async_copy(
            far_refs[side_at(h, side)].at[line], buf.at[entry, pl.ds(h * half, half)], sem.at[h, entry]
        )

    def target_rows(t):
        return jnp.concatenate(
            [unit_ref[pl.ds(t * BS + (v ^ d) * quarter, quarter), :] for d in range(len(out_refs))], axis=0
        )

    @pl.when(s == 0)
    def _():
        for o in range(1, slots):
            z, y, core = o >> 3, (o >> 1) & 3, o & 1
            entry = sc_ref[3 * entries + 1 + o]

            @pl.when((entry >= low) & (entry < high))
            def _():
                copy(0, 2 * y + core, z, entry).start()
                copy(1, 2 * z + core, y, entry).start()

        def own(t, _):
            rows = target_rows(t)
            aff = affinity(nt(rows, rows[:quarter]), feat)
            aff_ref[t] = aff
            p = jnp.dot(aff, vown_ref[part * HALF + t], preferred_element_type=f32)
            add_product(out_refs, t, p, True)
            return 0

        lax.fori_loop(0, HALF, own, 0)

    @pl.when((s > 0) & (low + (s - 1) * LANES < high))
    def _():
        first = jnp.clip(low + (s - 1) * LANES, 0, entries - LANES)

        def two(i, _):
            at = first + 2 * i
            used = [sc_ref[entries + at + k] > 0 for k in range(2)]
            for k in range(2):

                @pl.when(used[k])
                def _():
                    copy(0, 0, 0, at + k).wait()
                    copy(1, 0, 0, at + k).wait()

            t = jnp.clip(sc_ref[2 * entries + at] - part * HALF, 0, HALF - 1)
            rhs = jnp.concatenate([buf[at + k, :, :feat] for k in range(2)], axis=0)
            both = affinity(nt(target_rows(t), rhs), feat)
            affs, vecs = [], []
            for k in range(2):
                aff = both[:, k * quarter : (k + 1) * quarter]
                aff = jnp.where(used[k], aff, jnp.zeros_like(aff))
                vec = buf[at + k, :, feat:]
                vecs.append(jnp.where(used[k], vec, jnp.zeros_like(vec)))
                aff_ref[2 * i + k] = aff
                affs.append(aff)
            p = jnp.dot(
                jnp.concatenate(affs, axis=1), jnp.concatenate(vecs, axis=0), preferred_element_type=f32
            )
            add_product(out_refs, t, p, False)
            return 0

        lax.fori_loop(0, LANES // 2, two, 0)


def pairs_next_body(entries, part, sc_ref, my_ref, aff_ref, *refs):
    far_refs, vown_ref, out_refs = refs[:LANES], refs[LANES], refs[LANES + 1 :]
    s = pl.program_id(0)
    low, high = entry_range(sc_ref, entries, NEAR * NEAR * 2, part)

    @pl.when(s == 0)
    def _():
        def own(t, _):
            p = jnp.dot(aff_ref[t], vown_ref[part * HALF + t], preferred_element_type=f32)
            add_product(out_refs, t, p, True)
            return 0

        lax.fori_loop(0, HALF, own, 0)

    @pl.when((s > 0) & (low + (s - 1) * LANES < high))
    def _():
        first = jnp.clip(low + (s - 1) * LANES, 0, entries - LANES)
        for k in range(0, LANES, 2):
            t = jnp.clip(sc_ref[2 * entries + first + k] - part * HALF, 0, HALF - 1)
            aff = jnp.concatenate([aff_ref[k], aff_ref[k + 1]], axis=1)
            vec = jnp.concatenate([far_refs[k][0], far_refs[k + 1][0]], axis=0)
            add_product(out_refs, t, jnp.dot(aff, vec, preferred_element_type=f32), False)


def pair_specs(blocks, quarter, width, entries, part):
    quarters = BS // quarter
    whole = lambda s, sc, my: (0, 0, 0)

    def last_step(sc):
        low, high = entry_range(sc, entries, NEAR * NEAR * 2, part)
        return (high - low + LANES - 1) // LANES

    def slot_map(k):
        def index(s, sc, my):
            low, _ = entry_range(sc, entries, NEAR * NEAR * 2, part)
            first = low + jnp.maximum(jnp.minimum(s, last_step(sc)) - 1, 0) * LANES
            return (sc[jnp.minimum(first, entries - LANES) + k], 0, 0)

        return index

    aff_spec = pl.BlockSpec((LANES, BS, quarter), lambda s, sc, my: (jnp.minimum(s, last_step(sc)), 0, 0))
    own_spec = pl.BlockSpec((blocks, quarter, width), whole)
    out_spec = pl.BlockSpec((HALF, quarter, width), whole)
    out_shapes = [jax.ShapeDtypeStruct((HALF, quarter, width), f32)] * quarters
    far_specs = [pl.BlockSpec((1, quarter, width), slot_map(k)) for k in range(LANES)]
    return aff_spec, own_spec, far_specs, [out_spec] * quarters, out_shapes


def pairs_first(sc, my, unit, fars, vown, entries, part):
    blocks, quarter, width = vown.shape
    far_width = fars[0].shape[2]
    aff_spec, own_spec, _, out_specs, out_shapes = pair_specs(blocks, quarter, width, entries, part)
    out = pl.pallas_call(
        functools.partial(pairs_first_body, entries, part),
        out_shape=[jax.ShapeDtypeStruct((LANES + entries, BS, quarter), bf16)] + out_shapes,
        grid_spec=pltpu.PrefetchScalarGridSpec(
            num_scalar_prefetch=2,
            grid=(1 + entries // LANES,),
            in_specs=[pl.BlockSpec((HALF * BS, unit.shape[1]), lambda s, sc, my: (part, 0))]
            + [pl.BlockSpec(memory_space=pl.ANY)] * len(fars)
            + [own_spec],
            out_specs=[aff_spec] + out_specs,
            scratch_shapes=[
                pltpu.VMEM((entries, quarter, far_width), bf16),
                pltpu.SemaphoreType.DMA((2, entries)),
            ],
        ),
        cost_estimate=pl.CostEstimate(flops=6 * 10**9, bytes_accessed=12 * 2**20, transcendentals=2 * 10**6),
    )(sc, my, unit, *fars, vown)
    return out[0], out[1:]


def pairs_next(sc, my, far, vown, aff, entries, part):
    blocks, quarter, width = vown.shape
    aff_spec, own_spec, far_specs, out_specs, out_shapes = pair_specs(blocks, quarter, width, entries, part)
    return pl.pallas_call(
        functools.partial(pairs_next_body, entries, part),
        out_shape=out_shapes,
        grid_spec=pltpu.PrefetchScalarGridSpec(
            num_scalar_prefetch=2,
            grid=(1 + entries // LANES,),
            in_specs=[aff_spec] + far_specs + [own_spec],
            out_specs=out_specs,
        ),
        cost_estimate=pl.CostEstimate(flops=2 * 10**9, bytes_accessed=12 * 2**20, transcendentals=0),
    )(sc, my, aff, *[far] * LANES, vown)


def gram_body(nvec, my_ref, *refs):
    part_refs, prod_ref, piece_refs, full = refs[:nvec], refs[nvec], refs[nvec + 1 : -1], refs[-1]
    rows = part_refs[0].shape[0]
    for i in range(0, nvec, 4):
        a, b, c, d = (r[...] for r in part_refs[i : i + 4])
        prod_ref[(i // 4) * rows : (i // 4 + 1) * rows] = (a + b) + (c + d)
    p = prod_ref[...]
    full[...] = lax.dot_general(
        p, p, (((0,), (0,)), ((), ())), precision=HI, preferred_element_type=f32
    )
    for d, piece in enumerate(piece_refs):
        rows = piece.shape[0]
        piece[...] = full[pl.ds(pl.multiple_of((my_ref[0] ^ d) * rows, rows), rows), :]


def gram(parts, my, nvec):
    rows, width = parts[0].shape
    vmem = pl.BlockSpec(memory_space=pltpu.VMEM)
    out = pl.pallas_call(
        functools.partial(gram_body, len(parts)),
        out_shape=[jax.ShapeDtypeStruct((rows * len(parts) // nvec, width), f32)]
        + [jax.ShapeDtypeStruct((width // nvec, width), f32)] * nvec,
        in_specs=[pl.BlockSpec(memory_space=pltpu.SMEM)] + [vmem] * len(parts),
        out_specs=[vmem] * (nvec + 1),
        scratch_shapes=[pltpu.VMEM((width, width), f32)],
        name="gram",
    )(my, *parts)
    return out[0], out[1:]


def lane_splat(x, j):
    return jnp.broadcast_to(x[:, j : j + 1], x.shape)


def row_splat(x, s):
    return jnp.broadcast_to(x[s : s + 1, :], x.shape)


def split3(x):
    high = x.astype(bf16)
    rest = x - high.astype(f32)
    mid = rest.astype(bf16)
    return high, mid, (rest - mid.astype(f32)).astype(bf16)


PANEL = 16


def inverse_factor(a):
    n = a.shape[0]
    row_at = lax.broadcasted_iota(jnp.int32, (PANEL, n), 0)
    square = (n, n)
    on_diag = lax.broadcasted_iota(jnp.int32, square, 0) == lax.broadcasted_iota(jnp.int32, square, 1)
    inv = jnp.where(on_diag, 1.0, 0.0).astype(f32)
    done = []
    for j in range(0, n, PANEL):
        top, itop = a[:PANEL, :], inv[:PANEL, :]
        cols = [lane_splat(top, j + c) for c in range(PANEL)]
        for c in range(PANEL):
            scale = lax.rsqrt(row_splat(cols[c], c))
            below = jnp.where(row_at > c, cols[c] * scale, 0.0)
            for k in range(c + 1, PANEL):
                cols[k] = cols[k] - below * (row_splat(cols[k], c) * scale)
            row, irow = row_splat(top, c) * scale, row_splat(itop, c) * scale
            top = jnp.where(row_at == c, row, top - below * row)
            itop = jnp.where(row_at == c, irow, itop - below * irow)
        done.append(itop)
        if j + PANEL < n:
            h, m, l = split3(top)
            ih, im, il = split3(itop)
            left = jnp.concatenate([h, h, m, h, l, m], axis=0)
            right = jnp.concatenate(
                [jnp.concatenate([h, m, h, l, h, m], axis=0), jnp.concatenate([ih, im, ih, il, ih, im], axis=0)],
                axis=1,
            )
            update = lax.dot_general(left, right, (((0,), (0,)), ((), ())), preferred_element_type=f32)
            update = update[j + PANEL :, :]
            a = a[PANEL:, :] - update[:, :n]
            inv = inv[PANEL:, :] - update[:, n:]
    return jnp.concatenate(done, axis=0)


def whiten(my_ref, chunk_refs, a_ref, w_ref, label_total):
    n = a_ref.shape[0]
    h = n // 2
    rows = chunk_refs[0].shape[0]
    for d, chunk in enumerate(chunk_refs):
        at = pl.multiple_of((my_ref[0] ^ d) * rows, rows)
        a_ref[pl.ds(at, rows), :] = chunk[...] * (1.0 / label_total)

    def half(i, _):
        at = pl.multiple_of(i * h, h)
        w = inverse_factor(a_ref[pl.ds(at, h), :h])
        w_ref[pl.ds(at, h), h:] = w

        @pl.when(i == 0)
        def _():
            low = nt(a_ref[h:, :h], w, precision=HI)
            w_ref[:h, :h] = jnp.dot(low, w, precision=HI, preferred_element_type=f32)
            a_ref[h:, :h] = a_ref[h:, h:] - nt(low, low, precision=HI)

        return 0

    lax.fori_loop(0, 2, half, 0)
    w11, w22, mid = w_ref[:h, h:], w_ref[h:, h:], w_ref[:h, :h]
    w_ref[h:, :h] = -jnp.dot(w22, mid, precision=HI, preferred_element_type=f32)
    w_ref[:h, :h] = w11
    w_ref[:h, h:] = jnp.zeros((h, h), f32)


def step_body(label_total, chunks, my_ref, pb_ref, *refs):
    chunk_refs, (prod_ref, own_ref, out_ref, a_ref, w_ref, sem) = refs[:chunks], refs[chunks:]
    whiten(my_ref, chunk_refs, a_ref, w_ref, label_total)
    own_ref[...] = nt(prod_ref[...], w_ref[...], precision=HI).astype(bf16).reshape(own_ref.shape)
    spread(own_ref, pb_ref, out_ref, sem)


def step(gram_chunks, prod, my, pb, blocks, quarter, label_total):
    width = prod.shape[1]
    slots = pb.shape[0]
    chunks = len(gram_chunks)
    smem = pl.BlockSpec(memory_space=pltpu.SMEM)
    vmem = pl.BlockSpec(memory_space=pltpu.VMEM)
    return pl.pallas_call(
        functools.partial(step_body, label_total, chunks),
        out_shape=(
            jax.ShapeDtypeStruct((blocks, quarter, width), bf16),
            jax.ShapeDtypeStruct((slots, quarter, width), bf16),
        ),
        in_specs=[smem, smem] + [vmem] * (chunks + 1),
        out_specs=(vmem, pl.BlockSpec(memory_space=pl.ANY)),
        scratch_shapes=[
            pltpu.VMEM((width, width), f32),
            pltpu.VMEM((width, width), f32),
            pltpu.SemaphoreType.DMA((slots,)),
        ],
        name="step",
    )(my, pb, *gram_chunks, prod)


def last_body(label_total, chunks, my_ref, *refs):
    chunk_refs, prod_refs, (out_ref, a_ref, w_ref) = refs[:chunks], refs[chunks:-3], refs[-3:]
    whiten(my_ref, chunk_refs, a_ref, w_ref, label_total)
    narrow, rows = out_ref.shape
    quarter = BS // len(prod_refs)
    v = my_ref[0]
    w = w_ref[pl.ds(pl.multiple_of(v * narrow, narrow), narrow), :]
    for d, prod_ref in enumerate(prod_refs):
        piece = nt(w, prod_ref[...], precision=HI)
        for t in range(rows // BS):
            at = pl.multiple_of(t * BS + (v ^ d) * quarter, quarter)
            out_ref[:, pl.ds(at, quarter)] = piece[:, t * quarter : (t + 1) * quarter]


def last(gram_chunks, prods, my, label_total):
    rows, width = prods[0].shape
    chunks = len(gram_chunks)
    smem = pl.BlockSpec(memory_space=pltpu.SMEM)
    vmem = pl.BlockSpec(memory_space=pltpu.VMEM)
    return pl.pallas_call(
        functools.partial(last_body, label_total, chunks),
        out_shape=jax.ShapeDtypeStruct((width // len(prods), rows * len(prods)), f32),
        in_specs=[smem] + [vmem] * (chunks + len(prods)),
        out_specs=vmem,
        scratch_shapes=[pltpu.VMEM((width, width), f32), pltpu.VMEM((width, width), f32)],
        name="last",
    )(my, *gram_chunks, *prods)


def make(mesh):
    nblk, nvec = mesh.shape["blk"], mesh.shape["vec"]

    def swap(x, owner_bits, vec_bits):
        perm = [
            (o * nvec + v, (o ^ owner_bits) * nvec + (v ^ vec_bits))
            for o in range(nblk)
            for v in range(nvec)
        ]
        return lax.ppermute(x, AXES, perm)

    def exchange(x, axis):
        return lax.all_to_all(x, axis, split_axis=0, concat_axis=0, tiled=True)

    def gram_sum(pieces, prod, gather):
        total = pieces[0]
        for d in range(1, nvec):
            total = total + swap(pieces[d], 0, d)
        prods = [prod]
        if gather:
            total, prod = lax.optimization_barrier((total, prod))
            prods = [prod] + [swap(prod, 0, d) for d in range(1, nvec)]
        for shift in (1, 3):
            got = [swap(total, d << shift, 0) for d in (1, 2, 3)]
            total = (total + got[0]) + (got[1] + got[2])
        total = total + swap(total, 1, 0)
        return [total] + [swap(total, 0, d) for d in range(1, nvec)], prods

    def body(x, basis, pair_block, pair_live):
        rows, _ = x.shape
        narrow = basis.shape[1]
        blocks = rows // BS
        quarter = BS // nvec
        label_total = rows * nblk
        v = lax.axis_index("vec")
        my = v[None].astype(jnp.int32)
        pb, live = pair_block[0], pair_live[0]

        owner = lax.axis_index("blk").astype(jnp.int32)
        cuts = cut_start(basis.T, my, nvec)
        x, cuts = lax.optimization_barrier((x, cuts))
        vts = [cuts[0]]
        for d in range(1, nvec):
            vts.append(swap(cuts[d], 0, d))
        units = own_quarter(x, my, blocks, quarter)

        def along(x, h, d):
            return x if d == 0 else swap(x, d << SHIFT[LINES[h][0]], 0)

        feats = []
        for d in STEPS:
            for h in range(2):
                feats.append(along(units[h], h, d))
        vown, packs = send_start(vts, pb, my, blocks, quarter)
        vecs = [along(packs[h], h, d) for d in STEPS for h in range(2)]
        sends = relay(feats, vecs, owner[None])
        fars = [
            sends[side_at(h, o)] if o == 0 else swap(sends[side_at(h, o)], offset(LINES[h][1], o), 0)
            for o in FORWARD
            for h in range(2)
        ]

        (x, pb_late, live), fars[2] = lax.optimization_barrier(((x, pb, live), fars[2]))
        entries = entries_of(nblk, blocks)
        sc = pair_table(pb_late, live, owner, blocks, entries)
        unit = normalize(x)

        affs = [None] * (blocks // HALF)
        for it in range(ITERS):
            parts = []
            for part in range(len(affs)):
                if it:
                    out = pairs_next(sc, my, far, vown, affs[part], entries, part)
                else:
                    affs[part], out = pairs_first(sc, my, unit, fars, vown, entries, part)
                sc, out = lax.optimization_barrier((sc, list(out)))
                out = [o.reshape(HALF * quarter, nvec * narrow) for o in out]
                parts.append(out[0])
                for d in range(1, nvec):
                    parts.append(swap(out[d], 0, d))
            prod, pieces = gram(parts, my, nvec)
            sums, prods = gram_sum(pieces, prod, it + 1 == ITERS)
            if it + 1 < ITERS:
                vown, vsend = step(sums, prod, my, pb, blocks, quarter, label_total)
                far = exchange(vsend, "blk")
        return last(sums, prods, my, label_total).T

    return body


def solution(mesh):
    in_specs = (P("blk", None), P("blk", "vec"), P("blk", None), P("blk", None))
    return jax.shard_map(
        make(mesh), mesh=mesh, in_specs=in_specs, out_specs=P("blk", "vec"), check_vma=False
    )
```
